128 devices in a mesh: gx: 16 (over y, z), gy: 8 (over x, core).
Axes of the slice: x: 4, y: 4, z: 4, core: 2. Of those that a mesh axis runs over, the one named last changes fastest.
Arguments:
- fields: float32 [256, 64, 1536], P('gx', 'gy'), may hold values from -6 to 6
- resid: float32 [256, 64, 1536], P('gx', 'gy'), may hold values from -3 to 3
- permit: float32 [256, 64, 256], P('gx', 'gy'), may hold values from 1 to 8
- metric: float32 [256, 64, 768], P('gx', 'gy'), may hold values from 0.5 to 2
- route: int32 [16, 1024], P('gx', 'gy'), may hold values from 0 to 127, as said below
- stencil: int32 [1024, 1024], P('gx', 'gy'), may hold values from 0 to 255, as said below
- coords: float32 [2, 1024, 1024], P(None, 'gx', 'gy'), may hold values from -1 to 1
Outputs:
- fields_out: float32 [256, 64, 1536], P('gx', 'gy')
- resid_out: float32 [256, 64, 1536], P('gx', 'gy')
- plane: float32 [12, 1024, 1024], P(None, 'gx', 'gy')
The draws below stay inside these ranges and needn't reach their ends.
Inputs may be any that keep to these rules, and one draw needn't show every extreme that they name: `route`: of the 128 columns of one partition, at most 2 have the same tile, and some tile has exactly 2 of them in every partition; every tile is the tile of exactly 128 columns in all. stencil[p, q] = s * 2 + r where r is below the number of columns of partition s whose tile is the pixel's tile.
All inputs are finite; a program needn't handle non-finite values.
Results may differ from the reference program's by a relative error of at most 0.0001.
Values sent between devices are 32-bit elements; how exact they have to be, the bound alone decides.
A program may use at most 128 MiB of HBM per device.

```python
import math
import jax
import jax.numpy as jnp
import numpy as np
from jax import lax

LX = 16
LY = 8
LZ = 4
TILE_X = 64
TILE_Y = 128
PARTS_X = 16
PARTS_Y = 8
TILES = 128
COLS = 128
CAP = 2
NEX = 256
NEY = 64
PIX_X = 1024
PIX_Y = 1024


def tier_counts(key):
    ranking = jax.random.permutation(jax.random.fold_in(key, 11), TILES)
    source_ids = jnp.arange(TILES)[:, None]
    tile_ids = jnp.arange(TILES)[None, :]
    position = ranking[(source_ids + tile_ids) % TILES]
    counts = jnp.where(position < TILES // 4, CAP, jnp.where(position < 3 * TILES // 4, CAP // 2, 0))
    return counts.astype(jnp.int32)


def draw_route(key, part):
    counts = tier_counts(key)

    def one_source(counts_row, source_index):
        listed = jnp.repeat(jnp.arange(TILES, dtype=jnp.int32), counts_row, total_repeat_length=COLS)
        shuffle = jax.random.permutation(jax.random.fold_in(jax.random.fold_in(key, 23), source_index), COLS)
        return listed[shuffle]
    routes = jax.vmap(one_source)(counts, jnp.arange(TILES))
    grid_rows = NEX // LX
    return routes.reshape(grid_rows, TILES // grid_rows * COLS).astype(jnp.int32)


def draw_stencil(key, part):
    counts = tier_counts(key)
    tile_counts = counts.T
    running = jnp.cumsum(tile_counts, axis=1)
    chosen = jax.random.randint(jax.random.fold_in(key, 37), (TILES, TILE_X * TILE_Y), 0, COLS)
    chosen = chosen.at[:, 0].set(0).at[:, 1].set(COLS - 1)
    source = jax.vmap(lambda c, q: jnp.searchsorted(c, q, side='right'))(running, chosen).astype(jnp.int32)
    before = jnp.take_along_axis(running - tile_counts, source, axis=1)
    slot_ids = source * CAP + chosen - before
    grid_rows = NEX // LX
    slot_ids = slot_ids.reshape(grid_rows, TILES // grid_rows, TILE_X, TILE_Y).transpose(0, 2, 1, 3)
    return slot_ids.reshape(grid_rows * TILE_X, TILES // grid_rows * TILE_Y).astype(jnp.int32)


def level_of(rng, extent, cuts, least, high):
    def one(axis_at, shards_of):
        draws = jax.random.uniform(jax.random.fold_in(jax.random.fold_in(rng, 6), axis_at), (shards_of,), jnp.float32, least / len(cuts), high / len(cuts))
        return jnp.repeat(jnp.exp(draws), extent[axis_at] // shards_of).reshape((-1,) + (1,) * (len(extent) - axis_at - 1))

    factor_of = one(*cuts[0])
    for cut in cuts[1:]:
        factor_of = factor_of * one(*cut)
    return factor_of


def gaussian(rng, shape, spread, most, cuts=(), held_as=jnp.bfloat16):
    entries = spread * jax.random.normal(rng, shape, jnp.float32)
    if cuts:
        entries = entries * level_of(rng, shape, cuts, -0.22, 0.18)
    return jnp.clip(entries, -most, most).astype(held_as)


def setup_inputs(seed: int = 0) -> dict:
    key_list = jax.random.split(jax.random.key(seed), 8)
    return {
        "fields": gaussian(key_list[0], (NEX, NEY, 6 * LZ * 64), 1.0, 6.0, ((0, 16), (1, 8)), jnp.float32),
        "resid": gaussian(key_list[1], (NEX, NEY, 6 * LZ * 64), 0.5, 3.0, ((0, 16), (1, 8)), jnp.float32),
        "permit": jnp.clip(jnp.exp(math.log(8.0) - 2.0794415 * jax.random.uniform(key_list[2], (NEX, NEY, LZ * 64), jnp.float32) ** level_of(key_list[2], (NEX, NEY, LZ * 64), ((0, 16), (1, 8)), -0.2, 0.2)), 1.0, 8.0),
        "metric": jnp.clip(jnp.exp(math.log(2.0) - 1.3862944 * jax.random.uniform(key_list[3], (NEX, NEY, 3 * LZ * 64), jnp.float32) ** level_of(key_list[3], (NEX, NEY, 3 * LZ * 64), ((0, 16), (1, 8)), -0.2, 0.2)), 0.5, 2.0),
        "route": draw_route(jax.random.fold_in(key_list[7], 71), 0),
        "stencil": draw_stencil(jax.random.fold_in(key_list[7], 71), 0),
        "coords": jnp.clip(jax.random.uniform(key_list[6], (2, PIX_X, PIX_Y), jnp.float32, -1.0, 1.0) * level_of(key_list[6], (2, PIX_X, PIX_Y), ((1, 16), (2, 8)), -0.4, 0.0), -1.0, 1.0),
    }


section_decay = (-0.41789047449985195, -1.192151694642677)
section_gain = (0.37921031299962726, 0.8229550293869817)
time_step = 0.05
lift_factor = 3.0

def gll_points():
    return np.array([-1.0, -np.sqrt(0.2), np.sqrt(0.2), 1.0])

def derivative_table():
    points = gll_points()
    barycentric = np.array([1.0 / np.prod([points[j] - points[k] for k in range(4) if k != j]) for j in range(4)])
    table = np.zeros((4, 4))
    for i in range(4):
        for j in range(4):
            if i != j:
                table[i, j] = barycentric[j] / barycentric[i] / (points[i] - points[j])
        table[i, i] = -np.sum(table[i])
    return table

def lagrange_weights(first, second):
    points = gll_points()

    def basis(coord):
        listing = []
        for j in range(4):
            result = jnp.ones_like(coord)
            for k in range(4):
                if k != j:
                    result = result * (coord - float(points[k])) / float(points[j] - points[k])
            listing.append(result)
        return listing
    along_u = basis(first)
    along_v = basis(second)
    return jnp.stack([along_u[i] * along_v[j] for i in range(4) for j in range(4)], axis=-1)

def normal_cross(axis, sign, parts):
    first, second, third = parts
    nothing = jnp.zeros_like(first)
    if axis == 0:
        return [nothing, -sign * third, sign * second]
    if axis == 1:
        return [sign * third, nothing, -sign * first]
    return [-sign * second, sign * first, nothing]

def face_flux(inner, outer, axis, sign, scale):
    change = outer - inner
    delta_e = [change[:, :, c] for c in range(3)]
    delta_h = [change[:, :, c + 3] for c in range(3)]
    cross_h = normal_cross(axis, sign, delta_h)
    cross_e = normal_cross(axis, sign, delta_e)
    flux_e = [cross_h[c] if c == axis else cross_h[c] + delta_e[c] for c in range(3)]
    flux_h = [-cross_e[c] if c == axis else delta_h[c] - cross_e[c] for c in range(3)]
    return lift_factor * scale[:, :, None] * jnp.stack(flux_e + flux_h, axis=2)

def combine(state, permit_nodes, metric_nodes, slopes, exteriors):
    along_x, along_y, along_z = slopes
    curl_e = [along_y[:, :, 2] - along_z[:, :, 1], along_z[:, :, 0] - along_x[:, :, 2], along_x[:, :, 1] - along_y[:, :, 0]]
    curl_h = [along_y[:, :, 5] - along_z[:, :, 4], along_z[:, :, 3] - along_x[:, :, 5], along_x[:, :, 4] - along_y[:, :, 3]]
    tend = jnp.stack(curl_h + [-part for part in curl_e], axis=2)
    minus_x, plus_x, minus_y, plus_y = exteriors
    tend = tend.at[:, :, :, :, 0].add(face_flux(state[:, :, :, :, 0], minus_x, 0, -1.0, metric_nodes[:, :, 0, :, 0]))
    tend = tend.at[:, :, :, :, 3].add(face_flux(state[:, :, :, :, 3], plus_x, 0, 1.0, metric_nodes[:, :, 0, :, 3]))
    tend = tend.at[:, :, :, :, :, 0].add(face_flux(state[:, :, :, :, :, 0], minus_y, 1, -1.0, metric_nodes[:, :, 1, :, :, 0]))
    tend = tend.at[:, :, :, :, :, 3].add(face_flux(state[:, :, :, :, :, 3], plus_y, 1, 1.0, metric_nodes[:, :, 1, :, :, 3]))
    bottom = state[:, :, :, :, :, :, 0]
    upper = state[:, :, :, :, :, :, 3]
    flip = jnp.array([-1.0, -1.0, -1.0, 1.0, 1.0, 1.0], dtype=jnp.float32).reshape(1, 1, 6, 1, 1, 1)
    below = jnp.concatenate([bottom[:, :, :, 0:1] * flip, upper[:, :, :, :-1]], axis=3)
    above = jnp.concatenate([bottom[:, :, :, 1:], jnp.zeros_like(upper[:, :, :, 0:1])], axis=3)
    tend = tend.at[:, :, :, :, :, :, 0].add(face_flux(bottom, below, 2, -1.0, metric_nodes[:, :, 2, :, :, :, 0]))
    tend = tend.at[:, :, :, :, :, :, 3].add(face_flux(upper, above, 2, 1.0, metric_nodes[:, :, 2, :, :, :, 3]))
    return jnp.concatenate([tend[:, :, 0:3] / permit_nodes[:, :, None], tend[:, :, 3:]], axis=2)

def block_tendency(pieces):
    state, permit_nodes, metric_nodes, minus_x, plus_x, minus_y, plus_y = pieces
    table = jnp.asarray(derivative_table(), dtype=jnp.float32)
    highest = lax.Precision.HIGHEST
    along_x = jnp.einsum('ai,xyclijk->xyclajk', table, state, precision=highest) * metric_nodes[:, :, 0][:, :, None]
    along_y = jnp.einsum('bj,xyclijk->xyclibk', table, state, precision=highest) * metric_nodes[:, :, 1][:, :, None]
    along_z = jnp.einsum('mk,xyclijk->xyclijm', table, state, precision=highest) * metric_nodes[:, :, 2][:, :, None]
    return combine(state, permit_nodes, metric_nodes, (along_x, along_y, along_z), (minus_x, plus_x, minus_y, plus_y))

def split_rows(array):
    return array.reshape((PARTS_X, LX) + array.shape[1:])

def tendency(state, permit_nodes, metric_nodes):
    face_px = state[:, :, :, :, 3]
    face_mx = state[:, :, :, :, 0]
    face_py = state[:, :, :, :, :, 3]
    face_my = state[:, :, :, :, :, 0]
    minus_x = jnp.concatenate([jnp.zeros_like(face_px[0:1]), face_px[:-1]], axis=0)
    plus_x = jnp.concatenate([face_mx[1:], jnp.zeros_like(face_mx[0:1])], axis=0)
    minus_y = jnp.concatenate([jnp.zeros_like(face_py[:, 0:1]), face_py[:, :-1]], axis=1)
    plus_y = jnp.concatenate([face_my[:, 1:], jnp.zeros_like(face_my[:, 0:1])], axis=1)
    pieces = tuple((split_rows(array) for array in (state, permit_nodes, metric_nodes, minus_x, plus_x, minus_y, plus_y)))
    result = lax.map(block_tendency, pieces)
    return result.reshape(state.shape)

def reference(fields, resid, permit, metric, route, stencil, coords):
    field_shape = (NEX, NEY, 6, LZ, 4, 4, 4)
    state = fields.reshape(field_shape)
    register = resid.reshape(field_shape)
    permit_nodes = permit.reshape(NEX, NEY, LZ, 4, 4, 4)
    metric_nodes = metric.reshape(NEX, NEY, 3, LZ, 4, 4, 4)
    samples = [state[:, :, :, LZ - 1, :, :, 3]]
    for section in range(2):
        register = section_decay[section] * register + time_step * tendency(state, permit_nodes, metric_nodes)
        state = state + section_gain[section] * register
        if section == 0:
            samples.append(state[:, :, :, LZ - 1, :, :, 3])
    payload = jnp.stack(samples, axis=2).reshape(PARTS_X, LX, PARTS_Y, LY, 192)
    payload = payload.transpose(0, 2, 1, 3, 4).reshape(TILES * COLS, 192)
    routes = route.reshape(TILES, COLS)
    one_hot = (routes[:, :, None] == jnp.arange(TILES, dtype=jnp.int32)[None, None, :]).astype(jnp.int32)
    earlier = jnp.cumsum(one_hot, axis=1) - one_hot
    ranks = lax.optimization_barrier(jnp.sum(earlier * one_hot, axis=2))
    target = routes * (TILES * CAP) + jnp.arange(TILES, dtype=jnp.int32)[:, None] * CAP + ranks
    owner = jnp.zeros((TILES * TILES * CAP,), jnp.int32).at[target.reshape(-1)].set(jnp.arange(TILES * COLS, dtype=jnp.int32))
    slot_tiles = stencil.reshape(PARTS_X, TILE_X, PARTS_Y, TILE_Y).transpose(0, 2, 1, 3).reshape(TILES, TILE_X * TILE_Y)
    coord_tiles = coords.reshape(2, PARTS_X, TILE_X, PARTS_Y, TILE_Y).transpose(1, 3, 0, 2, 4).reshape(TILES, 2, TILE_X * TILE_Y)

    def one_tile(pieces):
        tile_index, slot_ids, where = pieces
        chosen = owner[tile_index * (TILES * CAP) + slot_ids]
        values = payload[chosen].reshape(-1, 12, 16)
        weights = lagrange_weights(where[0], where[1])
        return lax.optimization_barrier(jnp.sum(values * weights[:, None, :], axis=2)).T
    tiles_out = lax.map(one_tile, (jnp.arange(TILES, dtype=jnp.int32), slot_tiles, coord_tiles))
    plane = tiles_out.reshape(PARTS_X, PARTS_Y, 12, TILE_X, TILE_Y).transpose(2, 0, 3, 1, 4).reshape(12, PIX_X, PIX_Y)
    return (state.reshape(fields.shape), register.reshape(fields.shape), plane)
```

```python
import functools

import jax
import jax.numpy as jnp
import numpy as np
from jax import lax
from jax.experimental import pallas as pl
from jax.experimental.pallas import tpu as pltpu
from jax.sharding import PartitionSpec as P

section_decay = (-0.41789047449985195, -1.192151694642677)
section_gain = (0.37921031299962726, 0.8229550293869817)
time_step = 0.05
lift_factor = 3.0

MESH = pl.DeviceIdType.MESH
F32 = jnp.float32
BF16 = jnp.bfloat16
NX, NY = 16, 8
CH = 16


def gll_points():
    return np.array([-1.0, -np.sqrt(0.2), np.sqrt(0.2), 1.0])


def derivative_table():
    points = gll_points()
    barycentric = np.array(
        [1.0 / np.prod([points[j] - points[k] for k in range(4) if k != j]) for j in range(4)]
    )
    table = np.zeros((4, 4))
    for i in range(4):
        for j in range(4):
            if i != j:
                table[i, j] = barycentric[j] / barycentric[i] / (points[i] - points[j])
        table[i, i] = -np.sum(table[i])
    return table


def stacked_tables():
    table = derivative_table()
    table[3, 3] -= lift_factor
    table[0, 0] += lift_factor
    eye = np.eye(4)
    along = [
        np.kron(np.kron(table, eye), eye),
        np.kron(np.kron(eye, table), eye),
        np.kron(np.kron(eye, eye), table),
    ]
    two = [np.kron(np.eye(2), m).T for m in along]
    full = np.stack(
        [np.concatenate([two[(g + 1) % 3], two[(g + 2) % 3]], axis=1) for g in range(3)]
    ).astype(np.float32)
    high = full.astype(jnp.bfloat16)
    low = (full - high.astype(np.float32)).astype(jnp.bfloat16)
    return np.concatenate([high, high], axis=1), low


def lane_iota(rows):
    return lax.broadcasted_iota(jnp.int32, (rows, 128), 1)


def node_digit(axis, lane):
    return (lane >> (4 - 2 * axis)) & 3


def basis(coord):
    points = gll_points()
    listing = []
    for j in range(4):
        result = None
        for k in range(4):
            if k != j:
                term = (coord - float(points[k])) * float(1.0 / (points[j] - points[k]))
                result = term if result is None else result * term
        listing.append(result)
    return listing


def split2(value):
    high = value.astype(BF16)
    return high, (value - high.astype(F32)).astype(BF16)


def kernel(
    f_in, r_in, p_in, m_in, rt_in, st_in, co_in, w1_in, w2_in,
    f_out, r_out, pl_out,
    u, r, ep, me, rt, st, co, w1, w2,
    gxb, gyb, hys, hyr, qz, xs, rr, pay, og, b1, b2, tb, tt, oh, wt, pls,
    in_sem, out_sem, hs_sem, hr_sem, s1_sem, r1_sem, s2_sem, r2_sem,
):
    ix = lax.axis_index("gx")
    iy = lax.axis_index("gy")

    loads = [
        pltpu.make_async_copy(src, dst, in_sem.at[n])
        for n, (src, dst) in enumerate(
            [(f_in, u), (rt_in, rt), (w1_in, w1), (w2_in, w2), (m_in, me), (r_in, r),
             (p_in, ep), (st_in, st), (co_in, co)]
        )
    ]
    for load in loads:
        load.start()

    barrier = pltpu.get_barrier_semaphore()

    def greet_x(d, carry):
        pl.semaphore_signal(barrier, inc=1, device_id=(lax.rem(ix + d, NX), iy), device_id_type=MESH)
        return carry

    def greet_y(d, carry):
        pl.semaphore_signal(barrier, inc=1, device_id=(ix, lax.rem(iy + d, NY)), device_id_type=MESH)
        return carry

    lax.fori_loop(1, NX, greet_x, 0)
    lax.fori_loop(1, NY, greet_y, 0)

    lane = lane_iota(CH)
    digit = [node_digit(a, lane) for a in range(3)]
    sg = [
        jnp.where(d == 3, 1.0, jnp.where(d == 0, -1.0, 0.0)).astype(F32) for d in digit
    ]
    bd3 = [jnp.where((d == 3) | (d == 0), lift_factor, 0.0).astype(F32) for d in digit]
    sg3 = [lift_factor * s for s in sg]
    swap = []
    for a in range(3):
        reach = 3 << (4 - 2 * a)
        base = lane if a < 2 else lane ^ 64
        swap.append(
            jnp.where(digit[a] == 0, base + reach, jnp.where(digit[a] == 3, base - reach, lane))
        )
    is3 = [digit[0] == 3, digit[1] == 3]
    low_bottom = (digit[2] == 0) & (lane < 64)
    high_top = (digit[2] == 3) & (lane >= 64)
    pick = 64 + 4 * (lane >> 3) + 3
    comp_lane = lane & 7

    def permute(value, index):
        return jnp.take_along_axis(value, index, axis=1)

    def faces(sec, r0, ee, hh):
        xt = pl.multiple_of(r0, CH)
        for a in range(3):
            b, c = (a + 1) % 3, (a + 2) % 3
            for pair in range(2):
                sums, moved = [], []
                for lp in range(2):
                    if pair == 0:
                        t = ee[lp][b] + sg[a] * hh[lp][c]
                    else:
                        t = ee[lp][c] - sg[a] * hh[lp][b]
                    sums.append(t)
                    moved.append(permute(t, swap[a]))
                for lp in range(2):
                    k = pair * 2 + lp
                    if a == 0:
                        gxb[sec, k, pl.ds(xt + 8, CH), :] = moved[lp]
                    elif a == 1:
                        gyb[sec, k, pl.ds(2 * xt + 8, 8), :] = moved[lp][0:8]
                        gyb[sec, k, pl.ds(2 * xt + 24, 8), :] = moved[lp][8:16]
                    elif lp == 0:
                        qz[k, pl.ds(xt, CH), :] = jnp.where(
                            low_bottom, -sums[0], jnp.where(high_top, moved[1], moved[0])
                        )
                    else:
                        qz[k, pl.ds(xt, CH), :] = jnp.where(
                            high_top, 0.0, jnp.where(low_bottom, moved[0], moved[1])
                        )
        for g in range(3):
            for e, side in enumerate((ee, hh)):
                for lp in range(2):
                    high, low = split2(side[lp][g])
                    rows = pl.ds((e * 2 + lp) * 128 + xt, CH)
                    xs[g, rows, 0:128] = high
                    xs[g, rows, 128:256] = low

    def trace_rows(r0, ee, hh):
        total = jnp.zeros((CH, 128), F32)
        for c in range(6):
            side = ee if c < 3 else hh
            total = jnp.where(comp_lane == c, permute(side[1][c % 3], pick), total)
        pay[pl.ds(r0, CH), :] = total

    def tiles(ref, r0):
        return [
            [ref[pl.ds(r0, CH), (c * 2 + lp) * 128 : (c * 2 + lp + 1) * 128] for c in range(6)]
            for lp in range(2)
        ]

    def halo_copies(sec):
        below = {"x": lax.rem(ix + NX - 1, NX), "y": lax.rem(iy + NY - 1, NY)}
        above = {"x": lax.rem(ix + 1, NX), "y": lax.rem(iy + 1, NY)}
        plan = [
            (gxb.at[sec, :, pl.ds(8, 8)], gxb.at[sec, :, pl.ds(136, 8)], (below["x"], iy)),
            (gxb.at[sec, :, pl.ds(128, 8)], gxb.at[sec, :, pl.ds(0, 8)], (above["x"], iy)),
            (hys.at[sec, 0], hyr.at[sec, 0], (ix, below["y"])),
            (hys.at[sec, 1], hyr.at[sec, 1], (ix, above["y"])),
        ]
        return [
            pltpu.make_async_remote_copy(
                src_ref=src, dst_ref=dst, send_sem=hs_sem.at[sec, n], recv_sem=hr_sem.at[sec, n],
                device_id=device, device_id_type=MESH,
            )
            for n, (src, dst, device) in enumerate(plan)
        ]

    def send_halo(sec):
        for k in range(4):
            hys[sec, 0, k] = gyb[sec, k, pl.ds(8, 16, stride=16), :]
            hys[sec, 1, k] = gyb[sec, k, pl.ds(15, 16, stride=16), :]
        for copy in halo_copies(sec):
            copy.start()

    def take_halo(sec):
        for copy in halo_copies(sec):
            copy.wait_recv()

        @pl.when(ix == NX - 1)
        def _():
            gxb[sec, :, 136:144, :] = jnp.zeros((4, 8, 128), F32)

        @pl.when(ix == 0)
        def _():
            gxb[sec, :, 0:8, :] = jnp.zeros((4, 8, 128), F32)

        has_up = jnp.where(iy == NY - 1, 0.0, 1.0).astype(F32)
        has_down = jnp.where(iy == 0, 0.0, 1.0).astype(F32)
        for k in range(4):
            gyb[sec, k, pl.ds(16, 16, stride=16), :] = hyr[sec, 0, k] * has_up
            gyb[sec, k, pl.ds(7, 16, stride=16), :] = hyr[sec, 1, k] * has_down

    def products():
        def one(g, carry):
            rr[g] = jnp.dot(xs[g], w1[g], preferred_element_type=F32) + jnp.dot(
                xs[g, :, 0:128], w2[g], preferred_element_type=F32
            )
            return carry

        lax.fori_loop(0, 3, one, 0)

    def finish(sec, r0):
        xt = pl.multiple_of(r0, CH)
        rows = pl.ds(xt, CH)
        new = [[None] * 6, [None] * 6]
        for lp in range(2):
            cols = [slice((c * 2 + lp) * 128, (c * 2 + lp + 1) * 128) for c in range(6)]
            val = [u[rows, cols[c]] for c in range(6)]
            tend = [None] * 6

            def add(c, term):
                tend[c] = term if tend[c] is None else tend[c] + term

            def slope(comp, axis):
                g, e = comp % 3, comp // 3
                half = 0 if axis == (g + 1) % 3 else 1
                return rr[g, pl.ds((e * 2 + lp) * 128 + xt, CH), half * 128 : half * 128 + 128]

            for a in range(3):
                b, c = (a + 1) % 3, (a + 2) % 3
                met = me[rows, (a * 2 + lp) * 128 : (a * 2 + lp + 1) * 128]
                q = []
                for pair in range(2):
                    k = pair * 2 + lp
                    if a == 0:
                        q.append(
                            jnp.where(
                                is3[0],
                                gxb[sec, k, pl.ds(xt + 16, CH), :],
                                gxb[sec, k, pl.ds(xt, CH), :],
                            )
                        )
                    elif a == 1:
                        up = jnp.concatenate(
                            [gyb[sec, k, pl.ds(2 * xt + 9, 8), :], gyb[sec, k, pl.ds(2 * xt + 25, 8), :]],
                            axis=0,
                        )
                        down = jnp.concatenate(
                            [gyb[sec, k, pl.ds(2 * xt + 7, 8), :], gyb[sec, k, pl.ds(2 * xt + 23, 8), :]],
                            axis=0,
                        )
                        q.append(jnp.where(is3[1], up, down))
                    else:
                        q.append(qz[k, rows, :])
                add(b, met * (bd3[a] * (q[0] - val[b]) - slope(c + 3, a)))
                add(c + 3, met * (-(sg3[a] * q[0]) - bd3[a] * val[c + 3] - slope(b, a)))
                add(c, met * (bd3[a] * (q[1] - val[c]) + slope(b + 3, a)))
                add(b + 3, met * (sg3[a] * q[1] - bd3[a] * val[b + 3] + slope(c, a)))
            scale = time_step / ep[rows, lp * 128 : (lp + 1) * 128]
            for c in range(6):
                rate = tend[c] * scale if c < 3 else tend[c] * time_step
                reg = section_decay[sec] * r[rows, cols[c]] + rate
                r[rows, cols[c]] = reg
                value = val[c] + section_gain[sec] * reg
                u[rows, cols[c]] = value
                new[lp][c] = value
        return new

    def stage1(sample):
        def make(d):
            peer = lax.rem(ix + d, NX)
            return pltpu.make_async_remote_copy(
                src_ref=og.at[sample, pl.ds(pl.multiple_of(peer * 16, 16), 16)],
                dst_ref=b1.at[sample, pl.ds(pl.multiple_of(ix * 16, 16), 16)],
                send_sem=s1_sem.at[sample, d], recv_sem=r1_sem.at[sample, d],
                device_id=(peer, iy), device_id_type=MESH,
            )
        return make

    def stage2(sample):
        def make(d):
            peer = lax.rem(iy + d, NY)
            return pltpu.make_async_remote_copy(
                src_ref=b2.at[sample, pl.ds(pl.multiple_of(peer * 32, 32), 32)],
                dst_ref=tb.at[sample, pl.ds(pl.multiple_of(iy * 32, 32), 32)],
                send_sem=s2_sem.at[sample, d], recv_sem=r2_sem.at[sample, d],
                device_id=(ix, peer), device_id_type=MESH,
            )
        return make

    def each(count, make, act):
        def body(d, carry):
            act(make(d))
            return carry

        lax.fori_loop(1, count, body, 0)

    def place(sample):
        value = pay[...]
        high, rest = value.astype(BF16), None
        rest = value - high.astype(F32)
        mid = rest.astype(BF16)
        low = (rest - mid.astype(F32)).astype(BF16)
        slot = jnp.broadcast_to(slots, (256, 128))
        where = lax.broadcasted_iota(jnp.int32, (256, 128), 0) == slot
        put = jnp.where(where, 1.0, 0.0).astype(BF16)
        og[sample] = (
            jnp.dot(put, high, preferred_element_type=F32)
            + jnp.dot(put, mid, preferred_element_type=F32)
        ) + jnp.dot(put, low, preferred_element_type=F32)
        own = pl.ds(pl.multiple_of(ix * 16, 16), 16)
        b1[sample, own, :] = og[sample, own, :]

    def forward(sample):
        each(NX, stage1(sample), lambda copy: copy.wait_recv())
        for g in range(NY):
            for side in range(2):
                b2[sample, pl.ds(g * 32 + side * 16, 16), :] = b1[
                    sample, pl.ds(g * 2 + side, 16, stride=16), :
                ]
        own = pl.ds(pl.multiple_of(iy * 32, 32), 32)
        tb[sample, own, :] = b2[sample, own, :]
        each(NY, stage2(sample), lambda copy: copy.start())

    def interpolate(sample):
        each(NY, stage2(sample), lambda copy: copy.wait_recv())
        high, low = split2(tb[sample].T)
        tt[0:128] = high
        tt[128:256] = low

        def rows_of(pp, carry):
            got = jnp.dot(tt[...], oh[pp], preferred_element_type=F32)
            for h in range(2):
                part = got[:, h * 128 : h * 128 + 128]
                total = None
                for n in range(16):
                    both = part[n * 8 : n * 8 + 8] + part[128 + n * 8 : 136 + n * 8]
                    term = both * wt[n, pl.ds(2 * pp + h, 1), :]
                    total = term if total is None else total + term
                pls[pl.ds(sample * 512 + 2 * pp + h, 8, stride=64), :] = total
            return carry

        lax.fori_loop(0, 32, rows_of, 0)

    loads[0].wait()
    loads[1].wait()

    def first_faces(ch, carry):
        r0 = ch * CH
        both = tiles(u, pl.multiple_of(r0, CH))
        ee = [both[lp][0:3] for lp in range(2)]
        hh = [both[lp][3:6] for lp in range(2)]
        faces(0, r0, ee, hh)
        trace_rows(pl.multiple_of(r0, CH), ee, hh)
        return carry

    lax.fori_loop(0, 128 // CH, first_faces, 0)

    targets = jnp.broadcast_to(rt[...], (128, 128))
    earlier = lax.broadcasted_iota(jnp.int32, (128, 128), 0) < lane_iota(128)
    same = jnp.where((targets.T == targets) & earlier, 1, 0)
    slots = rt[...] * 2 + jnp.sum(same, axis=0, keepdims=True)

    pl.semaphore_wait(barrier, NX - 1 + NY - 1)
    send_halo(0)
    place(0)
    each(NX, stage1(0), lambda copy: copy.start())

    loads[2].wait()
    loads[3].wait()
    products()

    for load in loads[4:]:
        load.wait()

    stv = st[...]
    slot_of = ((stv >> 1) & 7) * 32 + (stv & 1) * 16 + (stv >> 4)
    st[...] = slot_of
    along_u = basis(co[0])
    along_v = basis(co[1])
    for i in range(4):
        for j in range(4):
            wt[i * 4 + j] = along_u[i] * along_v[j]
    slot_iota = lax.broadcasted_iota(jnp.int32, (256, 128), 0)

    def one_hot(pp, carry):
        for h in range(2):
            row = jnp.broadcast_to(st[pl.ds(2 * pp + h, 1), :], (256, 128))
            oh[pp, :, h * 128 : h * 128 + 128] = jnp.where(slot_iota == row, 1.0, 0.0).astype(BF16)
        return carry

    lax.fori_loop(0, 32, one_hot, 0)

    take_halo(0)

    def first_section(ch, carry):
        r0 = ch * CH
        new = finish(0, r0)
        ee = [new[lp][0:3] for lp in range(2)]
        hh = [new[lp][3:6] for lp in range(2)]
        faces(1, r0, ee, hh)
        trace_rows(pl.multiple_of(r0, CH), ee, hh)
        return carry

    lax.fori_loop(0, 128 // CH, first_section, 0)
    send_halo(1)
    place(1)
    each(NX, stage1(1), lambda copy: copy.start())
    forward(0)
    products()
    forward(1)
    take_halo(1)

    def second_section(ch, carry):
        finish(1, ch * CH)
        return carry

    lax.fori_loop(0, 128 // CH, second_section, 0)
    stores = [
        pltpu.make_async_copy(u, f_out, out_sem.at[0]),
        pltpu.make_async_copy(r, r_out, out_sem.at[1]),
        pltpu.make_async_copy(pls.at[pl.ds(0, 384)], pl_out.at[pl.ds(0, 384)], out_sem.at[2]),
        pltpu.make_async_copy(pls.at[pl.ds(512, 384)], pl_out.at[pl.ds(384, 384)], out_sem.at[3]),
    ]
    stores[0].start()
    stores[1].start()
    interpolate(0)
    stores[2].start()
    interpolate(1)
    stores[3].start()
    for sec in range(2):
        for copy in halo_copies(sec):
            copy.wait_send()
        each(NX, stage1(sec), lambda copy: copy.wait_send())
        each(NY, stage2(sec), lambda copy: copy.wait_send())
    for store in stores:
        store.wait()


def on_device(fields, resid, permit, metric, route, stencil, coords):
    columns = fields.shape[0] * fields.shape[1]
    w1, w2 = stacked_tables()
    anywhere = pl.BlockSpec(memory_space=pl.ANY)
    dma = pltpu.SemaphoreType.DMA
    f_out, r_out, plane = pl.pallas_call(
        kernel,
        out_shape=(
            jax.ShapeDtypeStruct((columns, 1536), F32),
            jax.ShapeDtypeStruct((columns, 1536), F32),
            jax.ShapeDtypeStruct((768, 128), F32),
        ),
        in_specs=[anywhere] * 9,
        out_specs=(anywhere,) * 3,
        scratch_shapes=[
            pltpu.VMEM((128, 1536), F32),
            pltpu.VMEM((128, 1536), F32),
            pltpu.VMEM((128, 256), F32),
            pltpu.VMEM((128, 768), F32),
            pltpu.VMEM((1, 128), jnp.int32),
            pltpu.VMEM((64, 128), jnp.int32),
            pltpu.VMEM((2, 64, 128), F32),
            pltpu.VMEM((3, 256, 256), BF16),
            pltpu.VMEM((3, 128, 256), BF16),
            pltpu.VMEM((2, 4, 144, 128), F32),
            pltpu.VMEM((2, 4, 272, 128), F32),
            pltpu.VMEM((2, 2, 4, 16, 128), F32),
            pltpu.VMEM((2, 2, 4, 16, 128), F32),
            pltpu.VMEM((4, 128, 128), F32),
            pltpu.VMEM((3, 512, 256), BF16),
            pltpu.VMEM((3, 512, 256), F32),
            pltpu.VMEM((128, 128), F32),
            pltpu.VMEM((2, 256, 128), F32),
            pltpu.VMEM((2, 256, 128), F32),
            pltpu.VMEM((2, 256, 128), F32),
            pltpu.VMEM((2, 256, 128), F32),
            pltpu.VMEM((256, 256), BF16),
            pltpu.VMEM((32, 256, 256), BF16),
            pltpu.VMEM((16, 64, 128), F32),
            pltpu.VMEM((1024, 128), F32),
            dma((9,)),
            dma((4,)),
            dma((2, 4)),
            dma((2, 4)),
            dma((2, NX)),
            dma((2, NX)),
            dma((2, NY)),
            dma((2, NY)),
        ],
        compiler_params=pltpu.CompilerParams(
            collective_id=0, has_side_effects=True, vmem_limit_bytes=40 * 1024 * 1024
        ),
    )(
        fields.reshape(columns, 1536),
        resid.reshape(columns, 1536),
        permit.reshape(columns, 256),
        metric.reshape(columns, 768),
        route,
        stencil,
        coords,
        jnp.asarray(w1),
        jnp.asarray(w2),
    )
    return (
        f_out.reshape(fields.shape),
        r_out.reshape(fields.shape),
        plane.reshape(12, stencil.shape[0], stencil.shape[1]),
    )


def solution(mesh):
    return jax.shard_map(
        on_device,
        mesh=mesh,
        in_specs=(
            P("gx", "gy", None),
            P("gx", "gy", None),
            P("gx", "gy", None),
            P("gx", "gy", None),
            P("gx", "gy"),
            P("gx", "gy"),
            P(None, "gx", "gy"),
        ),
        out_specs=(P("gx", "gy", None), P("gx", "gy", None), P(None, "gx", "gy")),
        check_vma=False,
    )
```

```python
import functools

import jax
import jax.numpy as jnp
import numpy as np
from jax import lax
from jax.experimental import pallas as pl
from jax.experimental.pallas import tpu as pltpu
from jax.sharding import PartitionSpec as P

section_decay = (-0.41789047449985195, -1.192151694642677)
section_gain = (0.37921031299962726, 0.8229550293869817)
time_step = 0.05
lift_factor = 3.0

MESH = pl.DeviceIdType.MESH
F32 = jnp.float32
BF16 = jnp.bfloat16
NX, NY = 16, 8
VMEM_A, VMEM_B = 54, 16
CH = 16


def gll_points():
    return np.array([-1.0, -np.sqrt(0.2), np.sqrt(0.2), 1.0])


def derivative_table():
    points = gll_points()
    barycentric = np.array(
        [1.0 / np.prod([points[j] - points[k] for k in range(4) if k != j]) for j in range(4)]
    )
    table = np.zeros((4, 4))
    for i in range(4):
        for j in range(4):
            if i != j:
                table[i, j] = barycentric[j] / barycentric[i] / (points[i] - points[j])
        table[i, i] = -np.sum(table[i])
    return table


def stacked_tables():
    table = derivative_table()
    table[3, 3] -= lift_factor
    table[0, 0] += lift_factor
    eye = np.eye(4)
    along = [
        np.kron(np.kron(table, eye), eye),
        np.kron(np.kron(eye, table), eye),
        np.kron(np.kron(eye, eye), table),
    ]
    two = [np.kron(np.eye(2), m).T for m in along]
    full = np.stack(
        [np.concatenate([two[(g + 1) % 3], two[(g + 2) % 3]], axis=1) for g in range(3)]
    ).astype(np.float32)
    high = full.astype(jnp.bfloat16)
    low = (full - high.astype(np.float32)).astype(jnp.bfloat16)
    return np.concatenate([high, high], axis=1), low


def lane_iota(rows):
    return lax.broadcasted_iota(jnp.int32, (rows, 128), 1)


def node_digit(axis, lane):
    return (lane >> (4 - 2 * axis)) & 3


def basis(coord):
    points = gll_points()
    listing = []
    for j in range(4):
        result = None
        for k in range(4):
            if k != j:
                term = (coord - float(points[k])) * float(1.0 / (points[j] - points[k]))
                result = term if result is None else result * term
        listing.append(result)
    return listing


def split2(value):
    high = value.astype(BF16)
    return high, (value - high.astype(F32)).astype(BF16)


def interpolate(table, tt, oh, wt, pls):
    high, low = split2(table.T)
    tt[0:128] = high
    tt[128:256] = low

    def rows_of(pp, carry):
        got = jnp.dot(tt[...], oh[pp], preferred_element_type=F32)
        for h in range(2):
            part = got[:, h * 128 : h * 128 + 128]
            total = None
            for n in range(16):
                both = part[n * 8 : n * 8 + 8] + part[128 + n * 8 : 136 + n * 8]
                term = both * wt[n, pl.ds(2 * pp + h, 1), :]
                total = term if total is None else total + term
            pls[pl.ds(2 * pp + h, 8, stride=64), :] = total
        return carry

    lax.fori_loop(0, 32, rows_of, 0, unroll=8)


def last_kernel(
    u, r, tb1, oh, wt, pls0, f_out, r_out, pl_out, pls1, tt, out_sem
):
    stores = [
        pltpu.make_async_copy(u, f_out, out_sem.at[0]),
        pltpu.make_async_copy(r, r_out, out_sem.at[1]),
        pltpu.make_async_copy(pls0.at[pl.ds(0, 384)], pl_out.at[pl.ds(0, 384)], out_sem.at[2]),
        pltpu.make_async_copy(pls1.at[pl.ds(0, 384)], pl_out.at[pl.ds(384, 384)], out_sem.at[3]),
    ]
    for store in stores[:3]:
        store.start()
    interpolate(tb1[...], tt, oh, wt, pls1)
    stores[3].start()
    for store in stores:
        store.wait()


def kernel(
    f_in, r_in, p_in, m_in, rt_in, st_in, co_in, w1_in, w2_in,
    u, r, tb1, oh, wt, pls,
    ep, me, rt, st, co, w1, w2,
    gxb, gyb, hys, hyr, qz, xs, rr, pay, og, b1, b2, tb0, tt,
    in_sem, hs_sem, hr_sem, s1_sem, r1_sem, s2_sem, r2_sem,
):
    tb = (tb0, tb1)
    ix = lax.axis_index("gx")
    iy = lax.axis_index("gy")

    loads = [
        pltpu.make_async_copy(src, dst, in_sem.at[n])
        for n, (src, dst) in enumerate(
            [(f_in, u), (rt_in, rt), (w1_in, w1), (w2_in, w2), (m_in, me), (r_in, r),
             (p_in, ep), (st_in, st), (co_in, co)]
        )
    ]
    for load in loads:
        load.start()

    barrier = pltpu.get_barrier_semaphore()

    def greet_x(d, carry):
        pl.semaphore_signal(barrier, inc=1, device_id=(lax.rem(ix + d, NX), iy), device_id_type=MESH)
        return carry

    def greet_y(d, carry):
        pl.semaphore_signal(barrier, inc=1, device_id=(ix, lax.rem(iy + d, NY)), device_id_type=MESH)
        return carry

    lax.fori_loop(1, NX, greet_x, 0)
    lax.fori_loop(1, NY, greet_y, 0)

    lane = lane_iota(CH)
    digit = [node_digit(a, lane) for a in range(3)]
    sg = [
        jnp.where(d == 3, 1.0, jnp.where(d == 0, -1.0, 0.0)).astype(F32) for d in digit
    ]
    bd3 = [jnp.where((d == 3) | (d == 0), lift_factor, 0.0).astype(F32) for d in digit]
    sg3 = [lift_factor * s for s in sg]
    swap = []
    for a in range(3):
        reach = 3 << (4 - 2 * a)
        base = lane if a < 2 else lane ^ 64
        swap.append(
            jnp.where(digit[a] == 0, base + reach, jnp.where(digit[a] == 3, base - reach, lane))
        )
    is3 = [digit[0] == 3, digit[1] == 3]
    low_bottom = (digit[2] == 0) & (lane < 64)
    high_top = (digit[2] == 3) & (lane >= 64)
    pick = 64 + 4 * (lane >> 3) + 3
    comp_lane = lane & 7

    def permute(value, index):
        return jnp.take_along_axis(value, index, axis=1)

    def faces(sec, r0, ee, hh):
        xt = pl.multiple_of(r0, CH)
        for a in range(3):
            b, c = (a + 1) % 3, (a + 2) % 3
            for pair in range(2):
                sums, moved = [], []
                for lp in range(2):
                    if pair == 0:
                        t = ee[lp][b] + sg[a] * hh[lp][c]
                    else:
                        t = ee[lp][c] - sg[a] * hh[lp][b]
                    sums.append(t)
                    moved.append(permute(t, swap[a]))
                for lp in range(2):
                    k = pair * 2 + lp
                    if a == 0:
                        gxb[sec, k, pl.ds(xt + 8, CH), :] = moved[lp]
                    elif a == 1:
                        gyb[sec, k, pl.ds(2 * xt + 8, 8), :] = moved[lp][0:8]
                        gyb[sec, k, pl.ds(2 * xt + 24, 8), :] = moved[lp][8:16]
                    elif lp == 0:
                        qz[k, pl.ds(xt, CH), :] = jnp.where(
                            low_bottom, -sums[0], jnp.where(high_top, moved[1], moved[0])
                        )
                    else:
                        qz[k, pl.ds(xt, CH), :] = jnp.where(
                            high_top, 0.0, jnp.where(low_bottom, moved[0], moved[1])
                        )
        for g in range(3):
            for e, side in enumerate((ee, hh)):
                for lp in range(2):
                    high, low = split2(side[lp][g])
                    rows = pl.ds((e * 2 + lp) * 128 + xt, CH)
                    xs[g, rows, 0:128] = high
                    xs[g, rows, 128:256] = low

    def trace_rows(r0, ee, hh):
        total = jnp.zeros((CH, 128), F32)
        for c in range(6):
            side = ee if c < 3 else hh
            total = jnp.where(comp_lane == c, permute(side[1][c % 3], pick), total)
        pay[pl.ds(r0, CH), :] = total

    def tiles(ref, r0):
        return [
            [ref[pl.ds(r0, CH), (c * 2 + lp) * 128 : (c * 2 + lp + 1) * 128] for c in range(6)]
            for lp in range(2)
        ]

    def halo_copies(sec):
        below = {"x": lax.rem(ix + NX - 1, NX), "y": lax.rem(iy + NY - 1, NY)}
        above = {"x": lax.rem(ix + 1, NX), "y": lax.rem(iy + 1, NY)}
        plan = [
            (gxb.at[sec, :, pl.ds(8, 8)], gxb.at[sec, :, pl.ds(136, 8)], (below["x"], iy)),
            (gxb.at[sec, :, pl.ds(128, 8)], gxb.at[sec, :, pl.ds(0, 8)], (above["x"], iy)),
            (hys.at[sec, 0], hyr.at[sec, 0], (ix, below["y"])),
            (hys.at[sec, 1], hyr.at[sec, 1], (ix, above["y"])),
        ]
        return [
            pltpu.make_async_remote_copy(
                src_ref=src, dst_ref=dst, send_sem=hs_sem.at[sec, n], recv_sem=hr_sem.at[sec, n],
                device_id=device, device_id_type=MESH,
            )
            for n, (src, dst, device) in enumerate(plan)
        ]

    def send_halo(sec):
        for k in range(4):
            hys[sec, 0, k] = gyb[sec, k, pl.ds(8, 16, stride=16), :]
            hys[sec, 1, k] = gyb[sec, k, pl.ds(15, 16, stride=16), :]
        for copy in halo_copies(sec):
            copy.start()

    def take_halo(sec):
        for copy in halo_copies(sec):
            copy.wait_recv()

        @pl.when(ix == NX - 1)
        def _():
            gxb[sec, :, 136:144, :] = jnp.zeros((4, 8, 128), F32)

        @pl.when(ix == 0)
        def _():
            gxb[sec, :, 0:8, :] = jnp.zeros((4, 8, 128), F32)

        has_up = jnp.where(iy == NY - 1, 0.0, 1.0).astype(F32)
        has_down = jnp.where(iy == 0, 0.0, 1.0).astype(F32)
        for k in range(4):
            gyb[sec, k, pl.ds(16, 16, stride=16), :] = hyr[sec, 0, k] * has_up
            gyb[sec, k, pl.ds(7, 16, stride=16), :] = hyr[sec, 1, k] * has_down

    def products():
        def one(g, carry):
            rr[g] = jnp.dot(xs[g], w1[g], preferred_element_type=F32) + jnp.dot(
                xs[g, :, 0:128], w2[g], preferred_element_type=F32
            )
            return carry

        lax.fori_loop(0, 3, one, 0)

    def finish(sec, r0):
        xt = pl.multiple_of(r0, CH)
        rows = pl.ds(xt, CH)
        new = [[None] * 6, [None] * 6]
        for lp in range(2):
            cols = [slice((c * 2 + lp) * 128, (c * 2 + lp + 1) * 128) for c in range(6)]
            val = [u[rows, cols[c]] for c in range(6)]
            tend = [None] * 6

            def add(c, term):
                tend[c] = term if tend[c] is None else tend[c] + term

            def slope(comp, axis):
                g, e = comp % 3, comp // 3
                half = 0 if axis == (g + 1) % 3 else 1
                return rr[g, pl.ds((e * 2 + lp) * 128 + xt, CH), half * 128 : half * 128 + 128]

            for a in range(3):
                b, c = (a + 1) % 3, (a + 2) % 3
                met = me[rows, (a * 2 + lp) * 128 : (a * 2 + lp + 1) * 128]
                q = []
                for pair in range(2):
                    k = pair * 2 + lp
                    if a == 0:
                        q.append(
                            jnp.where(
                                is3[0],
                                gxb[sec, k, pl.ds(xt + 16, CH), :],
                                gxb[sec, k, pl.ds(xt, CH), :],
                            )
                        )
                    elif a == 1:
                        up = jnp.concatenate(
                            [gyb[sec, k, pl.ds(2 * xt + 9, 8), :], gyb[sec, k, pl.ds(2 * xt + 25, 8), :]],
                            axis=0,
                        )
                        down = jnp.concatenate(
                            [gyb[sec, k, pl.ds(2 * xt + 7, 8), :], gyb[sec, k, pl.ds(2 * xt + 23, 8), :]],
                            axis=0,
                        )
                        q.append(jnp.where(is3[1], up, down))
                    else:
                        q.append(qz[k, rows, :])
                add(b, met * (bd3[a] * (q[0] - val[b]) - slope(c + 3, a)))
                add(c + 3, met * (-(sg3[a] * q[0]) - bd3[a] * val[c + 3] - slope(b, a)))
                add(c, met * (bd3[a] * (q[1] - val[c]) + slope(b + 3, a)))
                add(b + 3, met * (sg3[a] * q[1] - bd3[a] * val[b + 3] + slope(c, a)))
            scale = time_step / ep[rows, lp * 128 : (lp + 1) * 128]
            for c in range(6):
                rate = tend[c] * scale if c < 3 else tend[c] * time_step
                reg = section_decay[sec] * r[rows, cols[c]] + rate
                r[rows, cols[c]] = reg
                value = val[c] + section_gain[sec] * reg
                u[rows, cols[c]] = value
                new[lp][c] = value
        return new

    def stage1(sample):
        def make(d):
            peer = lax.rem(ix + d, NX)
            return pltpu.make_async_remote_copy(
                src_ref=og.at[sample, pl.ds(pl.multiple_of(peer * 16, 16), 16)],
                dst_ref=b1.at[sample, pl.ds(pl.multiple_of(ix * 16, 16), 16)],
                send_sem=s1_sem.at[sample, d], recv_sem=r1_sem.at[sample, d],
                device_id=(peer, iy), device_id_type=MESH,
            )
        return make

    def stage2(sample):
        def make(d):
            peer = lax.rem(iy + d, NY)
            return pltpu.make_async_remote_copy(
                src_ref=b2.at[sample, pl.ds(pl.multiple_of(peer * 32, 32), 32)],
                dst_ref=tb[sample].at[pl.ds(pl.multiple_of(iy * 32, 32), 32)],
                send_sem=s2_sem.at[sample, d], recv_sem=r2_sem.at[sample, d],
                device_id=(ix, peer), device_id_type=MESH,
            )
        return make

    def each(count, make, act):
        def body(d, carry):
            act(make(d))
            return carry

        lax.fori_loop(1, count, body, 0)

    def place(sample):
        value = pay[...]
        high, rest = value.astype(BF16), None
        rest = value - high.astype(F32)
        mid = rest.astype(BF16)
        low = (rest - mid.astype(F32)).astype(BF16)
        slot = jnp.broadcast_to(slots, (256, 128))
        where = lax.broadcasted_iota(jnp.int32, (256, 128), 0) == slot
        put = jnp.where(where, 1.0, 0.0).astype(BF16)
        og[sample] = (
            jnp.dot(put, high, preferred_element_type=F32)
            + jnp.dot(put, mid, preferred_element_type=F32)
        ) + jnp.dot(put, low, preferred_element_type=F32)
        own = pl.ds(pl.multiple_of(ix * 16, 16), 16)
        b1[sample, own, :] = og[sample, own, :]

    def forward(sample):
        each(NX, stage1(sample), lambda copy: copy.wait_recv())
        for g in range(NY):
            for side in range(2):
                b2[sample, pl.ds(g * 32 + side * 16, 16), :] = b1[
                    sample, pl.ds(g * 2 + side, 16, stride=16), :
                ]
        own = pl.ds(pl.multiple_of(iy * 32, 32), 32)
        tb[sample][own, :] = b2[sample, own, :]
        each(NY, stage2(sample), lambda copy: copy.start())

    loads[0].wait()
    loads[1].wait()

    def first_faces(ch, carry):
        r0 = ch * CH
        both = tiles(u, pl.multiple_of(r0, CH))
        ee = [both[lp][0:3] for lp in range(2)]
        hh = [both[lp][3:6] for lp in range(2)]
        faces(0, r0, ee, hh)
        trace_rows(pl.multiple_of(r0, CH), ee, hh)
        return carry

    lax.fori_loop(0, 128 // CH, first_faces, 0)

    targets = jnp.broadcast_to(rt[...], (128, 128))
    earlier = lax.broadcasted_iota(jnp.int32, (128, 128), 0) < lane_iota(128)
    same = jnp.where((targets.T == targets) & earlier, 1, 0)
    slots = rt[...] * 2 + jnp.sum(same, axis=0, keepdims=True)

    pl.semaphore_wait(barrier, NX - 1 + NY - 1)
    send_halo(0)
    place(0)
    each(NX, stage1(0), lambda copy: copy.start())

    loads[2].wait()
    loads[3].wait()
    products()

    for load in loads[4:]:
        load.wait()

    stv = st[...]
    slot_of = ((stv >> 1) & 7) * 32 + (stv & 1) * 16 + (stv >> 4)
    st[...] = slot_of
    along_u = basis(co[0])
    along_v = basis(co[1])
    for i in range(4):
        for j in range(4):
            wt[i * 4 + j] = along_u[i] * along_v[j]
    slot_iota = lax.broadcasted_iota(jnp.int32, (256, 128), 0)

    def one_hot(pp, carry):
        for h in range(2):
            row = jnp.broadcast_to(st[pl.ds(2 * pp + h, 1), :], (256, 128))
            oh[pp, :, h * 128 : h * 128 + 128] = jnp.where(slot_iota == row, 1.0, 0.0).astype(BF16)
        return carry

    lax.fori_loop(0, 32, one_hot, 0)

    forward(0)
    take_halo(0)

    def first_section(ch, carry):
        r0 = ch * CH
        new = finish(0, r0)
        ee = [new[lp][0:3] for lp in range(2)]
        hh = [new[lp][3:6] for lp in range(2)]
        faces(1, r0, ee, hh)
        trace_rows(pl.multiple_of(r0, CH), ee, hh)
        return carry

    lax.fori_loop(0, 128 // CH, first_section, 0)
    send_halo(1)
    place(1)
    each(NX, stage1(1), lambda copy: copy.start())
    products()
    each(NY, stage2(0), lambda copy: copy.wait_recv())
    interpolate(tb0[...], tt, oh, wt, pls)
    forward(1)
    take_halo(1)

    def second_section(ch, carry):
        finish(1, ch * CH)
        return carry

    lax.fori_loop(0, 128 // CH, second_section, 0)
    each(NY, stage2(1), lambda copy: copy.wait_recv())
    for sec in range(2):
        for copy in halo_copies(sec):
            copy.wait_send()
        each(NX, stage1(sec), lambda copy: copy.wait_send())
        each(NY, stage2(sec), lambda copy: copy.wait_send())


def on_device(fields, resid, permit, metric, route, stencil, coords):
    columns = fields.shape[0] * fields.shape[1]
    w1, w2 = stacked_tables()
    hbm = pl.BlockSpec(memory_space=pltpu.HBM)
    vmem = pl.BlockSpec(memory_space=pltpu.VMEM)
    dma = pltpu.SemaphoreType.DMA
    kept = (
        pltpu.VMEM((128, 1536), F32),
        pltpu.VMEM((128, 1536), F32),
        pltpu.VMEM((256, 128), F32),
        pltpu.VMEM((32, 256, 256), BF16),
        pltpu.VMEM((16, 64, 128), F32),
        pltpu.VMEM((512, 128), F32),
    )
    held = pl.pallas_call(
        kernel,
        out_shape=kept,
        in_specs=[hbm] * 9,
        out_specs=(vmem,) * len(kept),
        scratch_shapes=[
            pltpu.VMEM((128, 256), F32),
            pltpu.VMEM((128, 768), F32),
            pltpu.VMEM((1, 128), jnp.int32),
            pltpu.VMEM((64, 128), jnp.int32),
            pltpu.VMEM((2, 64, 128), F32),
            pltpu.VMEM((3, 256, 256), BF16),
            pltpu.VMEM((3, 128, 256), BF16),
            pltpu.VMEM((2, 4, 144, 128), F32),
            pltpu.VMEM((2, 4, 272, 128), F32),
            pltpu.VMEM((2, 2, 4, 16, 128), F32),
            pltpu.VMEM((2, 2, 4, 16, 128), F32),
            pltpu.VMEM((4, 128, 128), F32),
            pltpu.VMEM((3, 512, 256), BF16),
            pltpu.VMEM((3, 512, 256), F32),
            pltpu.VMEM((128, 128), F32),
            pltpu.VMEM((2, 256, 128), F32),
            pltpu.VMEM((2, 256, 128), F32),
            pltpu.VMEM((2, 256, 128), F32),
            pltpu.VMEM((256, 128), F32),
            pltpu.VMEM((256, 256), BF16),
            dma((9,)),
            dma((2, 4)),
            dma((2, 4)),
            dma((2, NX)),
            dma((2, NX)),
            dma((2, NY)),
            dma((2, NY)),
        ],
        compiler_params=pltpu.CompilerParams(
            collective_id=0, has_side_effects=True, vmem_limit_bytes=VMEM_A * 1024 * 1024
        ),
    )(
        fields.reshape(columns, 1536),
        resid.reshape(columns, 1536),
        permit.reshape(columns, 256),
        metric.reshape(columns, 768),
        route,
        stencil,
        coords,
        jnp.asarray(w1),
        jnp.asarray(w2),
    )
    f_out, r_out, plane = pl.pallas_call(
        last_kernel,
        out_shape=(
            jax.ShapeDtypeStruct((columns, 1536), F32),
            jax.ShapeDtypeStruct((columns, 1536), F32),
            jax.ShapeDtypeStruct((768, 128), F32),
        ),
        in_specs=[vmem] * len(kept),
        out_specs=(hbm,) * 3,
        scratch_shapes=[pltpu.VMEM((512, 128), F32), pltpu.VMEM((256, 256), BF16), dma((4,))],
        compiler_params=pltpu.CompilerParams(vmem_limit_bytes=VMEM_B * 1024 * 1024),
    )(*held)
    return (
        f_out.reshape(fields.shape),
        r_out.reshape(fields.shape),
        plane.reshape(12, stencil.shape[0], stencil.shape[1]),
    )


def solution(mesh):
    return jax.shard_map(
        on_device,
        mesh=mesh,
        in_specs=(
            P("gx", "gy", None),
            P("gx", "gy", None),
            P("gx", "gy", None),
            P("gx", "gy", None),
            P("gx", "gy"),
            P("gx", "gy"),
            P(None, "gx", "gy"),
        ),
        out_specs=(P("gx", "gy", None), P("gx", "gy", None), P(None, "gx", "gy")),
        check_vma=False,
    )
```

```python
import functools

import jax
import jax.numpy as jnp
import numpy as np
from jax import lax
from jax.experimental import pallas as pl
from jax.experimental.pallas import tpu as pltpu
from jax.sharding import PartitionSpec as P

section_decay = (-0.41789047449985195, -1.192151694642677)
section_gain = (0.37921031299962726, 0.8229550293869817)
time_step = 0.05
lift_factor = 3.0

MESH = pl.DeviceIdType.MESH
F32 = jnp.float32
BF16 = jnp.bfloat16
NX, NY = 16, 8
VMEM_A, VMEM_B = 54, 16
CH = 16


def gll_points():
    return np.array([-1.0, -np.sqrt(0.2), np.sqrt(0.2), 1.0])


def derivative_table():
    points = gll_points()
    barycentric = np.array(
        [1.0 / np.prod([points[j] - points[k] for k in range(4) if k != j]) for j in range(4)]
    )
    table = np.zeros((4, 4))
    for i in range(4):
        for j in range(4):
            if i != j:
                table[i, j] = barycentric[j] / barycentric[i] / (points[i] - points[j])
        table[i, i] = -np.sum(table[i])
    return table


def stacked_tables():
    table = derivative_table()
    table[3, 3] -= lift_factor
    table[0, 0] += lift_factor
    eye = np.eye(4)
    along = [
        np.kron(np.kron(table, eye), eye),
        np.kron(np.kron(eye, table), eye),
        np.kron(np.kron(eye, eye), table),
    ]
    two = [np.kron(np.eye(2), m).T for m in along]
    full = np.stack(
        [np.concatenate([two[(g + 1) % 3], two[(g + 2) % 3]], axis=1) for g in range(3)]
    ).astype(np.float32)
    high = full.astype(jnp.bfloat16)
    low = (full - high.astype(np.float32)).astype(jnp.bfloat16)
    return np.concatenate([high, high], axis=1), low


def lane_iota(rows):
    return lax.broadcasted_iota(jnp.int32, (rows, 128), 1)


def node_digit(axis, lane):
    return (lane >> (4 - 2 * axis)) & 3


def basis(coord):
    points = gll_points()
    listing = []
    for j in range(4):
        result = None
        for k in range(4):
            if k != j:
                term = (coord - float(points[k])) * float(1.0 / (points[j] - points[k]))
                result = term if result is None else result * term
        listing.append(result)
    return listing


def split2(value):
    high = value.astype(BF16)
    return high, (value - high.astype(F32)).astype(BF16)


def interpolate(table, tt, oh, wt, pls):
    high, low = split2(table.T)
    tt[0:128] = high
    tt[128:256] = low

    def rows_of(pp, carry):
        got = jnp.dot(tt[...], oh[pp], preferred_element_type=F32)
        for h in range(2):
            part = got[:, h * 128 : h * 128 + 128]
            total = None
            for n in range(16):
                both = part[n * 8 : n * 8 + 8] + part[128 + n * 8 : 136 + n * 8]
                term = both * wt[n, pl.ds(2 * pp + h, 1), :]
                total = term if total is None else total + term
            pls[pl.ds(2 * pp + h, 8, stride=64), :] = total
        return carry

    lax.fori_loop(0, 32, rows_of, 0, unroll=8)


def last_kernel(
    u, r, tb1, oh, wt, pls0, f_out, r_out, pl_out, pls1, tt, out_sem
):
    stores = [
        pltpu.make_async_copy(u, f_out, out_sem.at[0]),
        pltpu.make_async_copy(r, r_out, out_sem.at[1]),
        pltpu.make_async_copy(pls0.at[pl.ds(0, 384)], pl_out.at[pl.ds(0, 384)], out_sem.at[2]),
        pltpu.make_async_copy(pls1.at[pl.ds(0, 384)], pl_out.at[pl.ds(384, 384)], out_sem.at[3]),
    ]
    for store in stores[:3]:
        store.start()
    interpolate(tb1[...], tt, oh, wt, pls1)
    stores[3].start()
    for store in stores:
        store.wait()


def kernel(
    f_in, r_in, p_in, m_in, rt_in, st_in, co_in, w1_in, w2_in,
    u, r, tb1, oh, wt, pls,
    ep, me, rt, st, co, w1, w2,
    gxb, gyb, hys, hyr, qz, xs, rr, pay, og, b1, b2, tb0, nat, tt,
    in_sem, hs_sem, hr_sem, s1_sem, r1_sem, s2_sem, r2_sem, sd_sem, rd_sem, ready,
):
    ix = lax.axis_index("gx")
    iy = lax.axis_index("gy")

    loads = [
        pltpu.make_async_copy(src, dst, in_sem.at[n])
        for n, (src, dst) in enumerate(
            [(f_in, u), (rt_in, rt), (w1_in, w1), (w2_in, w2), (m_in, me), (r_in, r),
             (p_in, ep), (st_in, st), (co_in, co)]
        )
    ]
    for load in loads:
        load.start()

    barrier = pltpu.get_barrier_semaphore()

    def greet_x(d, carry):
        pl.semaphore_signal(barrier, inc=1, device_id=(lax.rem(ix + d, NX), iy), device_id_type=MESH)
        return carry

    def greet_y(d, carry):
        pl.semaphore_signal(barrier, inc=1, device_id=(ix, lax.rem(iy + d, NY)), device_id_type=MESH)
        return carry

    lax.fori_loop(1, NX, greet_x, 0)
    lax.fori_loop(1, NY, greet_y, 0)

    lane = lane_iota(CH)
    digit = [node_digit(a, lane) for a in range(3)]
    sg = [
        jnp.where(d == 3, 1.0, jnp.where(d == 0, -1.0, 0.0)).astype(F32) for d in digit
    ]
    bd3 = [jnp.where((d == 3) | (d == 0), lift_factor, 0.0).astype(F32) for d in digit]
    sg3 = [lift_factor * s for s in sg]
    swap = []
    for a in range(3):
        reach = 3 << (4 - 2 * a)
        base = lane if a < 2 else lane ^ 64
        swap.append(
            jnp.where(digit[a] == 0, base + reach, jnp.where(digit[a] == 3, base - reach, lane))
        )
    is3 = [digit[0] == 3, digit[1] == 3]
    low_bottom = (digit[2] == 0) & (lane < 64)
    high_top = (digit[2] == 3) & (lane >= 64)
    pick = 64 + 4 * (lane >> 3) + 3
    comp_lane = lane & 7

    def permute(value, index):
        return jnp.take_along_axis(value, index, axis=1)

    def faces(sec, r0, ee, hh):
        xt = pl.multiple_of(r0, CH)
        for a in range(3):
            b, c = (a + 1) % 3, (a + 2) % 3
            for pair in range(2):
                sums, moved = [], []
                for lp in range(2):
                    if pair == 0:
                        t = ee[lp][b] + sg[a] * hh[lp][c]
                    else:
                        t = ee[lp][c] - sg[a] * hh[lp][b]
                    sums.append(t)
                    moved.append(permute(t, swap[a]))
                for lp in range(2):
                    k = pair * 2 + lp
                    if a == 0:
                        gxb[sec, k, pl.ds(xt + 8, CH), :] = moved[lp]
                    elif a == 1:
                        gyb[sec, k, pl.ds(2 * xt + 8, 8), :] = moved[lp][0:8]
                        gyb[sec, k, pl.ds(2 * xt + 24, 8), :] = moved[lp][8:16]
                    elif lp == 0:
                        qz[k, pl.ds(xt, CH), :] = jnp.where(
                            low_bottom, -sums[0], jnp.where(high_top, moved[1], moved[0])
                        )
                    else:
                        qz[k, pl.ds(xt, CH), :] = jnp.where(
                            high_top, 0.0, jnp.where(low_bottom, moved[0], moved[1])
                        )
        for g in range(3):
            for e, side in enumerate((ee, hh)):
                for lp in range(2):
                    high, low = split2(side[lp][g])
                    rows = pl.ds((e * 2 + lp) * 128 + xt, CH)
                    xs[g, rows, 0:128] = high
                    xs[g, rows, 128:256] = low

    def trace_rows(r0, ee, hh):
        total = jnp.zeros((CH, 128), F32)
        for c in range(6):
            side = ee if c < 3 else hh
            total = jnp.where(comp_lane == c, permute(side[1][c % 3], pick), total)
        pay[pl.ds(r0, CH), :] = total

    def tiles(ref, r0):
        return [
            [ref[pl.ds(r0, CH), (c * 2 + lp) * 128 : (c * 2 + lp + 1) * 128] for c in range(6)]
            for lp in range(2)
        ]

    def halo_copies(sec):
        below = {"x": lax.rem(ix + NX - 1, NX), "y": lax.rem(iy + NY - 1, NY)}
        above = {"x": lax.rem(ix + 1, NX), "y": lax.rem(iy + 1, NY)}
        plan = [
            (gxb.at[sec, :, pl.ds(8, 8)], gxb.at[sec, :, pl.ds(136, 8)], (below["x"], iy)),
            (gxb.at[sec, :, pl.ds(128, 8)], gxb.at[sec, :, pl.ds(0, 8)], (above["x"], iy)),
            (hys.at[sec, 0], hyr.at[sec, 0], (ix, below["y"])),
            (hys.at[sec, 1], hyr.at[sec, 1], (ix, above["y"])),
        ]
        return [
            pltpu.make_async_remote_copy(
                src_ref=src, dst_ref=dst, send_sem=hs_sem.at[sec, n], recv_sem=hr_sem.at[sec, n],
                device_id=device, device_id_type=MESH,
            )
            for n, (src, dst, device) in enumerate(plan)
        ]

    def send_halo(sec):
        for k in range(4):
            hys[sec, 0, k] = gyb[sec, k, pl.ds(8, 16, stride=16), :]
            hys[sec, 1, k] = gyb[sec, k, pl.ds(15, 16, stride=16), :]
        for copy in halo_copies(sec):
            copy.start()

    def take_halo(sec):
        for copy in halo_copies(sec):
            copy.wait_recv()

        @pl.when(ix == NX - 1)
        def _():
            gxb[sec, :, 136:144, :] = jnp.zeros((4, 8, 128), F32)

        @pl.when(ix == 0)
        def _():
            gxb[sec, :, 0:8, :] = jnp.zeros((4, 8, 128), F32)

        has_up = jnp.where(iy == NY - 1, 0.0, 1.0).astype(F32)
        has_down = jnp.where(iy == 0, 0.0, 1.0).astype(F32)
        for k in range(4):
            gyb[sec, k, pl.ds(16, 16, stride=16), :] = hyr[sec, 0, k] * has_up
            gyb[sec, k, pl.ds(7, 16, stride=16), :] = hyr[sec, 1, k] * has_down

    def products():
        def one(g, carry):
            rr[g] = jnp.dot(xs[g], w1[g], preferred_element_type=F32) + jnp.dot(
                xs[g, :, 0:128], w2[g], preferred_element_type=F32
            )
            return carry

        lax.fori_loop(0, 3, one, 0)

    def finish(sec, r0):
        xt = pl.multiple_of(r0, CH)
        rows = pl.ds(xt, CH)
        new = [[None] * 6, [None] * 6]
        for lp in range(2):
            cols = [slice((c * 2 + lp) * 128, (c * 2 + lp + 1) * 128) for c in range(6)]
            val = [u[rows, cols[c]] for c in range(6)]
            tend = [None] * 6

            def add(c, term):
                tend[c] = term if tend[c] is None else tend[c] + term

            def slope(comp, axis):
                g, e = comp % 3, comp // 3
                half = 0 if axis == (g + 1) % 3 else 1
                return rr[g, pl.ds((e * 2 + lp) * 128 + xt, CH), half * 128 : half * 128 + 128]

            for a in range(3):
                b, c = (a + 1) % 3, (a + 2) % 3
                met = me[rows, (a * 2 + lp) * 128 : (a * 2 + lp + 1) * 128]
                q = []
                for pair in range(2):
                    k = pair * 2 + lp
                    if a == 0:
                        q.append(
                            jnp.where(
                                is3[0],
                                gxb[sec, k, pl.ds(xt + 16, CH), :],
                                gxb[sec, k, pl.ds(xt, CH), :],
                            )
                        )
                    elif a == 1:
                        up = jnp.concatenate(
                            [gyb[sec, k, pl.ds(2 * xt + 9, 8), :], gyb[sec, k, pl.ds(2 * xt + 25, 8), :]],
                            axis=0,
                        )
                        down = jnp.concatenate(
                            [gyb[sec, k, pl.ds(2 * xt + 7, 8), :], gyb[sec, k, pl.ds(2 * xt + 23, 8), :]],
                            axis=0,
                        )
                        q.append(jnp.where(is3[1], up, down))
                    else:
                        q.append(qz[k, rows, :])
                add(b, met * (bd3[a] * (q[0] - val[b]) - slope(c + 3, a)))
                add(c + 3, met * (-(sg3[a] * q[0]) - bd3[a] * val[c + 3] - slope(b, a)))
                add(c, met * (bd3[a] * (q[1] - val[c]) + slope(b + 3, a)))
                add(b + 3, met * (sg3[a] * q[1] - bd3[a] * val[b + 3] + slope(c, a)))
            scale = time_step / ep[rows, lp * 128 : (lp + 1) * 128]
            for c in range(6):
                rate = tend[c] * scale if c < 3 else tend[c] * time_step
                reg = section_decay[sec] * r[rows, cols[c]] + rate
                r[rows, cols[c]] = reg
                value = val[c] + section_gain[sec] * reg
                u[rows, cols[c]] = value
                new[lp][c] = value
        return new

    def stage1(d):
        peer = lax.rem(ix + d, NX)
        return pltpu.make_async_remote_copy(
            src_ref=og.at[0, pl.ds(pl.multiple_of(peer * 16, 16), 16)],
            dst_ref=b1.at[pl.ds(pl.multiple_of(ix * 16, 16), 16)],
            send_sem=s1_sem.at[d], recv_sem=r1_sem.at[d],
            device_id=(peer, iy), device_id_type=MESH,
        )

    def stage2(d):
        peer = lax.rem(iy + d, NY)
        return pltpu.make_async_remote_copy(
            src_ref=b2.at[pl.ds(pl.multiple_of(peer * 32, 32), 32)],
            dst_ref=tb0.at[pl.ds(pl.multiple_of(iy * 32, 32), 32)],
            send_sem=s2_sem.at[d], recv_sem=r2_sem.at[d],
            device_id=(ix, peer), device_id_type=MESH,
        )

    me_flat = ix * NY + iy

    def straight(d):
        peer = lax.rem(me_flat + d, NX * NY)
        return pltpu.make_async_remote_copy(
            src_ref=og.at[1, pl.ds(peer * 2, 2)],
            dst_ref=tb1.at[pl.ds(me_flat * 2, 2)],
            send_sem=sd_sem, recv_sem=rd_sem,
            device_id=(lax.div(peer, NY), lax.rem(peer, NY)), device_id_type=MESH,
        )

    def all_straight():
        whole = pl.ds(0, 2 * (NX * NY - 1))
        return pltpu.make_async_remote_copy(
            src_ref=og.at[1, whole], dst_ref=tb1.at[whole],
            send_sem=sd_sem, recv_sem=rd_sem,
            device_id=(lax.rem(ix + 1, NX), iy), device_id_type=MESH,
        )

    def each(count, make, act):
        def body(d, carry):
            act(make(d))
            return carry

        lax.fori_loop(1, count, body, 0)

    def place(sample):
        value = pay[...]
        high, rest = value.astype(BF16), None
        rest = value - high.astype(F32)
        mid = rest.astype(BF16)
        low = (rest - mid.astype(F32)).astype(BF16)
        slot = jnp.broadcast_to(slots, (256, 128))
        where = lax.broadcasted_iota(jnp.int32, (256, 128), 0) == slot
        put = jnp.where(where, 1.0, 0.0).astype(BF16)
        og[sample] = (
            jnp.dot(put, high, preferred_element_type=F32)
            + jnp.dot(put, mid, preferred_element_type=F32)
        ) + jnp.dot(put, low, preferred_element_type=F32)

    def forward():
        each(NX, stage1, lambda copy: copy.wait_recv())
        for g in range(NY):
            for side in range(2):
                b2[pl.ds(g * 32 + side * 16, 16), :] = b1[pl.ds(g * 2 + side, 16, stride=16), :]
        own = pl.ds(pl.multiple_of(iy * 32, 32), 32)
        tb0[own, :] = b2[own, :]
        each(NY, stage2, lambda copy: copy.start())

    def gathered():
        each(NY, stage2, lambda copy: copy.wait_recv())
        for g in range(NY):
            for side in range(2):
                nat[pl.ds(g * 2 + side, 16, stride=16), :] = tb0[pl.ds(g * 32 + side * 16, 16), :]
        return nat[...]

    loads[0].wait()
    loads[1].wait()

    def first_faces(ch, carry):
        r0 = ch * CH
        both = tiles(u, pl.multiple_of(r0, CH))
        ee = [both[lp][0:3] for lp in range(2)]
        hh = [both[lp][3:6] for lp in range(2)]
        faces(0, r0, ee, hh)
        trace_rows(pl.multiple_of(r0, CH), ee, hh)
        return carry

    lax.fori_loop(0, 128 // CH, first_faces, 0)

    targets = jnp.broadcast_to(rt[...], (128, 128))
    earlier = lax.broadcasted_iota(jnp.int32, (128, 128), 0) < lane_iota(128)
    same = jnp.where((targets.T == targets) & earlier, 1, 0)
    slots = rt[...] * 2 + jnp.sum(same, axis=0, keepdims=True)

    pl.semaphore_wait(barrier, NX - 1 + NY - 1)
    send_halo(0)

    def tell(d, carry):
        pl.semaphore_signal(ready, inc=1, device_id=(ix, lax.rem(iy + d, NY)), device_id_type=MESH)
        return carry

    lax.fori_loop(1, NY, tell, 0)
    place(0)
    own = pl.ds(pl.multiple_of(ix * 16, 16), 16)
    b1[own, :] = og[0, own, :]
    each(NX, stage1, lambda copy: copy.start())

    loads[2].wait()
    loads[3].wait()
    products()

    for load in loads[4:]:
        load.wait()

    along_u = basis(co[0])
    along_v = basis(co[1])
    for i in range(4):
        for j in range(4):
            wt[i * 4 + j] = along_u[i] * along_v[j]
    slot_iota = lax.broadcasted_iota(jnp.int32, (256, 128), 0)

    def one_hot(pp, carry):
        for h in range(2):
            row = jnp.broadcast_to(st[pl.ds(2 * pp + h, 1), :], (256, 128))
            oh[pp, :, h * 128 : h * 128 + 128] = jnp.where(slot_iota == row, 1.0, 0.0).astype(BF16)
        return carry

    lax.fori_loop(0, 32, one_hot, 0)

    take_halo(0)

    def first_section(ch, carry):
        r0 = ch * CH
        new = finish(0, r0)
        ee = [new[lp][0:3] for lp in range(2)]
        hh = [new[lp][3:6] for lp in range(2)]
        faces(1, r0, ee, hh)
        trace_rows(pl.multiple_of(r0, CH), ee, hh)
        return carry

    lax.fori_loop(0, 128 // CH, first_section, 0)
    place(1)
    pl.semaphore_wait(ready, NY - 1)
    each(NX * NY, straight, lambda copy: copy.start())
    send_halo(1)
    mine = pl.ds(me_flat * 2, 2)
    tb1[mine, :] = og[1, mine, :]
    forward()
    products()
    take_halo(1)

    def second_section(ch, carry):
        finish(1, ch * CH)
        return carry

    lax.fori_loop(0, 128 // CH, second_section, 0)
    interpolate(gathered(), tt, oh, wt, pls)
    all_straight().wait_recv()
    for sec in range(2):
        for copy in halo_copies(sec):
            copy.wait_send()
    each(NX, stage1, lambda copy: copy.wait_send())
    each(NY, stage2, lambda copy: copy.wait_send())
    all_straight().wait_send()


def on_device(fields, resid, permit, metric, route, stencil, coords):
    columns = fields.shape[0] * fields.shape[1]
    w1, w2 = stacked_tables()
    hbm = pl.BlockSpec(memory_space=pltpu.HBM)
    vmem = pl.BlockSpec(memory_space=pltpu.VMEM)
    dma = pltpu.SemaphoreType.DMA
    kept = (
        pltpu.VMEM((128, 1536), F32),
        pltpu.VMEM((128, 1536), F32),
        pltpu.VMEM((256, 128), F32),
        pltpu.VMEM((32, 256, 256), BF16),
        pltpu.VMEM((16, 64, 128), F32),
        pltpu.VMEM((512, 128), F32),
    )
    held = pl.pallas_call(
        kernel,
        out_shape=kept,
        in_specs=[hbm] * 9,
        out_specs=(vmem,) * len(kept),
        scratch_shapes=[
            pltpu.VMEM((128, 256), F32),
            pltpu.VMEM((128, 768), F32),
            pltpu.VMEM((1, 128), jnp.int32),
            pltpu.VMEM((64, 128), jnp.int32),
            pltpu.VMEM((2, 64, 128), F32),
            pltpu.VMEM((3, 256, 256), BF16),
            pltpu.VMEM((3, 128, 256), BF16),
            pltpu.VMEM((2, 4, 144, 128), F32),
            pltpu.VMEM((2, 4, 272, 128), F32),
            pltpu.VMEM((2, 2, 4, 16, 128), F32),
            pltpu.VMEM((2, 2, 4, 16, 128), F32),
            pltpu.VMEM((4, 128, 128), F32),
            pltpu.VMEM((3, 512, 256), BF16),
            pltpu.VMEM((3, 512, 256), F32),
            pltpu.VMEM((128, 128), F32),
            pltpu.VMEM((2, 256, 128), F32),
            pltpu.VMEM((256, 128), F32),
            pltpu.VMEM((256, 128), F32),
            pltpu.VMEM((256, 128), F32),
            pltpu.VMEM((256, 128), F32),
            pltpu.VMEM((256, 256), BF16),
            dma((9,)),
            dma((2, 4)),
            dma((2, 4)),
            dma((NX,)),
            dma((NX,)),
            dma((NY,)),
            dma((NY,)),
            dma,
            dma,
            pltpu.SemaphoreType.REGULAR,
        ],
        compiler_params=pltpu.CompilerParams(
            collective_id=0, has_side_effects=True, vmem_limit_bytes=VMEM_A * 1024 * 1024
        ),
    )(
        fields.reshape(columns, 1536),
        resid.reshape(columns, 1536),
        permit.reshape(columns, 256),
        metric.reshape(columns, 768),
        route,
        stencil,
        coords,
        jnp.asarray(w1),
        jnp.asarray(w2),
    )
    f_out, r_out, plane = pl.pallas_call(
        last_kernel,
        out_shape=(
            jax.ShapeDtypeStruct((columns, 1536), F32),
            jax.ShapeDtypeStruct((columns, 1536), F32),
            jax.ShapeDtypeStruct((768, 128), F32),
        ),
        in_specs=[vmem] * len(kept),
        out_specs=(hbm,) * 3,
        scratch_shapes=[pltpu.VMEM((512, 128), F32), pltpu.VMEM((256, 256), BF16), dma((4,))],
        compiler_params=pltpu.CompilerParams(vmem_limit_bytes=VMEM_B * 1024 * 1024),
    )(*held)
    return (
        f_out.reshape(fields.shape),
        r_out.reshape(fields.shape),
        plane.reshape(12, stencil.shape[0], stencil.shape[1]),
    )


def solution(mesh):
    return jax.shard_map(
        on_device,
        mesh=mesh,
        in_specs=(
            P("gx", "gy", None),
            P("gx", "gy", None),
            P("gx", "gy", None),
            P("gx", "gy", None),
            P("gx", "gy"),
            P("gx", "gy"),
            P(None, "gx", "gy"),
        ),
        out_specs=(P("gx", "gy", None), P("gx", "gy", None), P(None, "gx", "gy")),
        check_vma=False,
    )
```

```python
import functools

import jax
import jax.numpy as jnp
import numpy as np
from jax import lax
from jax.experimental import pallas as pl
from jax.experimental.pallas import tpu as pltpu
from jax.sharding import PartitionSpec as P

section_decay = (-0.41789047449985195, -1.192151694642677)
section_gain = (0.37921031299962726, 0.8229550293869817)
time_step = 0.05
lift_factor = 3.0

MESH = pl.DeviceIdType.MESH
F32 = jnp.float32
BF16 = jnp.bfloat16
NX, NY = 16, 8
VMEM_A, VMEM_B = 54, 16
CH = 16


def gll_points():
    return np.array([-1.0, -np.sqrt(0.2), np.sqrt(0.2), 1.0])


def derivative_table():
    points = gll_points()
    barycentric = np.array(
        [1.0 / np.prod([points[j] - points[k] for k in range(4) if k != j]) for j in range(4)]
    )
    table = np.zeros((4, 4))
    for i in range(4):
        for j in range(4):
            if i != j:
                table[i, j] = barycentric[j] / barycentric[i] / (points[i] - points[j])
        table[i, i] = -np.sum(table[i])
    return table


def stacked_tables():
    table = derivative_table()
    table[3, 3] -= lift_factor
    table[0, 0] += lift_factor
    eye = np.eye(4)
    along = [
        np.kron(np.kron(table, eye), eye),
        np.kron(np.kron(eye, table), eye),
        np.kron(np.kron(eye, eye), table),
    ]
    two = [np.kron(np.eye(2), m).T for m in along]
    full = np.stack(
        [np.concatenate([two[(g + 1) % 3], two[(g + 2) % 3]], axis=1) for g in range(3)]
    ).astype(np.float32)
    high = full.astype(jnp.bfloat16)
    low = (full - high.astype(np.float32)).astype(jnp.bfloat16)
    return np.concatenate([high, high], axis=1), low


def lane_iota(rows):
    return lax.broadcasted_iota(jnp.int32, (rows, 128), 1)


def node_digit(axis, lane):
    return (lane >> (4 - 2 * axis)) & 3


def basis(coord):
    points = gll_points()
    listing = []
    for j in range(4):
        result = None
        for k in range(4):
            if k != j:
                term = (coord - float(points[k])) * float(1.0 / (points[j] - points[k]))
                result = term if result is None else result * term
        listing.append(result)
    return listing


def split2(value):
    high = value.astype(BF16)
    return high, (value - high.astype(F32)).astype(BF16)


def interpolate(table, tt, oh, wt, pls):
    high, low = split2(table.T)
    tt[0:128] = high
    tt[128:256] = low

    def rows_of(pp, carry):
        got = jnp.dot(tt[...], oh[pp], preferred_element_type=F32)
        for h in range(2):
            part = got[:, h * 128 : h * 128 + 128]
            total = None
            for n in range(16):
                both = part[n * 8 : n * 8 + 8] + part[128 + n * 8 : 136 + n * 8]
                term = both * wt[n, pl.ds(2 * pp + h, 1), :]
                total = term if total is None else total + term
            pls[pl.ds(2 * pp + h, 8, stride=64), :] = total
        return carry

    lax.fori_loop(0, 32, rows_of, 0, unroll=8)


def last_kernel(
    u, r, tb1, oh, wt, pls0, f_out, r_out, pl_out, pls1, tt, out_sem
):
    stores = [
        pltpu.make_async_copy(u, f_out, out_sem.at[0]),
        pltpu.make_async_copy(r, r_out, out_sem.at[1]),
        pltpu.make_async_copy(pls0.at[pl.ds(0, 384)], pl_out.at[pl.ds(0, 384)], out_sem.at[2]),
        pltpu.make_async_copy(pls1.at[pl.ds(0, 384)], pl_out.at[pl.ds(384, 384)], out_sem.at[3]),
    ]
    for store in stores[:3]:
        store.start()
    interpolate(tb1[...], tt, oh, wt, pls1)
    stores[3].start()
    for store in stores:
        store.wait()


def kernel(
    f_in, r_in, p_in, m_in, rt_in, st_in, co_in, w1_in, w2_in,
    u, r, tb1, oh, wt, pls,
    ep, me, rt, st, co, w1, w2,
    gxb, gyb, hys, hyr, qz, xs, rr, pay, og, tb0, tt,
    in_sem, hs_sem, hr_sem, sd_sem, rd_sem, ready,
):
    tb = (tb0, tb1)
    ix = lax.axis_index("gx")
    iy = lax.axis_index("gy")

    loads = [
        pltpu.make_async_copy(src, dst, in_sem.at[n])
        for n, (src, dst) in enumerate(
            [(f_in, u), (rt_in, rt), (w1_in, w1), (w2_in, w2), (m_in, me), (r_in, r),
             (p_in, ep), (st_in, st), (co_in, co)]
        )
    ]
    for load in loads:
        load.start()

    barrier = pltpu.get_barrier_semaphore()

    def greet_x(d, carry):
        pl.semaphore_signal(barrier, inc=1, device_id=(lax.rem(ix + d, NX), iy), device_id_type=MESH)
        return carry

    def greet_y(d, carry):
        pl.semaphore_signal(barrier, inc=1, device_id=(ix, lax.rem(iy + d, NY)), device_id_type=MESH)
        return carry

    lax.fori_loop(1, NX, greet_x, 0)
    lax.fori_loop(1, NY, greet_y, 0)

    lane = lane_iota(CH)
    digit = [node_digit(a, lane) for a in range(3)]
    sg = [
        jnp.where(d == 3, 1.0, jnp.where(d == 0, -1.0, 0.0)).astype(F32) for d in digit
    ]
    bd3 = [jnp.where((d == 3) | (d == 0), lift_factor, 0.0).astype(F32) for d in digit]
    sg3 = [lift_factor * s for s in sg]
    swap = []
    for a in range(3):
        reach = 3 << (4 - 2 * a)
        base = lane if a < 2 else lane ^ 64
        swap.append(
            jnp.where(digit[a] == 0, base + reach, jnp.where(digit[a] == 3, base - reach, lane))
        )
    is3 = [digit[0] == 3, digit[1] == 3]
    low_bottom = (digit[2] == 0) & (lane < 64)
    high_top = (digit[2] == 3) & (lane >= 64)
    pick = 64 + 4 * (lane >> 3) + 3
    comp_lane = lane & 7

    def permute(value, index):
        return jnp.take_along_axis(value, index, axis=1)

    def faces(sec, r0, ee, hh):
        xt = pl.multiple_of(r0, CH)
        for a in range(3):
            b, c = (a + 1) % 3, (a + 2) % 3
            for pair in range(2):
                sums, moved = [], []
                for lp in range(2):
                    if pair == 0:
                        t = ee[lp][b] + sg[a] * hh[lp][c]
                    else:
                        t = ee[lp][c] - sg[a] * hh[lp][b]
                    sums.append(t)
                    moved.append(permute(t, swap[a]))
                for lp in range(2):
                    k = pair * 2 + lp
                    if a == 0:
                        gxb[sec, k, pl.ds(xt + 8, CH), :] = moved[lp]
                    elif a == 1:
                        gyb[sec, k, pl.ds(2 * xt + 8, 8), :] = moved[lp][0:8]
                        gyb[sec, k, pl.ds(2 * xt + 24, 8), :] = moved[lp][8:16]
                    elif lp == 0:
                        qz[k, pl.ds(xt, CH), :] = jnp.where(
                            low_bottom, -sums[0], jnp.where(high_top, moved[1], moved[0])
                        )
                    else:
                        qz[k, pl.ds(xt, CH), :] = jnp.where(
                            high_top, 0.0, jnp.where(low_bottom, moved[0], moved[1])
                        )
        for g in range(3):
            for e, side in enumerate((ee, hh)):
                for lp in range(2):
                    high, low = split2(side[lp][g])
                    rows = pl.ds((e * 2 + lp) * 128 + xt, CH)
                    xs[g, rows, 0:128] = high
                    xs[g, rows, 128:256] = low

    def trace_rows(r0, ee, hh):
        total = jnp.zeros((CH, 128), F32)
        for c in range(6):
            side = ee if c < 3 else hh
            total = jnp.where(comp_lane == c, permute(side[1][c % 3], pick), total)
        pay[pl.ds(r0, CH), :] = total

    def tiles(ref, r0):
        return [
            [ref[pl.ds(r0, CH), (c * 2 + lp) * 128 : (c * 2 + lp + 1) * 128] for c in range(6)]
            for lp in range(2)
        ]

    def halo_copies(sec):
        below = {"x": lax.rem(ix + NX - 1, NX), "y": lax.rem(iy + NY - 1, NY)}
        above = {"x": lax.rem(ix + 1, NX), "y": lax.rem(iy + 1, NY)}
        plan = [
            (gxb.at[sec, :, pl.ds(8, 8)], gxb.at[sec, :, pl.ds(136, 8)], (below["x"], iy)),
            (gxb.at[sec, :, pl.ds(128, 8)], gxb.at[sec, :, pl.ds(0, 8)], (above["x"], iy)),
            (hys.at[sec, 0], hyr.at[sec, 0], (ix, below["y"])),
            (hys.at[sec, 1], hyr.at[sec, 1], (ix, above["y"])),
        ]
        return [
            pltpu.make_async_remote_copy(
                src_ref=src, dst_ref=dst, send_sem=hs_sem.at[sec, n], recv_sem=hr_sem.at[sec, n],
                device_id=device, device_id_type=MESH,
            )
            for n, (src, dst, device) in enumerate(plan)
        ]

    def send_halo(sec):
        for k in range(4):
            hys[sec, 0, k] = gyb[sec, k, pl.ds(8, 16, stride=16), :]
            hys[sec, 1, k] = gyb[sec, k, pl.ds(15, 16, stride=16), :]
        for copy in halo_copies(sec):
            copy.start()

    def take_halo(sec):
        for copy in halo_copies(sec):
            copy.wait_recv()

        @pl.when(ix == NX - 1)
        def _():
            gxb[sec, :, 136:144, :] = jnp.zeros((4, 8, 128), F32)

        @pl.when(ix == 0)
        def _():
            gxb[sec, :, 0:8, :] = jnp.zeros((4, 8, 128), F32)

        has_up = jnp.where(iy == NY - 1, 0.0, 1.0).astype(F32)
        has_down = jnp.where(iy == 0, 0.0, 1.0).astype(F32)
        for k in range(4):
            gyb[sec, k, pl.ds(16, 16, stride=16), :] = hyr[sec, 0, k] * has_up
            gyb[sec, k, pl.ds(7, 16, stride=16), :] = hyr[sec, 1, k] * has_down

    def products():
        def one(g, carry):
            rr[g] = jnp.dot(xs[g], w1[g], preferred_element_type=F32) + jnp.dot(
                xs[g, :, 0:128], w2[g], preferred_element_type=F32
            )
            return carry

        lax.fori_loop(0, 3, one, 0)

    def finish(sec, r0):
        xt = pl.multiple_of(r0, CH)
        rows = pl.ds(xt, CH)
        new = [[None] * 6, [None] * 6]
        for lp in range(2):
            cols = [slice((c * 2 + lp) * 128, (c * 2 + lp + 1) * 128) for c in range(6)]
            val = [u[rows, cols[c]] for c in range(6)]
            tend = [None] * 6

            def add(c, term):
                tend[c] = term if tend[c] is None else tend[c] + term

            def slope(comp, axis):
                g, e = comp % 3, comp // 3
                half = 0 if axis == (g + 1) % 3 else 1
                return rr[g, pl.ds((e * 2 + lp) * 128 + xt, CH), half * 128 : half * 128 + 128]

            for a in range(3):
                b, c = (a + 1) % 3, (a + 2) % 3
                met = me[rows, (a * 2 + lp) * 128 : (a * 2 + lp + 1) * 128]
                q = []
                for pair in range(2):
                    k = pair * 2 + lp
                    if a == 0:
                        q.append(
                            jnp.where(
                                is3[0],
                                gxb[sec, k, pl.ds(xt + 16, CH), :],
                                gxb[sec, k, pl.ds(xt, CH), :],
                            )
                        )
                    elif a == 1:
                        up = jnp.concatenate(
                            [gyb[sec, k, pl.ds(2 * xt + 9, 8), :], gyb[sec, k, pl.ds(2 * xt + 25, 8), :]],
                            axis=0,
                        )
                        down = jnp.concatenate(
                            [gyb[sec, k, pl.ds(2 * xt + 7, 8), :], gyb[sec, k, pl.ds(2 * xt + 23, 8), :]],
                            axis=0,
                        )
                        q.append(jnp.where(is3[1], up, down))
                    else:
                        q.append(qz[k, rows, :])
                add(b, met * (bd3[a] * (q[0] - val[b]) - slope(c + 3, a)))
                add(c + 3, met * (-(sg3[a] * q[0]) - bd3[a] * val[c + 3] - slope(b, a)))
                add(c, met * (bd3[a] * (q[1] - val[c]) + slope(b + 3, a)))
                add(b + 3, met * (sg3[a] * q[1] - bd3[a] * val[b + 3] + slope(c, a)))
            scale = time_step / ep[rows, lp * 128 : (lp + 1) * 128]
            for c in range(6):
                rate = tend[c] * scale if c < 3 else tend[c] * time_step
                reg = section_decay[sec] * r[rows, cols[c]] + rate
                r[rows, cols[c]] = reg
                value = val[c] + section_gain[sec] * reg
                u[rows, cols[c]] = value
                new[lp][c] = value
        return new

    me_flat = ix * NY + iy

    def straight(sample):
        def make(d):
            peer = lax.rem(me_flat + d, NX * NY)
            return pltpu.make_async_remote_copy(
                src_ref=og.at[sample, pl.ds(peer * 2, 2)],
                dst_ref=tb[sample].at[pl.ds(me_flat * 2, 2)],
                send_sem=sd_sem.at[sample], recv_sem=rd_sem.at[sample],
                device_id=(lax.div(peer, NY), lax.rem(peer, NY)), device_id_type=MESH,
            )
        return make

    def all_straight(sample):
        whole = pl.ds(0, 2 * (NX * NY - 1))
        return pltpu.make_async_remote_copy(
            src_ref=og.at[sample, whole], dst_ref=tb[sample].at[whole],
            send_sem=sd_sem.at[sample], recv_sem=rd_sem.at[sample],
            device_id=(lax.rem(ix + 1, NX), iy), device_id_type=MESH,
        )

    def send_traces(sample):
        each(NX * NY, straight(sample), lambda copy: copy.start())
        mine = pl.ds(me_flat * 2, 2)
        tb[sample][mine, :] = og[sample, mine, :]

    def each(count, make, act):
        def body(d, carry):
            act(make(d))
            return carry

        lax.fori_loop(1, count, body, 0)

    def place(sample):
        value = pay[...]
        high, rest = value.astype(BF16), None
        rest = value - high.astype(F32)
        mid = rest.astype(BF16)
        low = (rest - mid.astype(F32)).astype(BF16)
        slot = jnp.broadcast_to(slots, (256, 128))
        where = lax.broadcasted_iota(jnp.int32, (256, 128), 0) == slot
        put = jnp.where(where, 1.0, 0.0).astype(BF16)
        og[sample] = (
            jnp.dot(put, high, preferred_element_type=F32)
            + jnp.dot(put, mid, preferred_element_type=F32)
        ) + jnp.dot(put, low, preferred_element_type=F32)

    loads[0].wait()
    loads[1].wait()

    def first_faces(ch, carry):
        r0 = ch * CH
        both = tiles(u, pl.multiple_of(r0, CH))
        ee = [both[lp][0:3] for lp in range(2)]
        hh = [both[lp][3:6] for lp in range(2)]
        faces(0, r0, ee, hh)
        trace_rows(pl.multiple_of(r0, CH), ee, hh)
        return carry

    lax.fori_loop(0, 128 // CH, first_faces, 0)

    targets = jnp.broadcast_to(rt[...], (128, 128))
    earlier = lax.broadcasted_iota(jnp.int32, (128, 128), 0) < lane_iota(128)
    same = jnp.where((targets.T == targets) & earlier, 1, 0)
    slots = rt[...] * 2 + jnp.sum(same, axis=0, keepdims=True)

    pl.semaphore_wait(barrier, NX - 1 + NY - 1)
    send_halo(0)

    def tell(d, carry):
        pl.semaphore_signal(ready, inc=1, device_id=(ix, lax.rem(iy + d, NY)), device_id_type=MESH)
        return carry

    lax.fori_loop(1, NY, tell, 0)
    place(0)

    loads[2].wait()
    loads[3].wait()
    products()

    for load in loads[4:]:
        load.wait()

    along_u = basis(co[0])
    along_v = basis(co[1])
    for i in range(4):
        for j in range(4):
            wt[i * 4 + j] = along_u[i] * along_v[j]
    slot_iota = lax.broadcasted_iota(jnp.int32, (256, 128), 0)

    def one_hot(pp, carry):
        for h in range(2):
            row = jnp.broadcast_to(st[pl.ds(2 * pp + h, 1), :], (256, 128))
            oh[pp, :, h * 128 : h * 128 + 128] = jnp.where(slot_iota == row, 1.0, 0.0).astype(BF16)
        return carry

    lax.fori_loop(0, 32, one_hot, 0)

    pl.semaphore_wait(ready, NY - 1)
    send_traces(0)
    take_halo(0)

    def first_section(ch, carry):
        r0 = ch * CH
        new = finish(0, r0)
        ee = [new[lp][0:3] for lp in range(2)]
        hh = [new[lp][3:6] for lp in range(2)]
        faces(1, r0, ee, hh)
        trace_rows(pl.multiple_of(r0, CH), ee, hh)
        return carry

    lax.fori_loop(0, 128 // CH, first_section, 0)
    place(1)
    send_traces(1)
    send_halo(1)
    products()
    all_straight(0).wait_recv()
    interpolate(tb0[...], tt, oh, wt, pls)
    take_halo(1)

    def second_section(ch, carry):
        finish(1, ch * CH)
        return carry

    lax.fori_loop(0, 128 // CH, second_section, 0)
    all_straight(1).wait_recv()
    for sec in range(2):
        for copy in halo_copies(sec):
            copy.wait_send()
        all_straight(sec).wait_send()


def on_device(fields, resid, permit, metric, route, stencil, coords):
    columns = fields.shape[0] * fields.shape[1]
    w1, w2 = stacked_tables()
    hbm = pl.BlockSpec(memory_space=pltpu.HBM)
    vmem = pl.BlockSpec(memory_space=pltpu.VMEM)
    dma = pltpu.SemaphoreType.DMA
    kept = (
        pltpu.VMEM((128, 1536), F32),
        pltpu.VMEM((128, 1536), F32),
        pltpu.VMEM((256, 128), F32),
        pltpu.VMEM((32, 256, 256), BF16),
        pltpu.VMEM((16, 64, 128), F32),
        pltpu.VMEM((512, 128), F32),
    )
    held = pl.pallas_call(
        kernel,
        out_shape=kept,
        in_specs=[hbm] * 9,
        out_specs=(vmem,) * len(kept),
        scratch_shapes=[
            pltpu.VMEM((128, 256), F32),
            pltpu.VMEM((128, 768), F32),
            pltpu.VMEM((1, 128), jnp.int32),
            pltpu.VMEM((64, 128), jnp.int32),
            pltpu.VMEM((2, 64, 128), F32),
            pltpu.VMEM((3, 256, 256), BF16),
            pltpu.VMEM((3, 128, 256), BF16),
            pltpu.VMEM((2, 4, 144, 128), F32),
            pltpu.VMEM((2, 4, 272, 128), F32),
            pltpu.VMEM((2, 2, 4, 16, 128), F32),
            pltpu.VMEM((2, 2, 4, 16, 128), F32),
            pltpu.VMEM((4, 128, 128), F32),
            pltpu.VMEM((3, 512, 256), BF16),
            pltpu.VMEM((3, 512, 256), F32),
            pltpu.VMEM((128, 128), F32),
            pltpu.VMEM((2, 256, 128), F32),
            pltpu.VMEM((256, 128), F32),
            pltpu.VMEM((256, 256), BF16),
            dma((9,)),
            dma((2, 4)),
            dma((2, 4)),
            dma((2,)),
            dma((2,)),
            pltpu.SemaphoreType.REGULAR,
        ],
        compiler_params=pltpu.CompilerParams(
            collective_id=0, has_side_effects=True, vmem_limit_bytes=VMEM_A * 1024 * 1024
        ),
    )(
        fields.reshape(columns, 1536),
        resid.reshape(columns, 1536),
        permit.reshape(columns, 256),
        metric.reshape(columns, 768),
        route,
        stencil,
        coords,
        jnp.asarray(w1),
        jnp.asarray(w2),
    )
    f_out, r_out, plane = pl.pallas_call(
        last_kernel,
        out_shape=(
            jax.ShapeDtypeStruct((columns, 1536), F32),
            jax.ShapeDtypeStruct((columns, 1536), F32),
            jax.ShapeDtypeStruct((768, 128), F32),
        ),
        in_specs=[vmem] * len(kept),
        out_specs=(hbm,) * 3,
        scratch_shapes=[pltpu.VMEM((512, 128), F32), pltpu.VMEM((256, 256), BF16), dma((4,))],
        compiler_params=pltpu.CompilerParams(vmem_limit_bytes=VMEM_B * 1024 * 1024),
    )(*held)
    return (
        f_out.reshape(fields.shape),
        r_out.reshape(fields.shape),
        plane.reshape(12, stencil.shape[0], stencil.shape[1]),
    )


def solution(mesh):
    return jax.shard_map(
        on_device,
        mesh=mesh,
        in_specs=(
            P("gx", "gy", None),
            P("gx", "gy", None),
            P("gx", "gy", None),
            P("gx", "gy", None),
            P("gx", "gy"),
            P("gx", "gy"),
            P(None, "gx", "gy"),
        ),
        out_specs=(P("gx", "gy", None), P("gx", "gy", None), P(None, "gx", "gy")),
        check_vma=False,
    )
```

```python
import functools

import jax
import jax.numpy as jnp
import numpy as np
from jax import lax
from jax.experimental import pallas as pl
from jax.experimental.pallas import tpu as pltpu
from jax.sharding import PartitionSpec as P

section_decay = (-0.41789047449985195, -1.192151694642677)
section_gain = (0.37921031299962726, 0.8229550293869817)
time_step = 0.05
lift_factor = 3.0

MESH = pl.DeviceIdType.MESH
F32 = jnp.float32
BF16 = jnp.bfloat16
NX, NY = 16, 8
VMEM_A, VMEM_B = 54, 16
CH = 16


def gll_points():
    return np.array([-1.0, -np.sqrt(0.2), np.sqrt(0.2), 1.0])


def derivative_table():
    points = gll_points()
    barycentric = np.array(
        [1.0 / np.prod([points[j] - points[k] for k in range(4) if k != j]) for j in range(4)]
    )
    table = np.zeros((4, 4))
    for i in range(4):
        for j in range(4):
            if i != j:
                table[i, j] = barycentric[j] / barycentric[i] / (points[i] - points[j])
        table[i, i] = -np.sum(table[i])
    return table


def stacked_tables():
    table = derivative_table()
    table[3, 3] -= lift_factor
    table[0, 0] += lift_factor
    eye = np.eye(4)
    along = [
        np.kron(np.kron(table, eye), eye),
        np.kron(np.kron(eye, table), eye),
        np.kron(np.kron(eye, eye), table),
    ]
    two = [np.kron(np.eye(2), m).T for m in along]
    full = np.stack(
        [np.concatenate([two[(g + 1) % 3], two[(g + 2) % 3]], axis=1) for g in range(3)]
    ).astype(np.float32)
    high = full.astype(jnp.bfloat16)
    low = (full - high.astype(np.float32)).astype(jnp.bfloat16)
    return np.concatenate([high, high], axis=1), low


def lane_iota(rows):
    return lax.broadcasted_iota(jnp.int32, (rows, 128), 1)


def node_digit(axis, lane):
    return (lane >> (4 - 2 * axis)) & 3


def basis(coord):
    points = gll_points()
    listing = []
    for j in range(4):
        result = None
        for k in range(4):
            if k != j:
                term = (coord - float(points[k])) * float(1.0 / (points[j] - points[k]))
                result = term if result is None else result * term
        listing.append(result)
    return listing


def split2(value):
    high = value.astype(BF16)
    return high, (value - high.astype(F32)).astype(BF16)


def interpolate(table, tt, oh, wt, pls, done=None):
    high, low = split2(table.T)
    tt[0:128] = high
    tt[128:256] = low

    def rows_of(pp, carry):
        got = jnp.dot(tt[...], oh[pp], preferred_element_type=F32)
        for h in range(2):
            part = got[:, h * 128 : h * 128 + 128]
            total = None
            for n in range(16):
                both = part[n * 8 : n * 8 + 8] + part[128 + n * 8 : 136 + n * 8]
                term = both * wt[n, pl.ds(2 * pp + h, 1), :]
                total = term if total is None else total + term
            pls[pl.ds(2 * pp + h, 8, stride=64), :] = total
        return carry

    if done is None:
        lax.fori_loop(0, 32, rows_of, 0, unroll=8)
    else:
        for q in range(4):
            lax.fori_loop(8 * q, 8 * q + 8, rows_of, 0, unroll=8)
            done(q)


def last_kernel(
    u, r, tb1, oh, wt, pls0, f_out, r_out, pl_out, pls1, tt, out_sem
):
    stores = [
        pltpu.make_async_copy(u, f_out, out_sem.at[0]),
        pltpu.make_async_copy(r, r_out, out_sem.at[1]),
        pltpu.make_async_copy(pls0.at[pl.ds(0, 384)], pl_out.at[pl.ds(0, 384)], out_sem.at[2]),
    ] + [
        pltpu.make_async_copy(
            pls1.at[pl.ds(64 * c + 16 * q, 16)],
            pl_out.at[pl.ds(384 + 64 * c + 16 * q, 16)],
            out_sem.at[3 + 6 * q + c],
        )
        for q in range(4)
        for c in range(6)
    ]
    for store in stores[:3]:
        store.start()
    def done(q):
        for store in stores[3 + 6 * q : 9 + 6 * q]:
            store.start()

    interpolate(tb1[...], tt, oh, wt, pls1, done)
    for store in stores:
        store.wait()


def kernel(
    f_in, r_in, p_in, m_in, rt_in, st_in, co_in, w1_in, w2_in,
    u, r, tb1, oh, wt, pls,
    ep, me, rt, st, co, w1, w2,
    gxb, gyb, hys, hxr, hyr, qz, xs, rr, pay, og, tb0, tt,
    in_sem, hs_sem, hr_sem, sd_sem, rd_sem, ready,
):
    tb = (tb0, tb1)
    ix = lax.axis_index("gx")
    iy = lax.axis_index("gy")

    loads = [
        pltpu.make_async_copy(src, dst, in_sem.at[n])
        for n, (src, dst) in enumerate(
            [(f_in, u), (rt_in, rt), (w1_in, w1), (w2_in, w2), (m_in, me), (r_in, r),
             (p_in, ep), (st_in, st), (co_in, co)]
        )
    ]
    loads[0].start()

    barrier = pltpu.get_barrier_semaphore()

    def greet_x(d, carry):
        pl.semaphore_signal(barrier, inc=1, device_id=(lax.rem(ix + d, NX), iy), device_id_type=MESH)
        return carry

    def greet_y(d, carry):
        pl.semaphore_signal(barrier, inc=1, device_id=(ix, lax.rem(iy + d, NY)), device_id_type=MESH)
        return carry

    lax.fori_loop(1, NX, greet_x, 0)
    lax.fori_loop(1, NY, greet_y, 0)
    for load in loads[1:]:
        load.start()

    lane = lane_iota(CH)
    digit = [node_digit(a, lane) for a in range(3)]
    sg = [
        jnp.where(d == 3, 1.0, jnp.where(d == 0, -1.0, 0.0)).astype(F32) for d in digit
    ]
    bd3 = [jnp.where((d == 3) | (d == 0), lift_factor, 0.0).astype(F32) for d in digit]
    sg3 = [lift_factor * s for s in sg]
    swap = []
    for a in range(3):
        reach = 3 << (4 - 2 * a)
        base = lane if a < 2 else lane ^ 64
        swap.append(
            jnp.where(digit[a] == 0, base + reach, jnp.where(digit[a] == 3, base - reach, lane))
        )
    is3 = [digit[0] == 3, digit[1] == 3]
    low_bottom = (digit[2] == 0) & (lane < 64)
    high_top = (digit[2] == 3) & (lane >= 64)
    pick = 64 + 4 * (lane >> 3) + 3
    comp_lane = lane & 7

    def permute(value, index):
        return jnp.take_along_axis(value, index, axis=1)

    def faces(sec, r0, ee, hh):
        xt = pl.multiple_of(r0, CH)
        for a in range(3):
            b, c = (a + 1) % 3, (a + 2) % 3
            for pair in range(2):
                sums, moved = [], []
                for lp in range(2):
                    if pair == 0:
                        t = ee[lp][b] + sg[a] * hh[lp][c]
                    else:
                        t = ee[lp][c] - sg[a] * hh[lp][b]
                    sums.append(t)
                    moved.append(permute(t, swap[a]))
                for lp in range(2):
                    k = pair * 2 + lp
                    if a == 0:
                        gxb[sec, k, pl.ds(xt + 8, CH), :] = moved[lp]
                    elif a == 1:
                        gyb[sec, k, pl.ds(2 * xt + 8, 8), :] = moved[lp][0:8]
                        gyb[sec, k, pl.ds(2 * xt + 24, 8), :] = moved[lp][8:16]
                    elif lp == 0:
                        qz[k, pl.ds(xt, CH), :] = jnp.where(
                            low_bottom, -sums[0], jnp.where(high_top, moved[1], moved[0])
                        )
                    else:
                        qz[k, pl.ds(xt, CH), :] = jnp.where(
                            high_top, 0.0, jnp.where(low_bottom, moved[0], moved[1])
                        )
        for g in range(3):
            for e, side in enumerate((ee, hh)):
                for lp in range(2):
                    high, low = split2(side[lp][g])
                    rows = pl.ds((e * 2 + lp) * 128 + xt, CH)
                    xs[g, rows, 0:128] = high
                    xs[g, rows, 128:256] = low

    def trace_rows(r0, ee, hh):
        total = jnp.zeros((CH, 128), F32)
        for c in range(6):
            side = ee if c < 3 else hh
            total = jnp.where(comp_lane == c, permute(side[1][c % 3], pick), total)
        pay[pl.ds(r0, CH), :] = total

    def tiles(ref, r0):
        return [
            [ref[pl.ds(r0, CH), (c * 2 + lp) * 128 : (c * 2 + lp + 1) * 128] for c in range(6)]
            for lp in range(2)
        ]

    def halo_copies(sec):
        below = {"x": lax.rem(ix + NX - 1, NX), "y": lax.rem(iy + NY - 1, NY)}
        above = {"x": lax.rem(ix + 1, NX), "y": lax.rem(iy + 1, NY)}
        plan = [
            (gxb.at[sec, :, pl.ds(8, 8)], hxr.at[sec, 0], (below["x"], iy)),
            (gxb.at[sec, :, pl.ds(128, 8)], hxr.at[sec, 1], (above["x"], iy)),
            (hys.at[sec, 0], hyr.at[sec, 0], (ix, below["y"])),
            (hys.at[sec, 1], hyr.at[sec, 1], (ix, above["y"])),
        ]
        return [
            pltpu.make_async_remote_copy(
                src_ref=src, dst_ref=dst, send_sem=hs_sem.at[sec, n], recv_sem=hr_sem.at[sec, n],
                device_id=device, device_id_type=MESH,
            )
            for n, (src, dst, device) in enumerate(plan)
        ]

    def send_halo(sec):
        for k in range(4):
            hys[sec, 0, k] = gyb[sec, k, pl.ds(8, 16, stride=16), :]
            hys[sec, 1, k] = gyb[sec, k, pl.ds(15, 16, stride=16), :]
        for copy in halo_copies(sec):
            copy.start()

    above_is = [
        jnp.where(ix == NX - 1, 0.0, 1.0).astype(F32), jnp.where(iy == NY - 1, 0.0, 1.0).astype(F32)
    ]
    below_is = [jnp.where(ix == 0, 0.0, 1.0).astype(F32), jnp.where(iy == 0, 0.0, 1.0).astype(F32)]

    def beside_y(sec, k, xt):
        up, down = (
            jnp.concatenate(
                [gyb[sec, k, pl.ds(2 * xt + at, 8), :], gyb[sec, k, pl.ds(2 * xt + at + 16, 8), :]],
                axis=0,
            )
            for at in (9, 7)
        )
        return jnp.where(is3[1], up, down)

    def no_halo(sec):
        none = jnp.zeros((16, 128), F32)
        for k in range(4):
            gxb[sec, k, 136:144, :] = none[0:8]
            gxb[sec, k, 0:8, :] = none[0:8]
            gyb[sec, k, pl.ds(16, 16, stride=16), :] = none
            gyb[sec, k, pl.ds(7, 16, stride=16), :] = none

    def take_halo(sec):
        for copy in halo_copies(sec):
            copy.wait_recv()
        for k in range(4):
            gxb[sec, k, 136:144, :] = hxr[sec, 0, k] * above_is[0]
            gxb[sec, k, 0:8, :] = hxr[sec, 1, k] * below_is[0]
            gyb[sec, k, pl.ds(16, 16, stride=16), :] = hyr[sec, 0, k] * above_is[1]
            gyb[sec, k, pl.ds(7, 16, stride=16), :] = hyr[sec, 1, k] * below_is[1]

    def add_halo(sec):
        take_halo(sec)

        def share(rows, a, lp, mask, sign, values):
            b, c = (a + 1) % 3, (a + 2) % 3
            met = me[rows, (a * 2 + lp) * 128 : (a * 2 + lp + 1) * 128] * mask
            scale = time_step / ep[rows, lp * 128 : (lp + 1) * 128]
            for pair, e_comp, h_comp in ((0, b, c + 3), (1, c, b + 3)):
                flux = met * values[pair]
                turned = flux * (-sign if pair == 0 else sign)
                for comp, rate in ((e_comp, flux * scale), (h_comp, turned)):
                    cols = slice((comp * 2 + lp) * 128, (comp * 2 + lp + 1) * 128)
                    r[rows, cols] += rate
                    u[rows, cols] += section_gain[sec] * rate

        for side in range(2):
            rows = pl.ds(120 * side, 8)
            mask = jnp.where(node_digit(0, lane_iota(8)) == 3 * side, lift_factor, 0.0)
            sign = time_step * (2.0 * side - 1.0)
            for lp in range(2):
                share(
                    rows, 0, lp, mask, sign,
                    [gxb[sec, pair * 2 + lp, 136 * side : 136 * side + 8, :] for pair in range(2)],
                )
        col_y = lax.broadcasted_iota(jnp.int32, (CH, 128), 0) & 7
        edge = ((digit[1] == 0) & (col_y == 0)) | (is3[1] & (col_y == 7))
        mask = jnp.where(edge, lift_factor, 0.0)
        sign = time_step * sg[1]

        def rows_y(ch, carry):
            r0 = pl.multiple_of(ch * CH, CH)
            for lp in range(2):
                share(
                    pl.ds(r0, CH), 1, lp, mask, sign,
                    [beside_y(sec, pair * 2 + lp, r0) for pair in range(2)],
                )
            return carry

        lax.fori_loop(0, 128 // CH, rows_y, 0, unroll=8)

    def products():
        def one(g, carry):
            rr[g] = jnp.dot(xs[g], w1[g], preferred_element_type=F32) + jnp.dot(
                xs[g, :, 0:128], w2[g], preferred_element_type=F32
            )
            return carry

        lax.fori_loop(0, 3, one, 0, unroll=3)

    def finish(sec, r0):
        xt = pl.multiple_of(r0, CH)
        rows = pl.ds(xt, CH)
        new = [[None] * 6, [None] * 6]
        for lp in range(2):
            cols = [slice((c * 2 + lp) * 128, (c * 2 + lp + 1) * 128) for c in range(6)]
            val = [u[rows, cols[c]] for c in range(6)]
            tend = [None] * 6

            def add(c, term):
                tend[c] = term if tend[c] is None else tend[c] + term

            def slope(comp, axis):
                g, e = comp % 3, comp // 3
                half = 0 if axis == (g + 1) % 3 else 1
                return rr[g, pl.ds((e * 2 + lp) * 128 + xt, CH), half * 128 : half * 128 + 128]

            for a in range(3):
                b, c = (a + 1) % 3, (a + 2) % 3
                met = me[rows, (a * 2 + lp) * 128 : (a * 2 + lp + 1) * 128]
                q = []
                for pair in range(2):
                    k = pair * 2 + lp
                    if a == 0:
                        q.append(
                            jnp.where(
                                is3[0],
                                gxb[sec, k, pl.ds(xt + 16, CH), :],
                                gxb[sec, k, pl.ds(xt, CH), :],
                            )
                        )
                    elif a == 1:
                        q.append(beside_y(sec, k, xt))
                    else:
                        q.append(qz[k, rows, :])
                add(b, met * (bd3[a] * (q[0] - val[b]) - slope(c + 3, a)))
                add(c + 3, met * (-(sg3[a] * q[0]) - bd3[a] * val[c + 3] - slope(b, a)))
                add(c, met * (bd3[a] * (q[1] - val[c]) + slope(b + 3, a)))
                add(b + 3, met * (sg3[a] * q[1] - bd3[a] * val[b + 3] + slope(c, a)))
            scale = time_step / ep[rows, lp * 128 : (lp + 1) * 128]
            for c in range(6):
                rate = tend[c] * scale if c < 3 else tend[c] * time_step
                reg = section_decay[sec] * r[rows, cols[c]] + rate
                r[rows, cols[c]] = reg
                value = val[c] + section_gain[sec] * reg
                u[rows, cols[c]] = value
                new[lp][c] = value
        return new

    me_flat = ix * NY + iy

    def straight(sample):
        def make(d):
            peer = lax.rem(me_flat + d, NX * NY)
            return pltpu.make_async_remote_copy(
                src_ref=og.at[sample, pl.ds(peer * 2, 2)],
                dst_ref=tb[sample].at[pl.ds(me_flat * 2, 2)],
                send_sem=sd_sem.at[sample], recv_sem=rd_sem.at[sample],
                device_id=(lax.div(peer, NY), lax.rem(peer, NY)), device_id_type=MESH,
            )
        return make

    def all_straight(sample):
        whole = pl.ds(0, 2 * (NX * NY - 1))
        return pltpu.make_async_remote_copy(
            src_ref=og.at[sample, whole], dst_ref=tb[sample].at[whole],
            send_sem=sd_sem.at[sample], recv_sem=rd_sem.at[sample],
            device_id=(lax.rem(ix + 1, NX), iy), device_id_type=MESH,
        )

    def send_traces(sample):
        each(NX * NY, straight(sample), lambda copy: copy.start())
        mine = pl.ds(me_flat * 2, 2)
        tb[sample][mine, :] = og[sample, mine, :]

    def each(count, make, act):
        def body(d, carry):
            act(make(d))
            return carry

        lax.fori_loop(1, count, body, 0)

    def place(sample):
        value = pay[...]
        high, rest = value.astype(BF16), None
        rest = value - high.astype(F32)
        mid = rest.astype(BF16)
        low = (rest - mid.astype(F32)).astype(BF16)
        slot = jnp.broadcast_to(slots, (256, 128))
        where = lax.broadcasted_iota(jnp.int32, (256, 128), 0) == slot
        put = jnp.where(where, 1.0, 0.0).astype(BF16)
        og[sample] = (
            jnp.dot(put, high, preferred_element_type=F32)
            + jnp.dot(put, mid, preferred_element_type=F32)
        ) + jnp.dot(put, low, preferred_element_type=F32)

    loads[0].wait()
    loads[1].wait()

    def first_faces(ch, carry):
        r0 = ch * CH
        both = tiles(u, pl.multiple_of(r0, CH))
        ee = [both[lp][0:3] for lp in range(2)]
        hh = [both[lp][3:6] for lp in range(2)]
        faces(0, r0, ee, hh)
        trace_rows(pl.multiple_of(r0, CH), ee, hh)
        return carry

    lax.fori_loop(0, 128 // CH, first_faces, 0, unroll=2)

    targets = jnp.broadcast_to(rt[...], (128, 128))
    earlier = lax.broadcasted_iota(jnp.int32, (128, 128), 0) < lane_iota(128)
    same = jnp.where((targets.T == targets) & earlier, 1, 0)
    slots = rt[...] * 2 + jnp.sum(same, axis=0, keepdims=True)

    pl.semaphore_wait(barrier, NX - 1 + NY - 1)
    send_halo(0)

    def tell(d, carry):
        pl.semaphore_signal(ready, inc=1, device_id=(ix, lax.rem(iy + d, NY)), device_id_type=MESH)
        return carry

    lax.fori_loop(1, NY, tell, 0)
    place(0)

    no_halo(0)
    for load in loads[2:7]:
        load.wait()
    products()

    def own_section(ch, carry):
        finish(0, ch * CH)
        return carry

    lax.fori_loop(0, 128 // CH, own_section, 0, unroll=4)
    pl.semaphore_wait(ready, NY - 1)
    send_traces(0)
    add_halo(0)

    def second_traces(ch, carry):
        r0 = pl.multiple_of(ch * CH, CH)
        both = tiles(u, r0)
        trace_rows(r0, [both[lp][0:3] for lp in range(2)], [both[lp][3:6] for lp in range(2)])
        return carry

    lax.fori_loop(0, 128 // CH, second_traces, 0, unroll=8)
    place(1)
    send_traces(1)

    def second_faces(ch, carry):
        both = tiles(u, pl.multiple_of(ch * CH, CH))
        faces(1, ch * CH, [both[lp][0:3] for lp in range(2)], [both[lp][3:6] for lp in range(2)])
        return carry

    lax.fori_loop(0, 128 // CH, second_faces, 0, unroll=2)
    send_halo(1)

    loads[7].wait()
    loads[8].wait()
    along_u = basis(co[0])
    along_v = basis(co[1])
    for i in range(4):
        for j in range(4):
            wt[i * 4 + j] = along_u[i] * along_v[j]
    slot_iota = lax.broadcasted_iota(jnp.int32, (256, 128), 0)

    def one_hot(pp, carry):
        for h in range(2):
            row = jnp.broadcast_to(st[pl.ds(2 * pp + h, 1), :], (256, 128))
            oh[pp, :, h * 128 : h * 128 + 128] = jnp.where(slot_iota == row, 1.0, 0.0).astype(BF16)
        return carry

    lax.fori_loop(0, 32, one_hot, 0, unroll=4)
    products()
    all_straight(0).wait_recv()
    interpolate(tb0[...], tt, oh, wt, pls)
    take_halo(1)

    def second_section(ch, carry):
        finish(1, ch * CH)
        return carry

    lax.fori_loop(0, 128 // CH, second_section, 0, unroll=2)
    all_straight(1).wait_recv()
    for sec in range(2):
        for copy in halo_copies(sec):
            copy.wait_send()
        all_straight(sec).wait_send()


def on_device(fields, resid, permit, metric, route, stencil, coords):
    columns = fields.shape[0] * fields.shape[1]
    w1, w2 = stacked_tables()
    hbm = pl.BlockSpec(memory_space=pltpu.HBM)
    vmem = pl.BlockSpec(memory_space=pltpu.VMEM)
    dma = pltpu.SemaphoreType.DMA
    kept = (
        pltpu.VMEM((128, 1536), F32),
        pltpu.VMEM((128, 1536), F32),
        pltpu.VMEM((256, 128), F32),
        pltpu.VMEM((32, 256, 256), BF16),
        pltpu.VMEM((16, 64, 128), F32),
        pltpu.VMEM((512, 128), F32),
    )
    held = pl.pallas_call(
        kernel,
        out_shape=kept,
        in_specs=[hbm] * 9,
        out_specs=(vmem,) * len(kept),
        scratch_shapes=[
            pltpu.VMEM((128, 256), F32),
            pltpu.VMEM((128, 768), F32),
            pltpu.VMEM((1, 128), jnp.int32),
            pltpu.VMEM((64, 128), jnp.int32),
            pltpu.VMEM((2, 64, 128), F32),
            pltpu.VMEM((3, 256, 256), BF16),
            pltpu.VMEM((3, 128, 256), BF16),
            pltpu.VMEM((2, 4, 144, 128), F32),
            pltpu.VMEM((2, 4, 272, 128), F32),
            pltpu.VMEM((2, 2, 4, 16, 128), F32),
            pltpu.VMEM((2, 2, 4, 8, 128), F32),
            pltpu.VMEM((2, 2, 4, 16, 128), F32),
            pltpu.VMEM((4, 128, 128), F32),
            pltpu.VMEM((3, 512, 256), BF16),
            pltpu.VMEM((3, 512, 256), F32),
            pltpu.VMEM((128, 128), F32),
            pltpu.VMEM((2, 256, 128), F32),
            pltpu.VMEM((256, 128), F32),
            pltpu.VMEM((256, 256), BF16),
            dma((9,)),
            dma((2, 4)),
            dma((2, 4)),
            dma((2,)),
            dma((2,)),
            pltpu.SemaphoreType.REGULAR,
        ],
        compiler_params=pltpu.CompilerParams(
            collective_id=0, has_side_effects=True, vmem_limit_bytes=VMEM_A * 1024 * 1024
        ),
    )(
        fields.reshape(columns, 1536),
        resid.reshape(columns, 1536),
        permit.reshape(columns, 256),
        metric.reshape(columns, 768),
        route,
        stencil,
        coords,
        jnp.asarray(w1),
        jnp.asarray(w2),
    )
    f_out, r_out, plane = pl.pallas_call(
        last_kernel,
        out_shape=(
            jax.ShapeDtypeStruct((columns, 1536), F32),
            jax.ShapeDtypeStruct((columns, 1536), F32),
            jax.ShapeDtypeStruct((768, 128), F32),
        ),
        in_specs=[vmem] * len(kept),
        out_specs=(hbm,) * 3,
        scratch_shapes=[pltpu.VMEM((512, 128), F32), pltpu.VMEM((256, 256), BF16), dma((27,))],
        compiler_params=pltpu.CompilerParams(vmem_limit_bytes=VMEM_B * 1024 * 1024),
    )(*held)
    return (
        f_out.reshape(fields.shape),
        r_out.reshape(fields.shape),
        plane.reshape(12, stencil.shape[0], stencil.shape[1]),
    )


def solution(mesh):
    return jax.shard_map(
        on_device,
        mesh=mesh,
        in_specs=(
            P("gx", "gy", None),
            P("gx", "gy", None),
            P("gx", "gy", None),
            P("gx", "gy", None),
            P("gx", "gy"),
            P("gx", "gy"),
            P(None, "gx", "gy"),
        ),
        out_specs=(P("gx", "gy", None), P("gx", "gy", None), P(None, "gx", "gy")),
        check_vma=False,
    )
```

```python
import functools

import jax
import jax.numpy as jnp
import numpy as np
from jax import lax
from jax.experimental import pallas as pl
from jax.experimental.pallas import tpu as pltpu
from jax.sharding import PartitionSpec as P

section_decay = (-0.41789047449985195, -1.192151694642677)
section_gain = (0.37921031299962726, 0.8229550293869817)
time_step = 0.05
lift_factor = 3.0

MESH = pl.DeviceIdType.MESH
F32 = jnp.float32
BF16 = jnp.bfloat16
NX, NY = 16, 8
VMEM_A, VMEM_B = 54, 16
CH = 16


def gll_points():
    return np.array([-1.0, -np.sqrt(0.2), np.sqrt(0.2), 1.0])


def derivative_table():
    points = gll_points()
    barycentric = np.array(
        [1.0 / np.prod([points[j] - points[k] for k in range(4) if k != j]) for j in range(4)]
    )
    table = np.zeros((4, 4))
    for i in range(4):
        for j in range(4):
            if i != j:
                table[i, j] = barycentric[j] / barycentric[i] / (points[i] - points[j])
        table[i, i] = -np.sum(table[i])
    return table


def stacked_tables():
    table = derivative_table()
    table[3, 3] -= lift_factor
    table[0, 0] += lift_factor
    eye = np.eye(4)
    along = [
        np.kron(np.kron(table, eye), eye),
        np.kron(np.kron(eye, table), eye),
        np.kron(np.kron(eye, eye), table),
    ]
    two = [np.kron(np.eye(2), m).T for m in along]
    full = np.stack(
        [np.concatenate([two[(g + 1) % 3], two[(g + 2) % 3]], axis=1) for g in range(3)]
    ).astype(np.float32)
    high = full.astype(jnp.bfloat16)
    low = (full - high.astype(np.float32)).astype(jnp.bfloat16)
    return np.concatenate([high, high], axis=1), low


def lane_iota(rows):
    return lax.broadcasted_iota(jnp.int32, (rows, 128), 1)


def node_digit(axis, lane):
    return (lane >> (4 - 2 * axis)) & 3


def basis(coord):
    points = gll_points()
    listing = []
    for j in range(4):
        result = None
        for k in range(4):
            if k != j:
                term = (coord - float(points[k])) * float(1.0 / (points[j] - points[k]))
                result = term if result is None else result * term
        listing.append(result)
    return listing


def split2(value):
    high = value.astype(BF16)
    return high, (value - high.astype(F32)).astype(BF16)


def interpolate(table, tt, oh, wt, pls, done=None):
    high, low = split2(table.T)
    tt[0:128] = high
    tt[128:256] = low

    def rows_of(pp, carry):
        got = jnp.dot(tt[...], oh[pp], preferred_element_type=F32)
        for h in range(2):
            part = got[:, h * 128 : h * 128 + 128]
            total = None
            for n in range(16):
                both = part[n * 8 : n * 8 + 8] + part[128 + n * 8 : 136 + n * 8]
                term = both * wt[n, pl.ds(2 * pp + h, 1), :]
                total = term if total is None else total + term
            pls[pl.ds(2 * pp + h, 8, stride=64), :] = total
        return carry

    if done is None:
        lax.fori_loop(0, 32, rows_of, 0, unroll=8)
    else:
        for q in range(4):
            lax.fori_loop(8 * q, 8 * q + 8, rows_of, 0, unroll=8)
            done(q)


def last_kernel(
    u, r, tb1, oh, wt, pls0, f_out, r_out, pl_out, pls1, tt, out_sem
):
    stores = [
        pltpu.make_async_copy(u, f_out, out_sem.at[0]),
        pltpu.make_async_copy(r, r_out, out_sem.at[1]),
        pltpu.make_async_copy(pls0.at[pl.ds(0, 384)], pl_out.at[pl.ds(0, 384)], out_sem.at[2]),
    ] + [
        pltpu.make_async_copy(
            pls1.at[pl.ds(64 * c + 16 * q, 16)],
            pl_out.at[pl.ds(384 + 64 * c + 16 * q, 16)],
            out_sem.at[3 + 6 * q + c],
        )
        for q in range(4)
        for c in range(6)
    ]
    for store in stores[:3]:
        store.start()
    def done(q):
        for store in stores[3 + 6 * q : 9 + 6 * q]:
            store.start()

    interpolate(tb1[...], tt, oh, wt, pls1, done)
    for store in stores:
        store.wait()


def kernel(
    f_in, r_in, p_in, m_in, rt_in, st_in, co_in, w1_in, w2_in,
    u, r, tb1, oh, wt, pls,
    ep, me, rt, st, co, w1, w2,
    gxb, gyb, hys, hxr, hyr, qz, xs, rr, pay, og, tb0, tt, put,
    in_sem, hs_sem, hr_sem, sd_sem, rd_sem, ready,
):
    tb = (tb0, tb1)
    ix = lax.axis_index("gx")
    iy = lax.axis_index("gy")

    loads = [
        pltpu.make_async_copy(src, dst, in_sem.at[n])
        for n, (src, dst) in enumerate(
            [(f_in, u), (rt_in, rt), (w1_in, w1), (w2_in, w2), (m_in, me), (r_in, r),
             (p_in, ep), (st_in, st), (co_in, co)]
        )
    ]
    barrier = pltpu.get_barrier_semaphore()

    def greet_x(d, carry):
        pl.semaphore_signal(barrier, inc=1, device_id=(lax.rem(ix + d, NX), iy), device_id_type=MESH)
        return carry

    def greet_y(d, carry):
        pl.semaphore_signal(barrier, inc=1, device_id=(ix, lax.rem(iy + d, NY)), device_id_type=MESH)
        return carry

    lax.fori_loop(1, NX, greet_x, 0, unroll=15)
    lax.fori_loop(1, NY, greet_y, 0, unroll=7)
    for load in loads:
        load.start()

    lane = lane_iota(CH)
    digit = [node_digit(a, lane) for a in range(3)]
    sg = [
        jnp.where(d == 3, 1.0, jnp.where(d == 0, -1.0, 0.0)).astype(F32) for d in digit
    ]
    bd3 = [jnp.where((d == 3) | (d == 0), lift_factor, 0.0).astype(F32) for d in digit]
    sg3 = [lift_factor * s for s in sg]
    swap = []
    for a in range(3):
        reach = 3 << (4 - 2 * a)
        base = lane if a < 2 else lane ^ 64
        swap.append(
            jnp.where(digit[a] == 0, base + reach, jnp.where(digit[a] == 3, base - reach, lane))
        )
    is3 = [digit[0] == 3, digit[1] == 3]
    low_bottom = (digit[2] == 0) & (lane < 64)
    high_top = (digit[2] == 3) & (lane >= 64)
    pick = 64 + 4 * (lane >> 3) + 3
    comp_lane = lane & 7

    def permute(value, index):
        return jnp.take_along_axis(value, index, axis=1)

    def faces(sec, r0, ee, hh):
        xt = pl.multiple_of(r0, CH)
        for a in range(3):
            b, c = (a + 1) % 3, (a + 2) % 3
            for pair in range(2):
                sums, moved = [], []
                for lp in range(2):
                    if pair == 0:
                        t = ee[lp][b] + sg[a] * hh[lp][c]
                    else:
                        t = ee[lp][c] - sg[a] * hh[lp][b]
                    sums.append(t)
                    moved.append(permute(t, swap[a]))
                for lp in range(2):
                    k = pair * 2 + lp
                    if a == 0:
                        gxb[sec, k, pl.ds(xt + 8, CH), :] = moved[lp]
                    elif a == 1:
                        gyb[sec, k, pl.ds(2 * xt + 8, 8), :] = moved[lp][0:8]
                        gyb[sec, k, pl.ds(2 * xt + 24, 8), :] = moved[lp][8:16]
                    elif lp == 0:
                        qz[k, pl.ds(xt, CH), :] = jnp.where(
                            low_bottom, -sums[0], jnp.where(high_top, moved[1], moved[0])
                        )
                    else:
                        qz[k, pl.ds(xt, CH), :] = jnp.where(
                            high_top, 0.0, jnp.where(low_bottom, moved[0], moved[1])
                        )
        for g in range(3):
            for e, side in enumerate((ee, hh)):
                for lp in range(2):
                    high, low = split2(side[lp][g])
                    rows = pl.ds((e * 2 + lp) * 128 + xt, CH)
                    xs[g, rows, 0:128] = high
                    xs[g, rows, 128:256] = low

    def trace_rows(r0, ee, hh):
        total = jnp.zeros((CH, 128), F32)
        for c in range(6):
            side = ee if c < 3 else hh
            total = jnp.where(comp_lane == c, permute(side[1][c % 3], pick), total)
        pay[pl.ds(r0, CH), :] = total

    def tiles(ref, r0):
        return [
            [ref[pl.ds(r0, CH), (c * 2 + lp) * 128 : (c * 2 + lp + 1) * 128] for c in range(6)]
            for lp in range(2)
        ]

    def halo_copies(sec):
        below = {"x": lax.rem(ix + NX - 1, NX), "y": lax.rem(iy + NY - 1, NY)}
        above = {"x": lax.rem(ix + 1, NX), "y": lax.rem(iy + 1, NY)}
        plan = [
            (gxb.at[sec, :, pl.ds(8, 8)], hxr.at[sec, 0], (below["x"], iy)),
            (gxb.at[sec, :, pl.ds(128, 8)], hxr.at[sec, 1], (above["x"], iy)),
            (hys.at[sec, 0], hyr.at[sec, 0], (ix, below["y"])),
            (hys.at[sec, 1], hyr.at[sec, 1], (ix, above["y"])),
        ]
        return [
            pltpu.make_async_remote_copy(
                src_ref=src, dst_ref=dst, send_sem=hs_sem.at[sec, n], recv_sem=hr_sem.at[sec, n],
                device_id=device, device_id_type=MESH,
            )
            for n, (src, dst, device) in enumerate(plan)
        ]

    def send_halo(sec):
        copies = halo_copies(sec)
        for copy in copies[:2]:
            copy.start()
        for k in range(4):
            hys[sec, 0, k] = gyb[sec, k, pl.ds(8, 16, stride=16), :]
            hys[sec, 1, k] = gyb[sec, k, pl.ds(15, 16, stride=16), :]
        for copy in copies[2:]:
            copy.start()

    above_is = [
        jnp.where(ix == NX - 1, 0.0, 1.0).astype(F32), jnp.where(iy == NY - 1, 0.0, 1.0).astype(F32)
    ]
    below_is = [jnp.where(ix == 0, 0.0, 1.0).astype(F32), jnp.where(iy == 0, 0.0, 1.0).astype(F32)]

    def beside_y(sec, k, xt):
        up, down = (
            jnp.concatenate(
                [gyb[sec, k, pl.ds(2 * xt + at, 8), :], gyb[sec, k, pl.ds(2 * xt + at + 16, 8), :]],
                axis=0,
            )
            for at in (9, 7)
        )
        return jnp.where(is3[1], up, down)

    def no_halo(sec):
        none = jnp.zeros((16, 128), F32)
        for k in range(4):
            gxb[sec, k, 136:144, :] = none[0:8]
            gxb[sec, k, 0:8, :] = none[0:8]
            gyb[sec, k, pl.ds(16, 16, stride=16), :] = none
            gyb[sec, k, pl.ds(7, 16, stride=16), :] = none

    def take_halo(sec):
        for copy in halo_copies(sec):
            copy.wait_recv()
        for k in range(4):
            gxb[sec, k, 136:144, :] = hxr[sec, 0, k] * above_is[0]
            gxb[sec, k, 0:8, :] = hxr[sec, 1, k] * below_is[0]
            gyb[sec, k, pl.ds(16, 16, stride=16), :] = hyr[sec, 0, k] * above_is[1]
            gyb[sec, k, pl.ds(7, 16, stride=16), :] = hyr[sec, 1, k] * below_is[1]

    def add_halo(sec, lp):
        def share(rows, a, lp, mask, sign, values):
            b, c = (a + 1) % 3, (a + 2) % 3
            met = me[rows, (a * 2 + lp) * 128 : (a * 2 + lp + 1) * 128] * mask
            scale = time_step / ep[rows, lp * 128 : (lp + 1) * 128]
            for pair, e_comp, h_comp in ((0, b, c + 3), (1, c, b + 3)):
                flux = met * values[pair]
                turned = flux * (-sign if pair == 0 else sign)
                for comp, rate in ((e_comp, flux * scale), (h_comp, turned)):
                    cols = slice((comp * 2 + lp) * 128, (comp * 2 + lp + 1) * 128)
                    r[rows, cols] += rate
                    u[rows, cols] += section_gain[sec] * rate

        for side in range(2):
            rows = pl.ds(120 * side, 8)
            mask = jnp.where(node_digit(0, lane_iota(8)) == 3 * side, lift_factor, 0.0)
            sign = time_step * (2.0 * side - 1.0)
            share(
                rows, 0, lp, mask, sign,
                [gxb[sec, pair * 2 + lp, 136 * side : 136 * side + 8, :] for pair in range(2)],
            )
        col_y = lax.broadcasted_iota(jnp.int32, (CH, 128), 0) & 7
        edge = ((digit[1] == 0) & (col_y == 0)) | (is3[1] & (col_y == 7))
        mask = jnp.where(edge, lift_factor, 0.0)
        sign = time_step * sg[1]

        def rows_y(ch, carry):
            r0 = pl.multiple_of(ch * CH, CH)
            share(
                pl.ds(r0, CH), 1, lp, mask, sign,
                [beside_y(sec, pair * 2 + lp, r0) for pair in range(2)],
            )
            return carry

        lax.fori_loop(0, 128 // CH, rows_y, 0, unroll=8)

    def products():
        def one(g, carry):
            rr[g] = jnp.dot(xs[g], w1[g], preferred_element_type=F32) + jnp.dot(
                xs[g, :, 0:128], w2[g], preferred_element_type=F32
            )
            return carry

        lax.fori_loop(0, 3, one, 0, unroll=3)

    def finish(sec, r0):
        xt = pl.multiple_of(r0, CH)
        rows = pl.ds(xt, CH)
        new = [[None] * 6, [None] * 6]
        for lp in range(2):
            cols = [slice((c * 2 + lp) * 128, (c * 2 + lp + 1) * 128) for c in range(6)]
            val = [u[rows, cols[c]] for c in range(6)]
            tend = [None] * 6

            def add(c, term):
                tend[c] = term if tend[c] is None else tend[c] + term

            def slope(comp, axis):
                g, e = comp % 3, comp // 3
                half = 0 if axis == (g + 1) % 3 else 1
                return rr[g, pl.ds((e * 2 + lp) * 128 + xt, CH), half * 128 : half * 128 + 128]

            for a in range(3):
                b, c = (a + 1) % 3, (a + 2) % 3
                met = me[rows, (a * 2 + lp) * 128 : (a * 2 + lp + 1) * 128]
                q = []
                for pair in range(2):
                    k = pair * 2 + lp
                    if a == 0:
                        q.append(
                            jnp.where(
                                is3[0],
                                gxb[sec, k, pl.ds(xt + 16, CH), :],
                                gxb[sec, k, pl.ds(xt, CH), :],
                            )
                        )
                    elif a == 1:
                        q.append(beside_y(sec, k, xt))
                    else:
                        q.append(qz[k, rows, :])
                add(b, met * (bd3[a] * (q[0] - val[b]) - slope(c + 3, a)))
                add(c + 3, met * (-(sg3[a] * q[0]) - bd3[a] * val[c + 3] - slope(b, a)))
                add(c, met * (bd3[a] * (q[1] - val[c]) + slope(b + 3, a)))
                add(b + 3, met * (sg3[a] * q[1] - bd3[a] * val[b + 3] + slope(c, a)))
            scale = time_step / ep[rows, lp * 128 : (lp + 1) * 128]
            for c in range(6):
                rate = tend[c] * scale if c < 3 else tend[c] * time_step
                reg = section_decay[sec] * r[rows, cols[c]] + rate
                r[rows, cols[c]] = reg
                value = val[c] + section_gain[sec] * reg
                u[rows, cols[c]] = value
                new[lp][c] = value
        return new

    me_flat = ix * NY + iy

    def straight(sample):
        def make(d):
            peer = lax.rem(me_flat + d, NX * NY)
            return pltpu.make_async_remote_copy(
                src_ref=og.at[sample, pl.ds(peer * 2, 2)],
                dst_ref=tb[sample].at[pl.ds(me_flat * 2, 2)],
                send_sem=sd_sem.at[sample], recv_sem=rd_sem.at[sample],
                device_id=(lax.div(peer, NY), lax.rem(peer, NY)), device_id_type=MESH,
            )
        return make

    def all_straight(sample):
        whole = pl.ds(0, 2 * (NX * NY - 1))
        return pltpu.make_async_remote_copy(
            src_ref=og.at[sample, whole], dst_ref=tb[sample].at[whole],
            send_sem=sd_sem.at[sample], recv_sem=rd_sem.at[sample],
            device_id=(lax.rem(ix + 1, NX), iy), device_id_type=MESH,
        )

    def send_traces(sample):
        each(NX * NY, straight(sample), lambda copy: copy.start())
        mine = pl.ds(me_flat * 2, 2)
        tb[sample][mine, :] = og[sample, mine, :]

    def each(count, make, act):
        def body(d, carry):
            act(make(d))
            return carry

        lax.fori_loop(1, count, body, 0)

    def place(sample):
        value = pay[...]
        high = value.astype(BF16)
        rest = value - high.astype(F32)
        mid = rest.astype(BF16)
        low = (rest - mid.astype(F32)).astype(BF16)
        og[sample] = jnp.dot(
            put[...], jnp.concatenate([high, mid, low], axis=0), preferred_element_type=F32
        )

    loads[0].wait()
    loads[1].wait()

    def first_faces(ch, carry):
        r0 = ch * CH
        both = tiles(u, pl.multiple_of(r0, CH))
        ee = [both[lp][0:3] for lp in range(2)]
        hh = [both[lp][3:6] for lp in range(2)]
        faces(0, r0, ee, hh)
        trace_rows(pl.multiple_of(r0, CH), ee, hh)
        return carry

    lax.fori_loop(0, 128 // CH, first_faces, 0, unroll=2)

    targets = jnp.broadcast_to(rt[...], (128, 128))
    earlier = lax.broadcasted_iota(jnp.int32, (128, 128), 0) < lane_iota(128)
    same = jnp.where((targets.T == targets) & earlier, 1, 0)
    slots = rt[...] * 2 + jnp.sum(same, axis=0, keepdims=True)
    where = lax.broadcasted_iota(jnp.int32, (256, 128), 0) == jnp.broadcast_to(slots, (256, 128))
    for n in range(3):
        put[:, n * 128 : n * 128 + 128] = jnp.where(where, 1.0, 0.0).astype(BF16)

    pl.semaphore_wait(barrier, NX - 1 + NY - 1)
    send_halo(0)

    def tell(d, carry):
        pl.semaphore_signal(ready, inc=1, device_id=(ix, lax.rem(iy + d, NY)), device_id_type=MESH)
        return carry

    lax.fori_loop(1, NY, tell, 0, unroll=7)
    place(0)

    no_halo(0)
    for load in loads[2:7]:
        load.wait()
    products()

    def own_section(ch, carry):
        finish(0, ch * CH)
        return carry

    lax.fori_loop(0, 128 // CH, own_section, 0, unroll=4)
    pl.semaphore_wait(ready, NY - 1)
    send_traces(0)
    take_halo(0)
    add_halo(0, 1)

    def second_traces(ch, carry):
        r0 = pl.multiple_of(ch * CH, CH)
        both = tiles(u, r0)
        trace_rows(r0, [both[lp][0:3] for lp in range(2)], [both[lp][3:6] for lp in range(2)])
        return carry

    lax.fori_loop(0, 128 // CH, second_traces, 0, unroll=8)
    place(1)
    send_traces(1)
    add_halo(0, 0)

    def second_faces(ch, carry):
        both = tiles(u, pl.multiple_of(ch * CH, CH))
        faces(1, ch * CH, [both[lp][0:3] for lp in range(2)], [both[lp][3:6] for lp in range(2)])
        return carry

    lax.fori_loop(0, 128 // CH, second_faces, 0, unroll=2)
    send_halo(1)

    loads[7].wait()
    loads[8].wait()
    along_u = basis(co[0])
    along_v = basis(co[1])
    for i in range(4):
        for j in range(4):
            wt[i * 4 + j] = along_u[i] * along_v[j]
    slot_iota = lax.broadcasted_iota(jnp.int32, (256, 128), 0)

    def one_hot(pp, carry):
        for h in range(2):
            row = jnp.broadcast_to(st[pl.ds(2 * pp + h, 1), :], (256, 128))
            oh[pp, :, h * 128 : h * 128 + 128] = jnp.where(slot_iota == row, 1.0, 0.0).astype(BF16)
        return carry

    lax.fori_loop(0, 32, one_hot, 0, unroll=4)
    products()
    all_straight(0).wait_recv()
    interpolate(tb0[...], tt, oh, wt, pls)
    take_halo(1)

    def second_section(ch, carry):
        finish(1, ch * CH)
        return carry

    lax.fori_loop(0, 128 // CH, second_section, 0, unroll=2)
    all_straight(1).wait_recv()
    for sec in range(2):
        for copy in halo_copies(sec):
            copy.wait_send()
        all_straight(sec).wait_send()


def on_device(fields, resid, permit, metric, route, stencil, coords):
    columns = fields.shape[0] * fields.shape[1]
    w1, w2 = stacked_tables()
    hbm = pl.BlockSpec(memory_space=pltpu.HBM)
    vmem = pl.BlockSpec(memory_space=pltpu.VMEM)
    dma = pltpu.SemaphoreType.DMA
    kept = (
        pltpu.VMEM((128, 1536), F32),
        pltpu.VMEM((128, 1536), F32),
        pltpu.VMEM((256, 128), F32),
        pltpu.VMEM((32, 256, 256), BF16),
        pltpu.VMEM((16, 64, 128), F32),
        pltpu.VMEM((512, 128), F32),
    )
    held = pl.pallas_call(
        kernel,
        out_shape=kept,
        in_specs=[hbm] * 9,
        out_specs=(vmem,) * len(kept),
        scratch_shapes=[
            pltpu.VMEM((128, 256), F32),
            pltpu.VMEM((128, 768), F32),
            pltpu.VMEM((1, 128), jnp.int32),
            pltpu.VMEM((64, 128), jnp.int32),
            pltpu.VMEM((2, 64, 128), F32),
            pltpu.VMEM((3, 256, 256), BF16),
            pltpu.VMEM((3, 128, 256), BF16),
            pltpu.VMEM((2, 4, 144, 128), F32),
            pltpu.VMEM((2, 4, 272, 128), F32),
            pltpu.VMEM((2, 2, 4, 16, 128), F32),
            pltpu.VMEM((2, 2, 4, 8, 128), F32),
            pltpu.VMEM((2, 2, 4, 16, 128), F32),
            pltpu.VMEM((4, 128, 128), F32),
            pltpu.VMEM((3, 512, 256), BF16),
            pltpu.VMEM((3, 512, 256), F32),
            pltpu.VMEM((128, 128), F32),
            pltpu.VMEM((2, 256, 128), F32),
            pltpu.VMEM((256, 128), F32),
            pltpu.VMEM((256, 256), BF16),
            pltpu.VMEM((256, 384), BF16),
            dma((9,)),
            dma((2, 4)),
            dma((2, 4)),
            dma((2,)),
            dma((2,)),
            pltpu.SemaphoreType.REGULAR,
        ],
        compiler_params=pltpu.CompilerParams(
            collective_id=0, has_side_effects=True, vmem_limit_bytes=VMEM_A * 1024 * 1024
        ),
    )(
        fields.reshape(columns, 1536),
        resid.reshape(columns, 1536),
        permit.reshape(columns, 256),
        metric.reshape(columns, 768),
        route,
        stencil,
        coords,
        jnp.asarray(w1),
        jnp.asarray(w2),
    )
    f_out, r_out, plane = pl.pallas_call(
        last_kernel,
        out_shape=(
            jax.ShapeDtypeStruct((columns, 1536), F32),
            jax.ShapeDtypeStruct((columns, 1536), F32),
            jax.ShapeDtypeStruct((768, 128), F32),
        ),
        in_specs=[vmem] * len(kept),
        out_specs=(hbm,) * 3,
        scratch_shapes=[pltpu.VMEM((512, 128), F32), pltpu.VMEM((256, 256), BF16), dma((27,))],
        compiler_params=pltpu.CompilerParams(vmem_limit_bytes=VMEM_B * 1024 * 1024),
    )(*held)
    return (
        f_out.reshape(fields.shape),
        r_out.reshape(fields.shape),
        plane.reshape(12, stencil.shape[0], stencil.shape[1]),
    )


def solution(mesh):
    return jax.shard_map(
        on_device,
        mesh=mesh,
        in_specs=(
            P("gx", "gy", None),
            P("gx", "gy", None),
            P("gx", "gy", None),
            P("gx", "gy", None),
            P("gx", "gy"),
            P("gx", "gy"),
            P(None, "gx", "gy"),
        ),
        out_specs=(P("gx", "gy", None), P("gx", "gy", None), P(None, "gx", "gy")),
        check_vma=False,
    )
```

```python
import functools

import jax
import jax.numpy as jnp
import numpy as np
from jax import lax
from jax.experimental import pallas as pl
from jax.experimental.pallas import tpu as pltpu
from jax.sharding import PartitionSpec as P

section_decay = (-0.41789047449985195, -1.192151694642677)
section_gain = (0.37921031299962726, 0.8229550293869817)
time_step = 0.05
lift_factor = 3.0

MESH = pl.DeviceIdType.MESH
F32 = jnp.float32
BF16 = jnp.bfloat16
NX, NY = 16, 8
VMEM_A, VMEM_B = 54, 16
CH = 16


def gll_points():
    return np.array([-1.0, -np.sqrt(0.2), np.sqrt(0.2), 1.0])


def derivative_table():
    points = gll_points()
    barycentric = np.array(
        [1.0 / np.prod([points[j] - points[k] for k in range(4) if k != j]) for j in range(4)]
    )
    table = np.zeros((4, 4))
    for i in range(4):
        for j in range(4):
            if i != j:
                table[i, j] = barycentric[j] / barycentric[i] / (points[i] - points[j])
        table[i, i] = -np.sum(table[i])
    return table


def stacked_tables():
    table = derivative_table()
    table[3, 3] -= lift_factor
    table[0, 0] += lift_factor
    eye = np.eye(4)
    along = [
        np.kron(np.kron(table, eye), eye),
        np.kron(np.kron(eye, table), eye),
        np.kron(np.kron(eye, eye), table),
    ]
    two = [np.kron(np.eye(2), m).T for m in along]
    full = np.stack(
        [np.concatenate([two[(g + 1) % 3], two[(g + 2) % 3]], axis=1) for g in range(3)]
    ).astype(np.float32)
    high = full.astype(jnp.bfloat16)
    low = (full - high.astype(np.float32)).astype(jnp.bfloat16)
    return np.concatenate([high, high], axis=1), low


def lane_iota(rows):
    return lax.broadcasted_iota(jnp.int32, (rows, 128), 1)


def node_digit(axis, lane):
    return (lane >> (4 - 2 * axis)) & 3


def basis(coord):
    points = gll_points()
    listing = []
    for j in range(4):
        result = None
        for k in range(4):
            if k != j:
                term = (coord - float(points[k])) * float(1.0 / (points[j] - points[k]))
                result = term if result is None else result * term
        listing.append(result)
    return listing


def split2(value):
    high = value.astype(BF16)
    return high, (value - high.astype(F32)).astype(BF16)


def interpolate(table, cmat, tt, oh, wt, pls, done=None):
    used = lax.dot_general(
        jnp.concatenate(split2(table.T), axis=0), cmat[...], (((1,), (1,)), ((), ())),
        preferred_element_type=F32,
    )
    tt[:, 0:128] = used[0:128].astype(BF16)
    tt[:, 128:256] = used[128:256].astype(BF16)

    def rows_of(pp, carry):
        got = jnp.dot(tt[...], oh[pp], preferred_element_type=F32)
        for h in range(2):
            part = got[:, h * 128 : h * 128 + 128]
            total = None
            for n in range(16):
                both = part[n * 8 : n * 8 + 8]
                term = both * wt[n, pl.ds(2 * pp + h, 1), :]
                total = term if total is None else total + term
            pls[pl.ds(2 * pp + h, 8, stride=64), :] = total
        return carry

    if done is None:
        lax.fori_loop(0, 32, rows_of, 0, unroll=8)
    else:
        for q in range(4):
            lax.fori_loop(8 * q, 8 * q + 8, rows_of, 0, unroll=8)
            done(q)


def last_kernel(
    u, r, tb1, cmat, oh, wt, pls0, f_out, r_out, pl_out, pls1, tt, out_sem
):
    stores = [
        pltpu.make_async_copy(u, f_out, out_sem.at[0]),
        pltpu.make_async_copy(r, r_out, out_sem.at[1]),
        pltpu.make_async_copy(pls0.at[pl.ds(0, 384)], pl_out.at[pl.ds(0, 384)], out_sem.at[2]),
    ] + [
        pltpu.make_async_copy(
            pls1.at[pl.ds(64 * c + 16 * q, 16)],
            pl_out.at[pl.ds(384 + 64 * c + 16 * q, 16)],
            out_sem.at[3 + 6 * q + c],
        )
        for q in range(4)
        for c in range(6)
    ]
    for store in stores[:3]:
        store.start()
    def done(q):
        for store in stores[3 + 6 * q : 9 + 6 * q]:
            store.start()

    interpolate(tb1[...], cmat, tt, oh, wt, pls1, done)
    for store in stores:
        store.wait()


def kernel(
    f_in, r_in, p_in, m_in, rt_in, st_in, co_in, w1_in, w2_in,
    u, r, tb1, cmat, oh, wt, pls,
    ep, me, rt, st, co, w1, w2,
    gxb, gyb, hys, hxr, hyr, qz, xs, rr, pay, og, tb0, tt, put,
    in_sem, hs_sem, hr_sem, sd_sem, rd_sem, ready,
):
    tb = (tb0, tb1)
    ix = lax.axis_index("gx")
    iy = lax.axis_index("gy")

    loads = [
        pltpu.make_async_copy(src, dst, in_sem.at[n])
        for n, (src, dst) in enumerate(
            [(f_in, u), (rt_in, rt), (w1_in, w1), (w2_in, w2), (m_in, me), (r_in, r),
             (p_in, ep), (st_in, st), (co_in, co)]
        )
    ]
    barrier = pltpu.get_barrier_semaphore()

    def greet_x(d, carry):
        pl.semaphore_signal(barrier, inc=1, device_id=(lax.rem(ix + d, NX), iy), device_id_type=MESH)
        return carry

    def greet_y(d, carry):
        pl.semaphore_signal(barrier, inc=1, device_id=(ix, lax.rem(iy + d, NY)), device_id_type=MESH)
        return carry

    lax.fori_loop(1, NX, greet_x, 0, unroll=15)
    lax.fori_loop(1, NY, greet_y, 0, unroll=7)
    for load in loads:
        load.start()

    lane = lane_iota(CH)
    digit = [node_digit(a, lane) for a in range(3)]
    sg = [
        jnp.where(d == 3, 1.0, jnp.where(d == 0, -1.0, 0.0)).astype(F32) for d in digit
    ]
    bd3 = [jnp.where((d == 3) | (d == 0), lift_factor, 0.0).astype(F32) for d in digit]
    sg3 = [lift_factor * s for s in sg]
    swap = []
    for a in range(3):
        reach = 3 << (4 - 2 * a)
        base = lane if a < 2 else lane ^ 64
        swap.append(
            jnp.where(digit[a] == 0, base + reach, jnp.where(digit[a] == 3, base - reach, lane))
        )
    is3 = [digit[0] == 3, digit[1] == 3]
    low_bottom = (digit[2] == 0) & (lane < 64)
    high_top = (digit[2] == 3) & (lane >= 64)
    pick = 64 + 4 * (lane >> 3) + 3
    comp_lane = lane & 7

    def permute(value, index):
        return jnp.take_along_axis(value, index, axis=1)

    def faces(sec, r0, ee, hh):
        xt = pl.multiple_of(r0, CH)
        for a in range(3):
            b, c = (a + 1) % 3, (a + 2) % 3
            for pair in range(2):
                sums, moved = [], []
                for lp in range(2):
                    if pair == 0:
                        t = ee[lp][b] + sg[a] * hh[lp][c]
                    else:
                        t = ee[lp][c] - sg[a] * hh[lp][b]
                    sums.append(t)
                    moved.append(permute(t, swap[a]))
                for lp in range(2):
                    k = pair * 2 + lp
                    if a == 0:
                        gxb[sec, k, pl.ds(xt + 8, CH), :] = moved[lp]
                    elif a == 1:
                        gyb[sec, k, pl.ds(2 * xt + 8, 8), :] = moved[lp][0:8]
                        gyb[sec, k, pl.ds(2 * xt + 24, 8), :] = moved[lp][8:16]
                    elif lp == 0:
                        qz[k, pl.ds(xt, CH), :] = jnp.where(
                            low_bottom, -sums[0], jnp.where(high_top, moved[1], moved[0])
                        )
                    else:
                        qz[k, pl.ds(xt, CH), :] = jnp.where(
                            high_top, 0.0, jnp.where(low_bottom, moved[0], moved[1])
                        )
        for g in range(3):
            for e, side in enumerate((ee, hh)):
                for lp in range(2):
                    high, low = split2(side[lp][g])
                    rows = pl.ds((e * 2 + lp) * 128 + xt, CH)
                    xs[g, rows, 0:128] = high
                    xs[g, rows, 128:256] = low

    def trace_rows(r0, ee, hh):
        total = jnp.where(lane == 6, 1.0, 0.0).astype(F32)
        for c in range(6):
            side = ee if c < 3 else hh
            total = jnp.where(comp_lane == c, permute(side[1][c % 3], pick), total)
        pay[pl.ds(r0, CH), :] = total

    def tiles(ref, r0):
        return [
            [ref[pl.ds(r0, CH), (c * 2 + lp) * 128 : (c * 2 + lp + 1) * 128] for c in range(6)]
            for lp in range(2)
        ]

    def halo_copies(sec):
        below = {"x": lax.rem(ix + NX - 1, NX), "y": lax.rem(iy + NY - 1, NY)}
        above = {"x": lax.rem(ix + 1, NX), "y": lax.rem(iy + 1, NY)}
        plan = [
            (gxb.at[sec, :, pl.ds(8, 8)], hxr.at[sec, 0], (below["x"], iy)),
            (gxb.at[sec, :, pl.ds(128, 8)], hxr.at[sec, 1], (above["x"], iy)),
            (hys.at[sec, 0], hyr.at[sec, 0], (ix, below["y"])),
            (hys.at[sec, 1], hyr.at[sec, 1], (ix, above["y"])),
        ]
        return [
            pltpu.make_async_remote_copy(
                src_ref=src, dst_ref=dst, send_sem=hs_sem.at[sec, n], recv_sem=hr_sem.at[sec, n],
                device_id=device, device_id_type=MESH,
            )
            for n, (src, dst, device) in enumerate(plan)
        ]

    def send_halo(sec):
        copies = halo_copies(sec)
        for copy in copies[:2]:
            copy.start()
        for k in range(4):
            hys[sec, 0, k] = gyb[sec, k, pl.ds(8, 16, stride=16), :]
            hys[sec, 1, k] = gyb[sec, k, pl.ds(15, 16, stride=16), :]
        for copy in copies[2:]:
            copy.start()

    above_is = [
        jnp.where(ix == NX - 1, 0.0, 1.0).astype(F32), jnp.where(iy == NY - 1, 0.0, 1.0).astype(F32)
    ]
    below_is = [jnp.where(ix == 0, 0.0, 1.0).astype(F32), jnp.where(iy == 0, 0.0, 1.0).astype(F32)]

    def beside_y(sec, k, xt):
        up, down = (
            jnp.concatenate(
                [gyb[sec, k, pl.ds(2 * xt + at, 8), :], gyb[sec, k, pl.ds(2 * xt + at + 16, 8), :]],
                axis=0,
            )
            for at in (9, 7)
        )
        return jnp.where(is3[1], up, down)

    def no_halo(sec):
        none = jnp.zeros((16, 128), F32)
        for k in range(4):
            gxb[sec, k, 136:144, :] = none[0:8]
            gxb[sec, k, 0:8, :] = none[0:8]
            gyb[sec, k, pl.ds(16, 16, stride=16), :] = none
            gyb[sec, k, pl.ds(7, 16, stride=16), :] = none

    def take_halo(sec):
        for copy in halo_copies(sec):
            copy.wait_recv()
        for k in range(4):
            gxb[sec, k, 136:144, :] = hxr[sec, 0, k] * above_is[0]
            gxb[sec, k, 0:8, :] = hxr[sec, 1, k] * below_is[0]
            gyb[sec, k, pl.ds(16, 16, stride=16), :] = hyr[sec, 0, k] * above_is[1]
            gyb[sec, k, pl.ds(7, 16, stride=16), :] = hyr[sec, 1, k] * below_is[1]

    def add_halo(sec, lp):
        def share(rows, a, lp, mask, sign, values):
            b, c = (a + 1) % 3, (a + 2) % 3
            met = me[rows, (a * 2 + lp) * 128 : (a * 2 + lp + 1) * 128] * mask
            scale = time_step / ep[rows, lp * 128 : (lp + 1) * 128]
            for pair, e_comp, h_comp in ((0, b, c + 3), (1, c, b + 3)):
                flux = met * values[pair]
                turned = flux * (-sign if pair == 0 else sign)
                for comp, rate in ((e_comp, flux * scale), (h_comp, turned)):
                    cols = slice((comp * 2 + lp) * 128, (comp * 2 + lp + 1) * 128)
                    r[rows, cols] += rate
                    u[rows, cols] += section_gain[sec] * rate

        for side in range(2):
            rows = pl.ds(120 * side, 8)
            mask = jnp.where(node_digit(0, lane_iota(8)) == 3 * side, lift_factor, 0.0)
            sign = time_step * (2.0 * side - 1.0)
            share(
                rows, 0, lp, mask, sign,
                [gxb[sec, pair * 2 + lp, 136 * side : 136 * side + 8, :] for pair in range(2)],
            )
        col_y = lax.broadcasted_iota(jnp.int32, (CH, 128), 0) & 7
        edge = ((digit[1] == 0) & (col_y == 0)) | (is3[1] & (col_y == 7))
        mask = jnp.where(edge, lift_factor, 0.0)
        sign = time_step * sg[1]

        def rows_y(ch, carry):
            r0 = pl.multiple_of(ch * CH, CH)
            share(
                pl.ds(r0, CH), 1, lp, mask, sign,
                [beside_y(sec, pair * 2 + lp, r0) for pair in range(2)],
            )
            return carry

        lax.fori_loop(0, 128 // CH, rows_y, 0, unroll=8)

    def products():
        def one(g, carry):
            rr[g] = jnp.dot(xs[g], w1[g], preferred_element_type=F32) + jnp.dot(
                xs[g, :, 0:128], w2[g], preferred_element_type=F32
            )
            return carry

        lax.fori_loop(0, 3, one, 0, unroll=3)

    def finish(sec, r0):
        xt = pl.multiple_of(r0, CH)
        rows = pl.ds(xt, CH)
        new = [[None] * 6, [None] * 6]
        for lp in range(2):
            cols = [slice((c * 2 + lp) * 128, (c * 2 + lp + 1) * 128) for c in range(6)]
            val = [u[rows, cols[c]] for c in range(6)]
            tend = [None] * 6

            def add(c, term):
                tend[c] = term if tend[c] is None else tend[c] + term

            def slope(comp, axis):
                g, e = comp % 3, comp // 3
                half = 0 if axis == (g + 1) % 3 else 1
                return rr[g, pl.ds((e * 2 + lp) * 128 + xt, CH), half * 128 : half * 128 + 128]

            for a in range(3):
                b, c = (a + 1) % 3, (a + 2) % 3
                met = me[rows, (a * 2 + lp) * 128 : (a * 2 + lp + 1) * 128]
                q = []
                for pair in range(2):
                    k = pair * 2 + lp
                    if a == 0:
                        q.append(
                            jnp.where(
                                is3[0],
                                gxb[sec, k, pl.ds(xt + 16, CH), :],
                                gxb[sec, k, pl.ds(xt, CH), :],
                            )
                        )
                    elif a == 1:
                        q.append(beside_y(sec, k, xt))
                    else:
                        q.append(qz[k, rows, :])
                add(b, met * (bd3[a] * (q[0] - val[b]) - slope(c + 3, a)))
                add(c + 3, met * (-(sg3[a] * q[0]) - bd3[a] * val[c + 3] - slope(b, a)))
                add(c, met * (bd3[a] * (q[1] - val[c]) + slope(b + 3, a)))
                add(b + 3, met * (sg3[a] * q[1] - bd3[a] * val[b + 3] + slope(c, a)))
            scale = time_step / ep[rows, lp * 128 : (lp + 1) * 128]
            for c in range(6):
                rate = tend[c] * scale if c < 3 else tend[c] * time_step
                reg = section_decay[sec] * r[rows, cols[c]] + rate
                r[rows, cols[c]] = reg
                value = val[c] + section_gain[sec] * reg
                u[rows, cols[c]] = value
                new[lp][c] = value
        return new

    me_flat = ix * NY + iy

    def straight(sample):
        def make(d):
            peer = lax.rem(me_flat + d, NX * NY)
            return pltpu.make_async_remote_copy(
                src_ref=og.at[sample, pl.ds(peer * 2, 2)],
                dst_ref=tb[sample].at[pl.ds(me_flat * 2, 2)],
                send_sem=sd_sem.at[sample], recv_sem=rd_sem.at[sample],
                device_id=(lax.div(peer, NY), lax.rem(peer, NY)), device_id_type=MESH,
            )
        return make

    def all_straight(sample):
        whole = pl.ds(0, 2 * (NX * NY - 1))
        return pltpu.make_async_remote_copy(
            src_ref=og.at[sample, whole], dst_ref=tb[sample].at[whole],
            send_sem=sd_sem.at[sample], recv_sem=rd_sem.at[sample],
            device_id=(lax.rem(ix + 1, NX), iy), device_id_type=MESH,
        )

    def send_traces(sample):
        each(NX * NY, straight(sample), lambda copy: copy.start())
        mine = pl.ds(me_flat * 2, 2)
        tb[sample][mine, :] = og[sample, mine, :]

    def each(count, make, act):
        def body(d, carry):
            act(make(d))
            return carry

        lax.fori_loop(1, count, body, 0)

    def place(sample):
        value = pay[...]
        high = value.astype(BF16)
        rest = value - high.astype(F32)
        mid = rest.astype(BF16)
        low = (rest - mid.astype(F32)).astype(BF16)
        og[sample] = jnp.dot(
            put[...], jnp.concatenate([high, mid, low], axis=0), preferred_element_type=F32
        )

    loads[0].wait()
    loads[1].wait()

    def first_faces(ch, carry):
        r0 = ch * CH
        both = tiles(u, pl.multiple_of(r0, CH))
        ee = [both[lp][0:3] for lp in range(2)]
        hh = [both[lp][3:6] for lp in range(2)]
        faces(0, r0, ee, hh)
        trace_rows(pl.multiple_of(r0, CH), ee, hh)
        return carry

    lax.fori_loop(0, 128 // CH, first_faces, 0, unroll=2)

    targets = jnp.broadcast_to(rt[...], (128, 128))
    earlier = lax.broadcasted_iota(jnp.int32, (128, 128), 0) < lane_iota(128)
    same = jnp.where((targets.T == targets) & earlier, 1, 0)
    slots = rt[...] * 2 + jnp.sum(same, axis=0, keepdims=True)
    where = lax.broadcasted_iota(jnp.int32, (256, 128), 0) == jnp.broadcast_to(slots, (256, 128))
    for n in range(3):
        put[:, n * 128 : n * 128 + 128] = jnp.where(where, 1.0, 0.0).astype(BF16)

    pl.semaphore_wait(barrier, NX - 1 + NY - 1)
    send_halo(0)

    def tell(d, carry):
        pl.semaphore_signal(ready, inc=1, device_id=(ix, lax.rem(iy + d, NY)), device_id_type=MESH)
        return carry

    lax.fori_loop(1, NY, tell, 0, unroll=7)
    place(0)

    no_halo(0)
    for load in loads[2:7]:
        load.wait()
    products()

    def own_section(ch, carry):
        finish(0, ch * CH)
        return carry

    lax.fori_loop(0, 128 // CH, own_section, 0, unroll=4)
    pl.semaphore_wait(ready, NY - 1)
    send_traces(0)
    take_halo(0)
    add_halo(0, 1)

    def second_traces(ch, carry):
        r0 = pl.multiple_of(ch * CH, CH)
        both = tiles(u, r0)
        trace_rows(r0, [both[lp][0:3] for lp in range(2)], [both[lp][3:6] for lp in range(2)])
        return carry

    lax.fori_loop(0, 128 // CH, second_traces, 0, unroll=8)
    place(1)
    send_traces(1)
    add_halo(0, 0)

    def second_faces(ch, carry):
        both = tiles(u, pl.multiple_of(ch * CH, CH))
        faces(1, ch * CH, [both[lp][0:3] for lp in range(2)], [both[lp][3:6] for lp in range(2)])
        return carry

    lax.fori_loop(0, 128 // CH, second_faces, 0, unroll=2)
    send_halo(1)

    loads[7].wait()
    loads[8].wait()
    along_u = basis(co[0])
    along_v = basis(co[1])
    for i in range(4):
        for j in range(4):
            wt[i * 4 + j] = along_u[i] * along_v[j]
    products()
    all_straight(0).wait_recv()

    used = tb0[...].T[6:7]
    before = lax.broadcasted_iota(jnp.int32, (256, 256), 0) < lax.broadcasted_iota(jnp.int32, (256, 256), 1)
    place_of = jnp.dot(
        jnp.broadcast_to(used, (8, 256)).astype(BF16), jnp.where(before, 1.0, 0.0).astype(BF16),
        preferred_element_type=F32,
    )[0:1]
    index = lax.broadcasted_iota(jnp.int32, (128, 256), 0).astype(F32)
    chosen = jnp.where(index == jnp.broadcast_to(place_of, (128, 256)), 1.0, 0.0)
    cmat[...] = (chosen * used).astype(BF16)
    row_ids = lax.broadcasted_iota(jnp.int32, (256, 128), 0).astype(F32).astype(BF16)
    ids = jnp.dot(cmat[...], row_ids, preferred_element_type=F32)

    def one_hot(pp, carry):
        for h in range(2):
            row = jnp.broadcast_to(st[pl.ds(2 * pp + h, 1), :].astype(F32), (128, 128))
            match = jnp.where(ids == row, 1.0, 0.0).astype(BF16)
            oh[pp, 0:128, h * 128 : h * 128 + 128] = match
            oh[pp, 128:256, h * 128 : h * 128 + 128] = match
        return carry

    lax.fori_loop(0, 32, one_hot, 0, unroll=4)
    interpolate(tb0[...], cmat, tt, oh, wt, pls)
    take_halo(1)

    def second_section(ch, carry):
        finish(1, ch * CH)
        return carry

    lax.fori_loop(0, 128 // CH, second_section, 0, unroll=2)
    all_straight(1).wait_recv()
    for sec in range(2):
        for copy in halo_copies(sec):
            copy.wait_send()
        all_straight(sec).wait_send()


def on_device(fields, resid, permit, metric, route, stencil, coords):
    columns = fields.shape[0] * fields.shape[1]
    w1, w2 = stacked_tables()
    hbm = pl.BlockSpec(memory_space=pltpu.HBM)
    vmem = pl.BlockSpec(memory_space=pltpu.VMEM)
    dma = pltpu.SemaphoreType.DMA
    kept = (
        pltpu.VMEM((128, 1536), F32),
        pltpu.VMEM((128, 1536), F32),
        pltpu.VMEM((256, 128), F32),
        pltpu.VMEM((128, 256), BF16),
        pltpu.VMEM((32, 256, 256), BF16),
        pltpu.VMEM((16, 64, 128), F32),
        pltpu.VMEM((512, 128), F32),
    )
    held = pl.pallas_call(
        kernel,
        out_shape=kept,
        in_specs=[hbm] * 9,
        out_specs=(vmem,) * len(kept),
        scratch_shapes=[
            pltpu.VMEM((128, 256), F32),
            pltpu.VMEM((128, 768), F32),
            pltpu.VMEM((1, 128), jnp.int32),
            pltpu.VMEM((64, 128), jnp.int32),
            pltpu.VMEM((2, 64, 128), F32),
            pltpu.VMEM((3, 256, 256), BF16),
            pltpu.VMEM((3, 128, 256), BF16),
            pltpu.VMEM((2, 4, 144, 128), F32),
            pltpu.VMEM((2, 4, 272, 128), F32),
            pltpu.VMEM((2, 2, 4, 16, 128), F32),
            pltpu.VMEM((2, 2, 4, 8, 128), F32),
            pltpu.VMEM((2, 2, 4, 16, 128), F32),
            pltpu.VMEM((4, 128, 128), F32),
            pltpu.VMEM((3, 512, 256), BF16),
            pltpu.VMEM((3, 512, 256), F32),
            pltpu.VMEM((128, 128), F32),
            pltpu.VMEM((2, 256, 128), F32),
            pltpu.VMEM((256, 128), F32),
            pltpu.VMEM((128, 256), BF16),
            pltpu.VMEM((256, 384), BF16),
            dma((9,)),
            dma((2, 4)),
            dma((2, 4)),
            dma((2,)),
            dma((2,)),
            pltpu.SemaphoreType.REGULAR,
        ],
        compiler_params=pltpu.CompilerParams(
            collective_id=0, has_side_effects=True, vmem_limit_bytes=VMEM_A * 1024 * 1024
        ),
    )(
        fields.reshape(columns, 1536),
        resid.reshape(columns, 1536),
        permit.reshape(columns, 256),
        metric.reshape(columns, 768),
        route,
        stencil,
        coords,
        jnp.asarray(w1),
        jnp.asarray(w2),
    )
    f_out, r_out, plane = pl.pallas_call(
        last_kernel,
        out_shape=(
            jax.ShapeDtypeStruct((columns, 1536), F32),
            jax.ShapeDtypeStruct((columns, 1536), F32),
            jax.ShapeDtypeStruct((768, 128), F32),
        ),
        in_specs=[vmem] * len(kept),
        out_specs=(hbm,) * 3,
        scratch_shapes=[pltpu.VMEM((512, 128), F32), pltpu.VMEM((128, 256), BF16), dma((27,))],
        compiler_params=pltpu.CompilerParams(vmem_limit_bytes=VMEM_B * 1024 * 1024),
    )(*held)
    return (
        f_out.reshape(fields.shape),
        r_out.reshape(fields.shape),
        plane.reshape(12, stencil.shape[0], stencil.shape[1]),
    )


def solution(mesh):
    return jax.shard_map(
        on_device,
        mesh=mesh,
        in_specs=(
            P("gx", "gy", None),
            P("gx", "gy", None),
            P("gx", "gy", None),
            P("gx", "gy", None),
            P("gx", "gy"),
            P("gx", "gy"),
            P(None, "gx", "gy"),
        ),
        out_specs=(P("gx", "gy", None), P("gx", "gy", None), P(None, "gx", "gy")),
        check_vma=False,
    )
```

```python
import functools

import jax
import jax.numpy as jnp
import numpy as np
from jax import lax
from jax.experimental import pallas as pl
from jax.experimental.pallas import tpu as pltpu
from jax.sharding import PartitionSpec as P

section_decay = (-0.41789047449985195, -1.192151694642677)
section_gain = (0.37921031299962726, 0.8229550293869817)
time_step = 0.05
lift_factor = 3.0

MESH = pl.DeviceIdType.MESH
F32 = jnp.float32
BF16 = jnp.bfloat16
NX, NY = 16, 8
VMEM_A, VMEM_B = 54, 16
CH = 16


def gll_points():
    return np.array([-1.0, -np.sqrt(0.2), np.sqrt(0.2), 1.0])


def derivative_table():
    points = gll_points()
    barycentric = np.array(
        [1.0 / np.prod([points[j] - points[k] for k in range(4) if k != j]) for j in range(4)]
    )
    table = np.zeros((4, 4))
    for i in range(4):
        for j in range(4):
            if i != j:
                table[i, j] = barycentric[j] / barycentric[i] / (points[i] - points[j])
        table[i, i] = -np.sum(table[i])
    return table


def stacked_tables():
    table = derivative_table()
    table[3, 3] -= lift_factor
    table[0, 0] += lift_factor
    eye = np.eye(4)
    along = [
        np.kron(np.kron(table, eye), eye),
        np.kron(np.kron(eye, table), eye),
        np.kron(np.kron(eye, eye), table),
    ]
    two = [np.kron(np.eye(2), m).T for m in along]
    full = np.stack(
        [np.concatenate([two[(g + 1) % 3], two[(g + 2) % 3]], axis=1) for g in range(3)]
    ).astype(np.float32)
    high = full.astype(jnp.bfloat16)
    low = (full - high.astype(np.float32)).astype(jnp.bfloat16)
    return np.concatenate([high, high], axis=1), low


def lane_iota(rows):
    return lax.broadcasted_iota(jnp.int32, (rows, 128), 1)


def node_digit(axis, lane):
    return (lane >> (4 - 2 * axis)) & 3


def basis(coord):
    points = gll_points()
    listing = []
    for j in range(4):
        result = None
        for k in range(4):
            if k != j:
                term = (coord - float(points[k])) * float(1.0 / (points[j] - points[k]))
                result = term if result is None else result * term
        listing.append(result)
    return listing


def split2(value):
    high = value.astype(BF16)
    return high, (value - high.astype(F32)).astype(BF16)


def interpolate(table, tt, oh, wt, pls, done=None):
    high, low = split2(table.T)
    tt[0:128] = high
    tt[128:256] = low

    def rows_of(pp, carry):
        got = jnp.dot(tt[...], oh[pp], preferred_element_type=F32)
        for h in range(2):
            part = got[:, h * 128 : h * 128 + 128]
            total = None
            for n in range(16):
                both = part[n * 8 : n * 8 + 8] + part[128 + n * 8 : 136 + n * 8]
                term = both * wt[n, pl.ds(2 * pp + h, 1), :]
                total = term if total is None else total + term
            pls[pl.ds(2 * pp + h, 8, stride=64), :] = total
        return carry

    if done is None:
        lax.fori_loop(0, 32, rows_of, 0, unroll=8)
    else:
        for q in range(4):
            lax.fori_loop(8 * q, 8 * q + 8, rows_of, 0, unroll=8)
            done(q)


def last_kernel(
    u, r, tb1, oh, wt, pls0, f_out, r_out, pl_out, pls1, tt, out_sem
):
    stores = [
        pltpu.make_async_copy(u, f_out, out_sem.at[0]),
        pltpu.make_async_copy(r, r_out, out_sem.at[1]),
        pltpu.make_async_copy(pls0.at[pl.ds(0, 384)], pl_out.at[pl.ds(0, 384)], out_sem.at[2]),
    ] + [
        pltpu.make_async_copy(
            pls1.at[pl.ds(64 * c + 16 * q, 16)],
            pl_out.at[pl.ds(384 + 64 * c + 16 * q, 16)],
            out_sem.at[3 + 6 * q + c],
        )
        for q in range(4)
        for c in range(6)
    ]
    for store in stores[:3]:
        store.start()
    def done(q):
        for store in stores[3 + 6 * q : 9 + 6 * q]:
            store.start()

    interpolate(tb1[...], tt, oh, wt, pls1, done)
    for store in stores:
        store.wait()


def kernel(
    f_in, r_in, p_in, m_in, rt_in, st_in, co_in, w1_in, w2_in,
    u, r, tb1, oh, wt, pls,
    ep, me, rt, st, co, w1, w2,
    gxb, gyb, hys, hxr, hyr, qz, xs, rr, pay, og, tb0, tt, put,
    in_sem, hs_sem, hr_sem, sd_sem, rd_sem, ready,
):
    tb = (tb0, tb1)
    ix = lax.axis_index("gx")
    iy = lax.axis_index("gy")

    loads = [
        pltpu.make_async_copy(src, dst, in_sem.at[n])
        for n, (src, dst) in enumerate(
            [(f_in, u), (rt_in, rt), (w1_in, w1), (w2_in, w2), (m_in, me), (r_in, r),
             (p_in, ep), (st_in, st), (co_in, co)]
        )
    ]
    barrier = pltpu.get_barrier_semaphore()

    def greet_x(d, carry):
        pl.semaphore_signal(barrier, inc=1, device_id=(lax.rem(ix + d, NX), iy), device_id_type=MESH)
        return carry

    def greet_y(d, carry):
        pl.semaphore_signal(barrier, inc=1, device_id=(ix, lax.rem(iy + d, NY)), device_id_type=MESH)
        return carry

    lax.fori_loop(1, NX, greet_x, 0, unroll=15)
    lax.fori_loop(1, NY, greet_y, 0, unroll=7)
    for load in loads:
        load.start()

    lane = lane_iota(CH)
    digit = [node_digit(a, lane) for a in range(3)]
    sg = [
        jnp.where(d == 3, 1.0, jnp.where(d == 0, -1.0, 0.0)).astype(F32) for d in digit
    ]
    bd3 = [jnp.where((d == 3) | (d == 0), lift_factor, 0.0).astype(F32) for d in digit]
    sg3 = [lift_factor * s for s in sg]
    swap = []
    for a in range(3):
        reach = 3 << (4 - 2 * a)
        base = lane if a < 2 else lane ^ 64
        swap.append(
            jnp.where(digit[a] == 0, base + reach, jnp.where(digit[a] == 3, base - reach, lane))
        )
    is3 = [digit[0] == 3, digit[1] == 3]
    low_bottom = (digit[2] == 0) & (lane < 64)
    high_top = (digit[2] == 3) & (lane >= 64)
    pick = 64 + 4 * (lane >> 3) + 3
    comp_lane = lane & 7

    def permute(value, index):
        return jnp.take_along_axis(value, index, axis=1)

    def faces(sec, r0, ee, hh):
        xt = pl.multiple_of(r0, CH)
        for a in range(3):
            b, c = (a + 1) % 3, (a + 2) % 3
            for pair in range(2):
                sums, moved = [], []
                for lp in range(2):
                    if pair == 0:
                        t = ee[lp][b] + sg[a] * hh[lp][c]
                    else:
                        t = ee[lp][c] - sg[a] * hh[lp][b]
                    sums.append(t)
                    moved.append(permute(t, swap[a]))
                for lp in range(2):
                    k = pair * 2 + lp
                    if a == 0:
                        gxb[sec, k, pl.ds(xt + 8, CH), :] = moved[lp]
                    elif a == 1:
                        gyb[sec, k, pl.ds(2 * xt + 8, 8), :] = moved[lp][0:8]
                        gyb[sec, k, pl.ds(2 * xt + 24, 8), :] = moved[lp][8:16]
                    elif lp == 0:
                        qz[k, pl.ds(xt, CH), :] = jnp.where(
                            low_bottom, -sums[0], jnp.where(high_top, moved[1], moved[0])
                        )
                    else:
                        qz[k, pl.ds(xt, CH), :] = jnp.where(
                            high_top, 0.0, jnp.where(low_bottom, moved[0], moved[1])
                        )
        for g in range(3):
            for e, side in enumerate((ee, hh)):
                for lp in range(2):
                    high, low = split2(side[lp][g])
                    rows = pl.ds((e * 2 + lp) * 128 + xt, CH)
                    xs[g, rows, 0:128] = high
                    xs[g, rows, 128:256] = low

    def trace_rows(r0, ee, hh):
        total = jnp.zeros((CH, 128), F32)
        for c in range(6):
            side = ee if c < 3 else hh
            total = jnp.where(comp_lane == c, permute(side[1][c % 3], pick), total)
        pay[pl.ds(r0, CH), :] = total

    def tiles(ref, r0):
        return [
            [ref[pl.ds(r0, CH), (c * 2 + lp) * 128 : (c * 2 + lp + 1) * 128] for c in range(6)]
            for lp in range(2)
        ]

    def halo_copies(sec):
        below = {"x": lax.rem(ix + NX - 1, NX), "y": lax.rem(iy + NY - 1, NY)}
        above = {"x": lax.rem(ix + 1, NX), "y": lax.rem(iy + 1, NY)}
        plan = [
            (gxb.at[sec, :, pl.ds(8, 8)], hxr.at[sec, 0], (below["x"], iy)),
            (gxb.at[sec, :, pl.ds(128, 8)], hxr.at[sec, 1], (above["x"], iy)),
            (hys.at[sec, 0], hyr.at[sec, 0], (ix, below["y"])),
            (hys.at[sec, 1], hyr.at[sec, 1], (ix, above["y"])),
        ]
        return [
            pltpu.make_async_remote_copy(
                src_ref=src, dst_ref=dst, send_sem=hs_sem.at[sec, n], recv_sem=hr_sem.at[sec, n],
                device_id=device, device_id_type=MESH,
            )
            for n, (src, dst, device) in enumerate(plan)
        ]

    def send_halo(sec):
        copies = halo_copies(sec)
        for copy in copies[:2]:
            copy.start()
        for k in range(4):
            hys[sec, 0, k] = gyb[sec, k, pl.ds(8, 16, stride=16), :]
            hys[sec, 1, k] = gyb[sec, k, pl.ds(15, 16, stride=16), :]
        for copy in copies[2:]:
            copy.start()

    above_is = [
        jnp.where(ix == NX - 1, 0.0, 1.0).astype(F32), jnp.where(iy == NY - 1, 0.0, 1.0).astype(F32)
    ]
    below_is = [jnp.where(ix == 0, 0.0, 1.0).astype(F32), jnp.where(iy == 0, 0.0, 1.0).astype(F32)]

    def beside_y(sec, k, xt):
        up, down = (
            jnp.concatenate(
                [gyb[sec, k, pl.ds(2 * xt + at, 8), :], gyb[sec, k, pl.ds(2 * xt + at + 16, 8), :]],
                axis=0,
            )
            for at in (9, 7)
        )
        return jnp.where(is3[1], up, down)

    def no_halo(sec):
        none = jnp.zeros((16, 128), F32)
        for k in range(4):
            gxb[sec, k, 136:144, :] = none[0:8]
            gxb[sec, k, 0:8, :] = none[0:8]
            gyb[sec, k, pl.ds(16, 16, stride=16), :] = none
            gyb[sec, k, pl.ds(7, 16, stride=16), :] = none

    def take_halo(sec):
        for copy in halo_copies(sec):
            copy.wait_recv()
        for k in range(4):
            gxb[sec, k, 136:144, :] = hxr[sec, 0, k] * above_is[0]
            gxb[sec, k, 0:8, :] = hxr[sec, 1, k] * below_is[0]
            gyb[sec, k, pl.ds(16, 16, stride=16), :] = hyr[sec, 0, k] * above_is[1]
            gyb[sec, k, pl.ds(7, 16, stride=16), :] = hyr[sec, 1, k] * below_is[1]

    def add_halo(sec, lp):
        def share(rows, a, lp, mask, sign, values):
            b, c = (a + 1) % 3, (a + 2) % 3
            met = me[rows, (a * 2 + lp) * 128 : (a * 2 + lp + 1) * 128] * mask
            scale = time_step / ep[rows, lp * 128 : (lp + 1) * 128]
            for pair, e_comp, h_comp in ((0, b, c + 3), (1, c, b + 3)):
                flux = met * values[pair]
                turned = flux * (-sign if pair == 0 else sign)
                for comp, rate in ((e_comp, flux * scale), (h_comp, turned)):
                    cols = slice((comp * 2 + lp) * 128, (comp * 2 + lp + 1) * 128)
                    r[rows, cols] += rate
                    u[rows, cols] += section_gain[sec] * rate

        for side in range(2):
            rows = pl.ds(120 * side, 8)
            mask = jnp.where(node_digit(0, lane_iota(8)) == 3 * side, lift_factor, 0.0)
            sign = time_step * (2.0 * side - 1.0)
            share(
                rows, 0, lp, mask, sign,
                [gxb[sec, pair * 2 + lp, 136 * side : 136 * side + 8, :] for pair in range(2)],
            )
        col_y = lax.broadcasted_iota(jnp.int32, (CH, 128), 0) & 7
        edge = ((digit[1] == 0) & (col_y == 0)) | (is3[1] & (col_y == 7))
        mask = jnp.where(edge, lift_factor, 0.0)
        sign = time_step * sg[1]

        def rows_y(ch, carry):
            r0 = pl.multiple_of(ch * CH, CH)
            share(
                pl.ds(r0, CH), 1, lp, mask, sign,
                [beside_y(sec, pair * 2 + lp, r0) for pair in range(2)],
            )
            return carry

        lax.fori_loop(0, 128 // CH, rows_y, 0, unroll=8)

    def products():
        def one(g, carry):
            rr[g] = jnp.dot(xs[g], w1[g], preferred_element_type=F32) + jnp.dot(
                xs[g, :, 0:128], w2[g], preferred_element_type=F32
            )
            return carry

        lax.fori_loop(0, 3, one, 0, unroll=3)

    def finish(sec, r0):
        xt = pl.multiple_of(r0, CH)
        rows = pl.ds(xt, CH)
        new = [[None] * 6, [None] * 6]
        for lp in range(2):
            cols = [slice((c * 2 + lp) * 128, (c * 2 + lp + 1) * 128) for c in range(6)]
            val = [u[rows, cols[c]] for c in range(6)]
            tend = [None] * 6

            def add(c, term):
                tend[c] = term if tend[c] is None else tend[c] + term

            def slope(comp, axis):
                g, e = comp % 3, comp // 3
                half = 0 if axis == (g + 1) % 3 else 1
                return rr[g, pl.ds((e * 2 + lp) * 128 + xt, CH), half * 128 : half * 128 + 128]

            for a in range(3):
                b, c = (a + 1) % 3, (a + 2) % 3
                met = me[rows, (a * 2 + lp) * 128 : (a * 2 + lp + 1) * 128]
                q = []
                for pair in range(2):
                    k = pair * 2 + lp
                    if a == 0:
                        q.append(
                            jnp.where(
                                is3[0],
                                gxb[sec, k, pl.ds(xt + 16, CH), :],
                                gxb[sec, k, pl.ds(xt, CH), :],
                            )
                        )
                    elif a == 1:
                        q.append(beside_y(sec, k, xt))
                    else:
                        q.append(qz[k, rows, :])
                add(b, met * (bd3[a] * (q[0] - val[b]) - slope(c + 3, a)))
                add(c + 3, met * (-(sg3[a] * q[0]) - bd3[a] * val[c + 3] - slope(b, a)))
                add(c, met * (bd3[a] * (q[1] - val[c]) + slope(b + 3, a)))
                add(b + 3, met * (sg3[a] * q[1] - bd3[a] * val[b + 3] + slope(c, a)))
            scale = time_step / ep[rows, lp * 128 : (lp + 1) * 128]
            for c in range(6):
                rate = tend[c] * scale if c < 3 else tend[c] * time_step
                reg = section_decay[sec] * r[rows, cols[c]] + rate
                r[rows, cols[c]] = reg
                value = val[c] + section_gain[sec] * reg
                u[rows, cols[c]] = value
                new[lp][c] = value
        return new

    me_flat = ix * NY + iy

    def straight(sample):
        def make(d):
            peer = lax.rem(me_flat + d, NX * NY)
            return pltpu.make_async_remote_copy(
                src_ref=og.at[sample, pl.ds(peer * 2, 2)],
                dst_ref=tb[sample].at[pl.ds(me_flat * 2, 2)],
                send_sem=sd_sem.at[sample], recv_sem=rd_sem.at[sample],
                device_id=(lax.div(peer, NY), lax.rem(peer, NY)), device_id_type=MESH,
            )
        return make

    def all_straight(sample):
        whole = pl.ds(0, 2 * (NX * NY - 1))
        return pltpu.make_async_remote_copy(
            src_ref=og.at[sample, whole], dst_ref=tb[sample].at[whole],
            send_sem=sd_sem.at[sample], recv_sem=rd_sem.at[sample],
            device_id=(lax.rem(ix + 1, NX), iy), device_id_type=MESH,
        )

    def send_traces(sample):
        each(NX * NY, straight(sample), lambda copy: copy.start())
        mine = pl.ds(me_flat * 2, 2)
        tb[sample][mine, :] = og[sample, mine, :]

    def each(count, make, act):
        def body(d, carry):
            act(make(d))
            return carry

        lax.fori_loop(1, count, body, 0)

    def place(sample):
        value = pay[...]
        high = value.astype(BF16)
        rest = value - high.astype(F32)
        mid = rest.astype(BF16)
        low = (rest - mid.astype(F32)).astype(BF16)
        og[sample] = jnp.dot(
            put[...], jnp.concatenate([high, mid, low], axis=0), preferred_element_type=F32
        )

    loads[0].wait()
    loads[1].wait()

    def first_faces(ch, carry):
        r0 = ch * CH
        both = tiles(u, pl.multiple_of(r0, CH))
        ee = [both[lp][0:3] for lp in range(2)]
        hh = [both[lp][3:6] for lp in range(2)]
        faces(0, r0, ee, hh)
        trace_rows(pl.multiple_of(r0, CH), ee, hh)
        return carry

    lax.fori_loop(0, 128 // CH, first_faces, 0, unroll=2)

    targets = jnp.broadcast_to(rt[...], (128, 128))
    earlier = lax.broadcasted_iota(jnp.int32, (128, 128), 0) < lane_iota(128)
    same = jnp.where((targets.T == targets) & earlier, 1, 0)
    slots = rt[...] * 2 + jnp.sum(same, axis=0, keepdims=True)
    where = lax.broadcasted_iota(jnp.int32, (256, 128), 0) == jnp.broadcast_to(slots, (256, 128))
    for n in range(3):
        put[:, n * 128 : n * 128 + 128] = jnp.where(where, 1.0, 0.0).astype(BF16)

    pl.semaphore_wait(barrier, NX - 1 + NY - 1)
    send_halo(0)

    def tell(d, carry):
        pl.semaphore_signal(ready, inc=1, device_id=(ix, lax.rem(iy + d, NY)), device_id_type=MESH)
        return carry

    lax.fori_loop(1, NY, tell, 0, unroll=7)
    place(0)

    no_halo(0)
    for load in loads[2:7]:
        load.wait()
    products()

    def own_section(ch, carry):
        finish(0, ch * CH)
        return carry

    lax.fori_loop(0, 128 // CH, own_section, 0, unroll=4)
    pl.semaphore_wait(ready, NY - 1)
    send_traces(0)
    take_halo(0)
    add_halo(0, 1)

    def second_traces(ch, carry):
        r0 = pl.multiple_of(ch * CH, CH)
        both = tiles(u, r0)
        trace_rows(r0, [both[lp][0:3] for lp in range(2)], [both[lp][3:6] for lp in range(2)])
        return carry

    lax.fori_loop(0, 128 // CH, second_traces, 0, unroll=8)
    place(1)
    send_traces(1)
    add_halo(0, 0)

    def second_faces(ch, carry):
        both = tiles(u, pl.multiple_of(ch * CH, CH))
        faces(1, ch * CH, [both[lp][0:3] for lp in range(2)], [both[lp][3:6] for lp in range(2)])
        return carry

    lax.fori_loop(0, 128 // CH, second_faces, 0, unroll=2)
    send_halo(1)

    loads[7].wait()
    loads[8].wait()
    along_u = basis(co[0])
    along_v = basis(co[1])
    for i in range(4):
        for j in range(4):
            wt[i * 4 + j] = along_u[i] * along_v[j]
    slot_iota = lax.broadcasted_iota(jnp.int32, (256, 128), 0)

    def one_hot(pp, carry):
        for h in range(2):
            row = jnp.broadcast_to(st[pl.ds(2 * pp + h, 1), :], (256, 128))
            oh[pp, :, h * 128 : h * 128 + 128] = jnp.where(slot_iota == row, 1.0, 0.0).astype(BF16)
        return carry

    lax.fori_loop(0, 32, one_hot, 0, unroll=4)
    products()
    all_straight(0).wait_recv()
    interpolate(tb0[...], tt, oh, wt, pls)
    take_halo(1)

    def second_section(ch, carry):
        finish(1, ch * CH)
        return carry

    lax.fori_loop(0, 128 // CH, second_section, 0, unroll=2)
    all_straight(1).wait_recv()
    for sec in range(2):
        for copy in halo_copies(sec):
            copy.wait_send()
        all_straight(sec).wait_send()


def on_device(fields, resid, permit, metric, route, stencil, coords):
    columns = fields.shape[0] * fields.shape[1]
    w1, w2 = stacked_tables()
    hbm = pl.BlockSpec(memory_space=pltpu.HBM)
    vmem = pl.BlockSpec(memory_space=pltpu.VMEM)
    dma = pltpu.SemaphoreType.DMA
    kept = (
        pltpu.VMEM((128, 1536), F32),
        pltpu.VMEM((128, 1536), F32),
        pltpu.VMEM((256, 128), F32),
        pltpu.VMEM((32, 256, 256), BF16),
        pltpu.VMEM((16, 64, 128), F32),
        pltpu.VMEM((576, 128), F32),
    )
    held = pl.pallas_call(
        kernel,
        out_shape=kept,
        in_specs=[hbm] * 9,
        out_specs=(vmem,) * len(kept),
        scratch_shapes=[
            pltpu.VMEM((128, 256), F32),
            pltpu.VMEM((128, 768), F32),
            pltpu.VMEM((1, 128), jnp.int32),
            pltpu.VMEM((64, 128), jnp.int32),
            pltpu.VMEM((2, 64, 128), F32),
            pltpu.VMEM((3, 256, 256), BF16),
            pltpu.VMEM((3, 128, 256), BF16),
            pltpu.VMEM((2, 4, 144, 128), F32),
            pltpu.VMEM((2, 4, 272, 128), F32),
            pltpu.VMEM((2, 2, 4, 16, 128), F32),
            pltpu.VMEM((2, 2, 4, 8, 128), F32),
            pltpu.VMEM((2, 2, 4, 16, 128), F32),
            pltpu.VMEM((4, 128, 128), F32),
            pltpu.VMEM((3, 512, 256), BF16),
            pltpu.VMEM((3, 512, 256), F32),
            pltpu.VMEM((128, 128), F32),
            pltpu.VMEM((2, 256, 128), F32),
            pltpu.VMEM((256, 128), F32),
            pltpu.VMEM((256, 256), BF16),
            pltpu.VMEM((256, 384), BF16),
            dma((9,)),
            dma((2, 4)),
            dma((2, 4)),
            dma((2,)),
            dma((2,)),
            pltpu.SemaphoreType.REGULAR,
        ],
        compiler_params=pltpu.CompilerParams(
            collective_id=0, has_side_effects=True, vmem_limit_bytes=VMEM_A * 1024 * 1024
        ),
    )(
        fields.reshape(columns, 1536),
        resid.reshape(columns, 1536),
        permit.reshape(columns, 256),
        metric.reshape(columns, 768),
        route,
        stencil,
        coords,
        jnp.asarray(w1),
        jnp.asarray(w2),
    )
    f_out, r_out, plane = pl.pallas_call(
        last_kernel,
        out_shape=(
            jax.ShapeDtypeStruct((columns, 1536), F32),
            jax.ShapeDtypeStruct((columns, 1536), F32),
            jax.ShapeDtypeStruct((768, 128), F32),
        ),
        in_specs=[vmem] * len(kept),
        out_specs=(hbm,) * 3,
        scratch_shapes=[pltpu.VMEM((576, 128), F32), pltpu.VMEM((256, 256), BF16), dma((27,))],
        compiler_params=pltpu.CompilerParams(vmem_limit_bytes=VMEM_B * 1024 * 1024),
    )(*held)
    return (
        f_out.reshape(fields.shape),
        r_out.reshape(fields.shape),
        plane.reshape(12, stencil.shape[0], stencil.shape[1]),
    )


def solution(mesh):
    return jax.shard_map(
        on_device,
        mesh=mesh,
        in_specs=(
            P("gx", "gy", None),
            P("gx", "gy", None),
            P("gx", "gy", None),
            P("gx", "gy", None),
            P("gx", "gy"),
            P("gx", "gy"),
            P(None, "gx", "gy"),
        ),
        out_specs=(P("gx", "gy", None), P("gx", "gy", None), P(None, "gx", "gy")),
        check_vma=False,
    )
```
